32 devices in a mesh: tm: 4 (over z), space: 8 (over y, x, core).
Axes of the slice: x: 2, y: 2, z: 4, core: 2. Of those that a mesh axis runs over, the one named last changes fastest.
Arguments:
- iterate: float32 [4, 8, 16, 16, 512], P('tm', 'space'), may hold values from -3 to 3
- source_term: float32 [4, 8, 16, 16, 512], P('tm', 'space'), may hold values from -6 to 6
- conductivity: float32 [8, 16, 16, 512], P('space'), may hold values from 0.5 to 4
Outputs:
- new_iterate: float32 [4, 8, 16, 16, 512], P('tm', 'space')
- residual: float32 [4, 8, 16, 16, 512], P('tm', 'space')
The draws below stay inside these ranges and needn't reach their ends.
All inputs are finite; a program needn't handle non-finite values.
Results may differ from the reference program's by a relative error of at most 0.00002.
Values sent between devices are 32-bit elements; how exact they have to be, the bound alone decides.
A program may use at most 64 MiB of HBM per device.

```python
import math
import jax
import jax.numpy as jnp

NZ = 16
TX = 16
TY = 512
TILES = 8
NT = 4
N_SPACE = 8


def level_of(own_key, dims, split, smallest, top_value):
    def one(dim, parts):
        draws = jax.random.uniform(jax.random.fold_in(jax.random.fold_in(own_key, 6), dim), (parts,), jnp.float32, smallest / len(split), top_value / len(split))
        return jnp.repeat(jnp.exp(draws), dims[dim] // parts).reshape((-1,) + (1,) * (len(dims) - dim - 1))

    factor_of = one(*split[0])
    for cut in split[1:]:
        factor_of = factor_of * one(*cut)
    return factor_of


def bell_draw(own_key, extent, scale, most, split=(), dtype=jnp.bfloat16):
    loudness = level_of(own_key, extent, split, -0.22, 0.18) if split else 1.0
    array = jax.random.normal(own_key, extent, jnp.float32) * scale * loudness
    return jnp.minimum(jnp.maximum(array, -most), most).astype(dtype)


def setup_inputs(seed: int = 0) -> dict:
    key_of = jax.random.split(jax.random.key(seed), 4)
    return {
        "iterate": bell_draw(key_of[0], (NT, TILES, NZ, TX, TY), 0.6, 3.0, ((0, 4), (1, 8)), jnp.float32),
        "source_term": bell_draw(key_of[1], (NT, TILES, NZ, TX, TY), 1.0, 6.0, ((0, 4), (1, 8)), jnp.float32),
        "conductivity": jnp.clip(jnp.exp(math.log(4.0) - 2.0794415 * jax.random.uniform(key_of[2], (TILES, NZ, TX, TY), jnp.float32) ** level_of(key_of[2], (TILES, NZ, TX, TY), ((0, 8),), -0.2, 0.2)), 0.5, 4.0),
    }


tau_step = 0.08
damping = 0.7


def to_grid(tiled):
    frames = tiled.shape[0]
    return tiled.transpose(0, 2, 1, 3, 4).reshape(frames, NZ, N_SPACE * TX, TY)


def from_grid(grid_field):
    frames = grid_field.shape[0]
    shaped = grid_field.reshape(frames, NZ, N_SPACE, TX, TY)
    return shaped.transpose(0, 2, 1, 3, 4)


def neighbours(grid_field):
    padded = jnp.pad(grid_field, ((0, 0), (1, 1), (1, 1), (1, 1)))
    return [padded[:, 1:-1, :-2, 1:-1], padded[:, 1:-1, 2:, 1:-1],
            padded[:, 1:-1, 1:-1, :-2], padded[:, 1:-1, 1:-1, 2:],
            padded[:, :-2, 1:-1, 1:-1], padded[:, 2:, 1:-1, 1:-1]]


def face_weights(conduct):
    weights = [0.5 * (conduct + other) for other in neighbours(conduct)]
    weight_sum = weights[0]
    for near_item in weights[1:]:
        weight_sum = weight_sum + near_item
    return weights, weight_sum


def earlier(grid_field):
    return jnp.concatenate([jnp.zeros_like(grid_field[:1]), grid_field[:-1]], axis=0)


def apply_operator(update, weights, weight_sum, step_size):
    near_list = neighbours(update)
    flux_sum = weights[0] * near_list[0]
    for position in range(1, 6):
        flux_sum = flux_sum + weights[position] * near_list[position]
    return update - earlier(update) + step_size * (weight_sum * update - flux_sum)


def smooth(rhs_field, weights, weight_sum, step_size, want_left):
    diag_term = 1.0 + step_size * weight_sum
    update = damping * rhs_field / diag_term
    update = update + damping * (rhs_field - apply_operator(update, weights, weight_sum, step_size)) / diag_term
    if want_left:
        return update, rhs_field - apply_operator(update, weights, weight_sum, step_size)
    return update, update


def reference(iterate, source_term, conductivity):
    state_grid = to_grid(iterate)
    source_grid = to_grid(source_term)
    kappa_grid = to_grid(conductivity[None])
    conduct = kappa_grid * (1.0 + state_grid * state_grid)
    weights, weight_sum = face_weights(conduct)
    residual = source_grid - apply_operator(state_grid, weights, weight_sum, tau_step)
    fine_update, fine_left = smooth(residual, weights, weight_sum, tau_step, True)
    mid_rhs = fine_left[0::2] + fine_left[1::2]
    mid_conduct = 0.5 * (conduct[0::2] + conduct[1::2])
    weights, weight_sum = face_weights(mid_conduct)
    mid_update, mid_left = smooth(mid_rhs, weights, weight_sum, 2.0 * tau_step, True)
    top_rhs = mid_left[0::2] + mid_left[1::2]
    top_conduct = 0.5 * (mid_conduct[0::2] + mid_conduct[1::2])
    weights, weight_sum = face_weights(top_conduct)
    top_update, unused = smooth(top_rhs, weights, weight_sum, 4.0 * tau_step, False)
    mid_update = mid_update + jnp.repeat(top_update, 2, axis=0)
    fine_update = fine_update + jnp.repeat(mid_update, 2, axis=0)
    return from_grid(state_grid + fine_update), from_grid(residual)
```

```python
import functools
import types

import jax
import jax.numpy as jnp
from jax import lax
from jax.experimental import pallas as pl
from jax.experimental.pallas import tpu as pltpu
from jax.sharding import PartitionSpec as P

tau_step = 0.08
damping = 0.7
group = 4
halo = 8
pad = 2 * halo
parts = 2
mesh_ids = pl.DeviceIdType.MESH
order = (2, 1, 3, 0)
unroll = 4


def kernel(tm_size, space_size, names, *refs):
    r = types.SimpleNamespace(**dict(zip(names, refs)))
    nz, _, width = r.packed.shape[1], None, r.kap.shape[-1]
    tx = r.state_in.shape[3]
    span = width // nz
    chained = tm_size > group
    half = 0.5 * tau_step
    piece = nz // parts

    full = (pad - halo, tx + 2 * halo)
    trim = (pad - halo // 2, tx + halo)
    core = (pad, tx)

    def rows(win, shift=0):
        return pl.ds(win[0] + shift, win[1])

    real = rows(core)
    planes = pl.ds(1, nz)
    me = lax.axis_index("tm")
    sp = lax.axis_index("space")
    q = me % group
    base = me - q
    has_dn, has_up = sp > 0, sp < space_size - 1
    has_left, has_right = q > 0, q < group - 1
    has_prev, has_next = base > 0, base + group < tm_size
    flanks = [(has_dn, {"space": sp - 1}), (has_up, {"space": sp + 1})]
    beside_has = [has_left, has_right]

    def columns(d):
        return pl.ds(pl.multiple_of(d * width, width), width)

    own_copies = [
        pltpu.make_async_copy(hbm.at[0, 0], r.own.at[f], r.loc_sem.at[f])
        for f, hbm in enumerate((r.state_in, r.source_in))
    ]
    kappa_copy = pltpu.make_async_copy(
        r.kappa_in.at[0, :, :, columns(q)], r.kap.at[:, real, :], r.loc_sem.at[2]
    )

    def beside_copy(side):
        block = r.kappa_in.at[0, :, :, columns(q - 1 + 2 * side)]
        return pltpu.make_async_copy(block, r.beside.at[side], r.loc_sem.at[3 + side])

    own_copies[0].start()
    kappa_copy.start()
    for side in range(2):

        @pl.when(beside_has[side])
        def _():
            beside_copy(side).start()

    own_copies[1].start()

    barrier = pltpu.get_barrier_semaphore()
    for j in range(1, group):
        pl.semaphore_signal(
            barrier, inc=1, device_id={"tm": base + (q + j) % group}, device_id_type=mesh_ids
        )
    greeted = list(flanks)
    if chained:
        greeted += [(has_prev, {"tm": me - group}), (has_next, {"tm": me + group})]
    for has, where in greeted:

        @pl.when(has)
        def _():
            pl.semaphore_signal(barrier, inc=1, device_id=where, device_id_type=mesh_ids)

    expected = group - 1
    for has, _ in greeted:
        expected = expected + jnp.where(has, 1, 0)
    pl.semaphore_wait(barrier, expected)

    def in_copy(a, j):
        d = (q + j) % group
        if a == 0:
            hbm, dst = r.state_in.at[0, 0, :, :, columns(d)], r.u.at[q + 1, planes, real, :]
        else:
            some = pl.ds((a - 1) * piece, piece)
            hbm, dst = r.source_in.at[0, 0, some, :, columns(d)], r.src.at[q, some, real, :]
        if j == 0:
            return pltpu.make_async_copy(hbm, dst, r.in_lsem.at[a])
        return pltpu.make_async_remote_copy(
            src_ref=hbm, dst_ref=dst, send_sem=r.in_ssem.at[a, j - 1],
            recv_sem=r.in_rsem.at[a, j - 1], device_id={"tm": base + d}, device_id_type=mesh_ids,
        )

    def out_copy(a, j, part):
        d = (q + j) % group
        some = pl.ds(part * piece, piece)
        hbm = (r.res_out, r.new_out)[a].at[0, 0, some, :, columns(q)]
        held = (r.res, r.new)[a].at[d, some, real, :]
        if j == 0:
            return pltpu.make_async_copy(held, hbm, r.out_lsem.at[a, part])
        return pltpu.make_async_remote_copy(
            src_ref=held, dst_ref=hbm, send_sem=r.out_ssem.at[a, part, j - 1],
            recv_sem=r.out_rsem.at[a, part, j - 1], device_id={"tm": base + d},
            device_id_type=mesh_ids,
        )

    def strip_copy(f, j):
        d = (q + j) % group
        return pltpu.make_async_remote_copy(
            src_ref=r.strip_send.at[f, d], dst_ref=r.strip_in.at[f, q, :, real, :],
            send_sem=r.strip_ssem.at[f, j - 1], recv_sem=r.strip_rsem.at[f, j - 1],
            device_id={"tm": base + d}, device_id_type=mesh_ids,
        )

    def edge_ref(kind, n, where):
        if kind == 0:
            return r.u.at[n + 1, planes, where, :]
        if kind <= parts:
            return r.src.at[n, pl.ds((kind - 1) * piece, piece), where, :]
        if kind <= parts + 2:
            return r.strip_in.at[kind - parts - 1, n, :, where, :]
        if kind == parts + 3:
            return r.kap.at[:, where, :]
        return r.kap_strip.at[:, where, :]

    def edge_copy(kind, n, number):
        if number == 0:
            source, target = pl.ds(pad, halo), pl.ds(pad + tx, halo)
        else:
            source, target = pl.ds(pad + tx - halo, halo), pl.ds(pad - halo, halo)
        return pltpu.make_async_remote_copy(
            src_ref=edge_ref(kind, n, source), dst_ref=edge_ref(kind, n, target),
            send_sem=r.edge_ssem.at[kind, n, number], recv_sem=r.edge_rsem.at[kind, n, number],
            device_id=flanks[number][1], device_id_type=mesh_ids,
        )

    def edge_start(kind, n=0):
        for number in range(2):

            @pl.when(flanks[number][0])
            def _():
                edge_copy(kind, n, number).start()

    def edge_wait(kind, n=0, send=False):
        for number in range(2):

            @pl.when(flanks[number][0])
            def _():
                if send:
                    edge_copy(kind, n, number).wait_send()
                else:
                    edge_copy(kind, n, 1 - number).wait_recv()

    def edge_recv_wait(kind, n=0):
        for number in range(2):

            @pl.when(flanks[number][0])
            def _():
                edge_copy(kind, n, 1 - number).wait_recv()

    time_refs = [(r.u, group), (r.e1, group), (r.e2, group), (r.me1, 2), (r.me2, 2), (r.te, 1)]
    time_strips = [
        (r.su, group), (r.se1, group), (r.se2, group), (r.sme1, 2), (r.sme2, 2), (r.ste, 1),
    ]

    def time_copies(number):
        made = []
        for kind, (ref, last) in enumerate((time_refs[number], time_strips[number])):
            middle = planes if kind == 0 else pl.ds(0, 2)
            made.append(
                pltpu.make_async_remote_copy(
                    src_ref=ref.at[last, middle, rows(full), :],
                    dst_ref=ref.at[0, middle, rows(full), :],
                    send_sem=r.time_ssem.at[number, kind], recv_sem=r.time_rsem.at[number, kind],
                    device_id={"tm": me + group}, device_id_type=mesh_ids,
                )
            )
        return made

    def time_send(number):
        if chained:

            @pl.when(has_next)
            def _():
                for copy in time_copies(number):
                    copy.start()

    def time_wait(number):
        if chained:

            @pl.when(has_prev)
            def _():
                for copy in time_copies(number):
                    copy.wait_recv()

    for j in order:
        in_copy(0, j).start()
    kappa_copy.wait()
    kappa_kind = parts + 3
    edge_start(kappa_kind)

    f32 = jnp.float32
    tall = r.u.shape[2]

    def blank(count):
        return jnp.zeros((count, width), f32)

    def clear_planes(ref):
        for n in range(ref.shape[0]):
            for plane in (0, nz + 1):
                ref[n, plane] = blank(tall)

    for ref in (r.u, r.c, r.cu, r.e1, r.ce1, r.e2, r.ce2, r.mc, r.me1, r.cme1, r.me2, r.cme2, r.tc, r.te, r.cte):
        clear_planes(ref)

    def clear_rows(p, carry):
        for ref in (r.u, r.c, r.cu, r.e1, r.ce1):
            for n in range(ref.shape[0]):
                ref[n, p + 1, pl.ds(0, halo), :] = blank(halo)
                ref[n, p + 1, pl.ds(tall - halo, halo), :] = blank(halo)
        for ref in (r.e2, r.ce2, r.mc, r.me1, r.cme1, r.me2, r.cme2, r.tc, r.te, r.cte):
            for n in range(ref.shape[0]):
                ref[n, p + 1, pl.ds(halo, halo), :] = blank(halo)
                ref[n, p + 1, pl.ds(tall - pad, halo), :] = blank(halo)
        return carry

    lax.fori_loop(0, nz, clear_rows, 0)
    strips = (r.su, r.sc, r.scu, r.se1, r.sce1, r.se2, r.sce2, r.smc, r.sme1, r.scme1, r.sme2, r.scme2, r.stc, r.ste, r.scte)
    for ref in strips:
        for n in range(ref.shape[0]):
            for side in range(2):
                ref[n, side] = blank(tall)
    if chained:

        @pl.when(jnp.logical_not(has_prev))
        def _():
            def clear_first(p, carry):
                for ref in (r.u, r.e1, r.e2, r.me1, r.me2, r.te):
                    ref[0, p + 1] = blank(tall)
                return carry

            lax.fori_loop(0, nz, clear_first, 0)

    for number, (has, _) in enumerate(flanks):
        edge = pl.ds((pad - halo, pad + tx)[number], halo)

        @pl.when(jnp.logical_not(has))
        def _():
            def clear_edges(p, carry):
                r.kap[p, edge, :] = blank(halo)
                for n in range(group):
                    r.u[n + 1, p + 1, edge, :] = blank(halo)
                    r.src[n, p, edge, :] = blank(halo)
                return carry

            lax.fori_loop(0, nz, clear_edges, 0)
            for side in range(2):
                r.kap_strip[side, edge, :] = blank(halo)
                for f in range(2):
                    for n in range(group):
                        r.strip_in[f, n, side, edge, :] = blank(halo)

    for side in range(2):

        @pl.when(jnp.logical_not(beside_has[side]))
        def _():
            def clear_beside(p, carry):
                r.beside[side, p] = blank(tx)
                return carry

            lax.fori_loop(0, nz, clear_beside, 0)

    lane_tx = lax.broadcasted_iota(jnp.int32, (tx, width), 1)
    lane = lax.broadcasted_iota(jnp.int32, (tx + 2 * halo, width), 1)

    def plane_of(side, lanes):
        return ((lanes + (span // 2, 0)[side]) % width) // span

    inside = [plane_of(side, lane_tx) for side in range(2)]

    def put_strip(packed, side, block, p):
        return jnp.where(inside[side] == p, pltpu.roll(block, span * p + 2, 1), packed)

    nothing = blank(tx)

    def pack_own(f):
        def body(p, packed):
            blocks = [r.own[f, p, :, d * width : (d + 1) * width] for d in range(group)]
            made = []
            for d in range(group):
                left, right = packed[2 * d], packed[2 * d + 1]
                turned_left = blocks[d - 1] if d else None
                turned_right = blocks[d + 1] if d < group - 1 else None
                made.append(left if turned_left is None else put_strip(left, 0, turned_left, p))
                made.append(right if turned_right is None else put_strip(right, 1, turned_right, p))
            return tuple(made)

        packed = lax.fori_loop(0, nz, body, (nothing,) * (2 * group), unroll=2)
        for d in range(group):
            for side in range(2):
                r.strip_send[f, d, side] = packed[2 * d + side]
        for side in range(2):
            r.strip_in[f, q, side, real, :] = r.strip_send[f, q, side]

    for f in range(2):
        own_copies[f].wait()
        pack_own(f)
        for j in order[:3]:
            strip_copy(f, j).start()
        for n in range(group):

            @pl.when(q == n)
            def _():
                edge_start(parts + 1 + f, n)

    for part in range(parts):
        for j in order:
            in_copy(1 + part, j).start()

    for side in range(2):

        @pl.when(beside_has[side])
        def _():
            beside_copy(side).wait()

    def kappa_body(p, packed):
        return tuple(put_strip(packed[side], side, r.beside[side, p], p) for side in range(2))

    packed = lax.fori_loop(0, nz, kappa_body, (nothing, nothing), unroll=2)
    for side in range(2):
        r.kap_strip[side, real, :] = packed[side]
    strip_kappa = parts + 4
    edge_start(strip_kappa)

    level = lax.broadcasted_iota(jnp.int32, (tx + 2 * halo, width), 0)
    below = jnp.where(has_dn, damping, 0.0)
    above = jnp.where(has_up, damping, 0.0)
    damp = jnp.where(level < halo, below, jnp.where(level < halo + tx, damping, above))
    r.damp[0, rows(full), :] = damp
    for side in range(2):
        r.damp[1 + side, rows(full), :] = damp * jnp.where(beside_has[side], 1.0, 0.0)

    first_plane = [plane_of(side, lane) == 0 for side in range(2)]
    last_plane = [plane_of(side, lane) == nz - 1 for side in range(2)]
    inject = [lane % span == 2, lane % span == 1]
    plane_lane = lane // span
    first_lane = lane == 0
    last_lane = lane == width - 1

    def cut(mask, win):
        return mask[: win[1]]

    def pack(packed, value, p, win):
        return jnp.where(cut(plane_lane, win) == p, pltpu.roll(value, span * p + 2, 1), packed)

    def ghosts(ref, n, win):
        left = pltpu.roll(ref[n, 0, rows(win), :], 1, 1)
        right = pltpu.roll(ref[n, 1, rows(win), :], width - 1, 1)
        return jnp.where(cut(inject[0], win), left, right)

    def sideways(value, ghost, p, win):
        edge = pltpu.roll(ghost, width - 2 - span * p, 1)
        left = jnp.where(cut(first_lane, win), edge, pltpu.roll(value, 1, 1))
        right = jnp.where(cut(last_lane, win), edge, pltpu.roll(value, width - 1, 1))
        return left, right

    def across(ref, n, p, win):
        return (
            (ref[n, p + 1, rows(win, -1), :] + ref[n, p + 1, rows(win, 1), :])
            + (ref[n, p, rows(win), :] + ref[n, p + 2, rows(win), :])
        )

    def planes_loop(body, init, first=0, count=None):
        count = nz if count is None else count
        return lax.fori_loop(first, first + count, body, init, unroll=unroll)

    def earlier(ref, n, middle, win):
        if n == 0 and not chained:
            return None
        return ref[n, middle, rows(win), :]

    def pull(v_ref, cv_ref, w, n, ghost, p, win, first):
        v = v_ref[first + n, p + 1, rows(win), :]
        left, right = sideways(v, ghost, p, win)
        total = w.l[n, p, rows(win), :] * left + w.r[n, p, rows(win), :] * right
        total = total + w.c[n, p + 1, rows(win), :] * across(v_ref, first + n, p, win)
        total = total + across(cv_ref, n, p, win)
        before = earlier(v_ref, n, p + 1, win)
        if before is not None:
            total = total + before
        return v, total - w.a[n, p, rows(win), :] * v

    def strip_pull(v_ref, cv_ref, w, n, side, win, first):
        v = v_ref[first + n, side, rows(win), :]
        total = w.sl[n, side, rows(win), :] * pltpu.roll(v, 1, 1)
        total = total + w.sr[n, side, rows(win), :] * pltpu.roll(v, width - 1, 1)
        total = total + w.sd[n, side, rows(win), :] * pltpu.roll(v, span, 1)
        total = total + w.su[n, side, rows(win), :] * pltpu.roll(v, width - span, 1)
        beside = v_ref[first + n, side, rows(win, -1), :] + v_ref[first + n, side, rows(win, 1), :]
        total = total + w.sc[n, side, rows(win), :] * beside
        total = total + (cv_ref[n, side, rows(win, -1), :] + cv_ref[n, side, rows(win, 1), :])
        before = earlier(v_ref, n, side, win)
        if before is not None:
            total = total + before
        return v, total - w.sa[n, side, rows(win), :] * v

    def put_values(v_ref, cv_ref, w, n, side, win, value, packed, first):
        value = jnp.where(cut(inject[side], win), packed, value)
        v_ref[first + n, side, rows(win), :] = value
        cv_ref[n, side, rows(win), :] = w.sc[n, side, rows(win), :] * value

    fine = types.SimpleNamespace(
        l=r.wl, r=r.wr, a=r.wa, c=r.c, d=r.rd, sl=r.swl, sr=r.swr, sd=r.swd, su=r.swu, sa=r.swa, sc=r.sc, sg=r.srd
    )
    mid = types.SimpleNamespace(
        l=r.mwl, r=r.mwr, a=r.mwa, c=r.mc, d=r.mrd, sl=r.smwl, sr=r.smwr, sd=r.smwd, su=r.smwu, sa=r.smwa,
        sc=r.smc, sg=r.smrd,
    )
    top = types.SimpleNamespace(
        l=r.twl, r=r.twr, a=r.twa, c=r.tc, d=r.trd, sl=r.stwl, sr=r.stwr, sd=r.stwd, su=r.stwu, sa=r.stwa,
        sc=r.stc, sg=r.strd,
    )

    wide = blank(full[1])
    edge_recv_wait(kappa_kind)
    edge_recv_wait(strip_kappa)
    kappa_edge = planes_loop(lambda p, packed: pack(packed, r.kap[p, rows(full), :], p, full), wide)

    def slices(body):
        for j in (0, 2, 1, 3):
            body(j)

    def arrived(copies, n_of, then):
        for j in (0,) + order[:3]:
            if j:
                copies(j).wait_recv()
            else:
                copies(j).wait()
        for n in range(group):
            then(n)

    arrived(lambda j: in_copy(0, j), None, lambda n: edge_start(0, n))
    for f in range(2):
        for j in order[:3]:
            strip_copy(f, j).wait_recv()
        for n in range(group):

            @pl.when(q != n)
            def _():
                edge_start(parts + 1 + f, n)

    for n in range(group):
        edge_recv_wait(0, n)
        edge_recv_wait(parts + 1, n)

        def body(p, packed):
            v = r.u[n + 1, p + 1, rows(full), :]
            cc = (half * r.kap[p, rows(full), :]) * (1.0 + v * v)
            r.c[n, p + 1, rows(full), :] = cc
            r.cu[n, p + 1, rows(full), :] = cc * v
            return pack(packed, v, p, full)

        packed = planes_loop(body, wide)
        for side in range(2):
            v = jnp.where(inject[side], packed, r.strip_in[0, n, side, rows(full), :])
            kk = jnp.where(inject[side], kappa_edge, r.kap_strip[side, rows(full), :])
            cc = (half * kk) * (1.0 + v * v)
            r.su[n + 1, side, rows(full), :] = v
            r.sc[n, side, rows(full), :] = cc
            r.scu[n, side, rows(full), :] = cc * v
    time_send(0)
    time_wait(0)

    for n in range(group):
        for side in range(2):
            cc = r.sc[n, side, rows(full), :]
            total = r.sc[n, side, rows(full, -1), :] + r.sc[n, side, rows(full, 1), :]
            for ref, shift, off in (
                (r.swl, 1, None), (r.swr, width - 1, None),
                (r.swd, span, first_plane[side]), (r.swu, width - span, last_plane[side]),
            ):
                near = pltpu.roll(cc, shift, 1)
                weight = cc + near
                if off is not None:
                    near, weight = jnp.where(off, 0.0, near), jnp.where(off, 0.0, weight)
                ref[n, side, rows(full), :] = weight
                total = total + near
            diagonal = 1.0 + (6.0 * cc + total)
            r.swa[n, side, rows(full), :] = diagonal
            r.srd[n, side, rows(full), :] = r.damp[1 + side, rows(full), :] / diagonal
        ghost_c, ghost_u = ghosts(r.sc, n, full), ghosts(r.su, n + 1, full)

        def body(p, carry):
            cc = r.c[n, p + 1, rows(full), :]
            left, right = sideways(cc, ghost_c, p, full)
            left, right = cc + left, cc + right
            r.wl[n, p, rows(full), :] = left
            r.wr[n, p, rows(full), :] = right
            diagonal = 1.0 + ((4.0 * cc + left) + (right + across(r.c, n, p, full)))
            r.wa[n, p, rows(full), :] = diagonal
            r.rd[n, p, rows(full), :] = r.damp[0, rows(full), :] / diagonal
            _, total = pull(r.u, r.cu, fine, n, ghost_u, p, full, 1)
            r.res[n, p, rows(full), :] = total
            return carry

        planes_loop(body, 0)
        for side in range(2):
            _, total = strip_pull(r.su, r.scu, fine, n, side, full, 1)
            r.sres[n, side, rows(full), :] = total

    pairs = ((mid, fine, 2), (top, mid, 1))
    for to, of, count in pairs:
        for n in range(count):

            def body(p, carry):
                to.c[n, p + 1, rows(full), :] = of.c[2 * n, p + 1, rows(full), :] + of.c[2 * n + 1, p + 1, rows(full), :]
                for one, two in ((to.l, of.l), (to.r, of.r)):
                    one[n, p, rows(full), :] = two[2 * n, p, rows(full), :] + two[2 * n + 1, p, rows(full), :]
                diagonal = (of.a[2 * n, p, rows(full), :] - 1.0) + of.a[2 * n + 1, p, rows(full), :]
                to.a[n, p, rows(full), :] = diagonal
                to.d[n, p, rows(full), :] = r.damp[0, rows(full), :] / diagonal
                return carry

            planes_loop(body, 0)
            for side in range(2):
                for one, two in (
                    (to.sc, of.sc), (to.sl, of.sl), (to.sr, of.sr), (to.sd, of.sd), (to.su, of.su),
                ):
                    one[n, side, rows(full), :] = two[2 * n, side, rows(full), :] + two[2 * n + 1, side, rows(full), :]
                diagonal = (of.sa[2 * n, side, rows(full), :] - 1.0) + of.sa[2 * n + 1, side, rows(full), :]
                to.sa[n, side, rows(full), :] = diagonal
                to.sg[n, side, rows(full), :] = r.damp[1 + side, rows(full), :] / diagonal

    for n in range(group):
        edge_recv_wait(parts + 2, n)

    def first_update(n, part, win, packed):
        def body(p, packed):
            left = r.src[n, p, rows(win), :] + r.res[n, p, rows(win), :]
            r.res[n, p, rows(win), :] = left
            update = left * r.rd[n, p, rows(win), :]
            r.e1[n + 1, p + 1, rows(win), :] = update
            r.ce1[n, p + 1, rows(win), :] = r.c[n, p + 1, rows(win), :] * update
            return pack(packed, update, p, win)

        return planes_loop(body, packed, part * piece, piece)

    outer = [(pad - halo, halo), (pad + tx, halo)]
    for part in range(parts):
        kind = 1 + part
        arrived(lambda j: in_copy(kind, j), None, lambda n: edge_start(kind, n))
        for n in range(group):
            packed = r.packed_one[n, rows(core), :] if part else nothing
            r.packed_one[n, rows(core), :] = first_update(n, part, core, packed)
        for j in order:
            out_copy(0, j, part).start()
        for n in range(group):
            edge_recv_wait(kind, n)
            for win in outer:
                packed = r.packed_one[n, rows(win), :] if part else blank(halo)
                r.packed_one[n, rows(win), :] = first_update(n, part, win, packed)
    for n in range(group):
        for side in range(2):
            left = r.strip_in[1, n, side, rows(full), :] + r.sres[n, side, rows(full), :]
            r.sres[n, side, rows(full), :] = left
            put_values(
                r.se1, r.sce1, fine, n, side, full, left * r.srd[n, side, rows(full), :],
                r.packed_one[n, rows(full), :], 1,
            )
    time_send(1)
    time_wait(1)

    narrow = blank(trim[1])

    def again(w, v, cv, sv, scv, b, sb, to_v, to_cv, to_sv, to_scv, count):
        for n in range(count):
            ghost = ghosts(sv, n + 1, trim)

            def body(p, packed):
                value, total = pull(v, cv, w, n, ghost, p, trim, 1)
                left = b[n, p, rows(trim), :] + total
                update = value + left * w.d[n, p, rows(trim), :]
                to_v[n + 1, p + 1, rows(trim), :] = update
                to_cv[n, p + 1, rows(trim), :] = w.c[n, p + 1, rows(trim), :] * update
                return pack(packed, update, p, trim)

            packed = planes_loop(body, narrow)
            for side in range(2):
                value, total = strip_pull(sv, scv, w, n, side, trim, 1)
                left = sb[n, side, rows(trim), :] + total
                update = value + left * w.sg[n, side, rows(trim), :]
                put_values(to_sv, to_scv, w, n, side, trim, update, packed, 1)

    def coarsen(w, to, v, cv, sv, scv, b, sb, to_b, to_sb, to_v, to_cv, to_sv, to_scv, count):
        for n in range(count):
            pair = [ghosts(sv, 2 * n + i + 1, trim) for i in range(2)]

            def body(p, packed):
                rhs = None
                for i in range(2):
                    _, total = pull(v, cv, w, 2 * n + i, pair[i], p, trim, 1)
                    left = b[2 * n + i, p, rows(trim), :] + total
                    rhs = left if rhs is None else rhs + left
                to_b[n, p, rows(trim), :] = rhs
                update = rhs * to.d[n, p, rows(trim), :]
                to_v[n + 1, p + 1, rows(trim), :] = update
                to_cv[n, p + 1, rows(trim), :] = to.c[n, p + 1, rows(trim), :] * update
                return pack(packed, update, p, trim)

            packed = planes_loop(body, narrow)
            for side in range(2):
                rhs = None
                for i in range(2):
                    _, total = strip_pull(sv, scv, w, 2 * n + i, side, trim, 1)
                    left = sb[2 * n + i, side, rows(trim), :] + total
                    rhs = left if rhs is None else rhs + left
                to_sb[n, side, rows(trim), :] = rhs
                update = rhs * to.sg[n, side, rows(trim), :]
                put_values(to_sv, to_scv, to, n, side, trim, update, packed, 1)

    again(fine, r.e1, r.ce1, r.se1, r.sce1, r.res, r.sres, r.e2, r.ce2, r.se2, r.sce2, group)
    time_send(2)
    time_wait(2)
    coarsen(
        fine, mid, r.e2, r.ce2, r.se2, r.sce2, r.res, r.sres, r.mb, r.smb, r.me1, r.cme1, r.sme1, r.scme1, 2
    )
    time_send(3)
    time_wait(3)
    again(mid, r.me1, r.cme1, r.sme1, r.scme1, r.mb, r.smb, r.me2, r.cme2, r.sme2, r.scme2, 2)
    time_send(4)
    time_wait(4)
    coarsen(
        mid, top, r.me2, r.cme2, r.sme2, r.scme2, r.mb, r.smb, r.tb, r.stb, r.te, r.cte, r.ste, r.scte, 1
    )
    time_send(5)
    time_wait(5)
    ghost = ghosts(r.ste, 1, core)

    def body(p, carry):
        value, total = pull(r.te, r.cte, top, 0, ghost, p, core, 1)
        update = value + (r.tb[0, p, real, :] + total) * r.trd[0, p, real, :]
        for n in range(group):
            middle = r.me2[n // 2 + 1, p + 1, real, :] + update
            r.new[n, p, real, :] = r.u[n + 1, p + 1, real, :] + (r.e2[n + 1, p + 1, real, :] + middle)
        return carry

    for part in range(parts):
        planes_loop(body, 0, part * piece, piece)
        for j in order:
            out_copy(1, j, part).start()

    for f in range(2):
        for j in order[:3]:
            strip_copy(f, j).wait_send()
    for a in range(1 + parts):
        for j in order[:3]:
            in_copy(a, j).wait_send()
    for kind in range(parts + 3):
        for n in range(group):
            edge_wait(kind, n, True)
    edge_wait(kappa_kind, 0, True)
    edge_wait(strip_kappa, 0, True)
    if chained:

        @pl.when(has_next)
        def _():
            for number in range(len(time_refs)):
                for copy in time_copies(number):
                    copy.wait_send()

    for a in range(2):
        for part in range(parts):
            for j in order:
                if j == 0:
                    out_copy(a, j, part).wait()
                else:
                    out_copy(a, j, part).wait_send()
                    out_copy(a, j, part).wait_recv()


def shards(tm_size, space_size, iterate, source_term, conductivity):
    _, nz, tx, ty = conductivity.shape
    width = ty // group
    tall = tx + 2 * pad
    f32 = jnp.float32
    dma = pltpu.SemaphoreType.DMA
    kinds = parts + 5

    def padded(count):
        return pltpu.VMEM((count, nz + 2, tall, width), f32)

    def plain(*lead):
        return pltpu.VMEM((*lead, nz, tall, width), f32)

    def strip(*lead):
        return pltpu.VMEM((*lead, 2, tall, width), f32)

    scratch = {"packed": pltpu.VMEM((1, nz, 8, width), f32)}
    scratch |= {name: padded(count) for name, count in (
        ("u", 5), ("c", 4), ("cu", 4), ("e1", 5), ("ce1", 4), ("e2", 5), ("ce2", 4), ("mc", 2), ("me1", 3),
        ("cme1", 2), ("me2", 3), ("cme2", 2), ("tc", 1), ("te", 2), ("cte", 1),
    )}
    scratch |= {name: plain(count) for name, count in (
        ("src", 4), ("res", 4), ("wl", 4), ("wr", 4), ("wa", 4), ("rd", 4), ("mwl", 2), ("mwr", 2), ("mwa", 2),
        ("mrd", 2), ("mb", 2), ("twl", 1), ("twr", 1), ("twa", 1), ("trd", 1), ("tb", 1), ("new", 4),
    )}
    scratch["kap"] = plain()
    scratch |= {name: strip(count) for name, count in (
        ("su", 5), ("sc", 4), ("scu", 4), ("se1", 5), ("sce1", 4), ("se2", 5), ("sce2", 4), ("smc", 2),
        ("sme1", 3), ("scme1", 2), ("sme2", 3), ("scme2", 2), ("stc", 1), ("ste", 2), ("scte", 1),
        ("swl", 4), ("swr", 4), ("swd", 4), ("swu", 4), ("swa", 4), ("srd", 4), ("sres", 4),
        ("smwl", 2), ("smwr", 2), ("smwd", 2), ("smwu", 2), ("smwa", 2), ("smrd", 2), ("smb", 2),
        ("stwl", 1), ("stwr", 1), ("stwd", 1), ("stwu", 1), ("stwa", 1), ("strd", 1), ("stb", 1),
    )}
    scratch["kap_strip"] = strip()
    scratch["strip_in"] = strip(2, group)
    scratch["strip_send"] = pltpu.VMEM((2, group, 2, tx, width), f32)
    scratch["own"] = pltpu.VMEM((2, nz, tx, ty), f32)
    scratch["beside"] = pltpu.VMEM((2, nz, tx, width), f32)
    scratch["packed_one"] = pltpu.VMEM((group, tall, width), f32)
    scratch["damp"] = pltpu.VMEM((3, tall, width), f32)
    for name, shape in (
        ("loc_sem", (5,)), ("in_lsem", (1 + parts,)), ("in_ssem", (1 + parts, group - 1)),
        ("in_rsem", (1 + parts, group - 1)), ("out_lsem", (2, parts)), ("out_ssem", (2, parts, group - 1)),
        ("out_rsem", (2, parts, group - 1)), ("strip_ssem", (2, group - 1)), ("strip_rsem", (2, group - 1)),
        ("edge_ssem", (kinds, group, 2)), ("edge_rsem", (kinds, group, 2)), ("time_ssem", (6, 2)),
        ("time_rsem", (6, 2)),
    ):
        scratch[name] = dma(shape)
    names = ("state_in", "source_in", "kappa_in", "new_out", "res_out", *scratch)
    out = jax.ShapeDtypeStruct(iterate.shape, f32)
    hbm = pl.BlockSpec(memory_space=pltpu.HBM)
    return pl.pallas_call(
        functools.partial(kernel, tm_size, space_size, names),
        out_shape=(out, out),
        in_specs=[hbm] * 3,
        out_specs=(hbm, hbm),
        scratch_shapes=list(scratch.values()),
        compiler_params=pltpu.CompilerParams(
            collective_id=0, has_side_effects=True, vmem_limit_bytes=67043328
        ),
    )(iterate, source_term, conductivity)


def solution(mesh):
    tiled = P("tm", "space", None, None, None)
    in_specs = (tiled, tiled, P("space", None, None, None))
    body = functools.partial(shards, mesh.shape["tm"], mesh.shape["space"])
    return jax.shard_map(
        body, mesh=mesh, in_specs=in_specs, out_specs=(tiled, tiled), check_vma=False
    )
```

```python
import functools
import types

import jax
import jax.numpy as jnp
from jax import lax
from jax.experimental import pallas as pl
from jax.experimental.pallas import tpu as pltpu
from jax.sharding import PartitionSpec as P

tau_step = 0.08
damping = 0.7
group = 4
halo = 8
pad = 2 * halo
parts = 4
out_parts = 2
mesh_ids = pl.DeviceIdType.MESH
order = (2, 1, 3, 0)
unroll = 8


def kernel(tm_size, space_size, names, *refs):
    r = types.SimpleNamespace(**dict(zip(names, refs)))
    _, nz, tx, _ = r.kappa_in.shape
    width = r.kap.shape[-1]
    span = width // nz
    chained = tm_size > group
    half = 0.5 * tau_step
    piece, out_piece = nz // parts, nz // out_parts

    full = (pad - halo, tx + 2 * halo)
    trim = (pad - halo // 2, tx + halo)
    core = (pad, tx)

    def rows(win, shift=0):
        return pl.ds(win[0] + shift, win[1])

    real = rows(core)
    planes = pl.ds(1, nz)
    me = lax.axis_index("tm")
    sp = lax.axis_index("space")
    q = me % group
    base = me - q
    has_dn, has_up = sp > 0, sp < space_size - 1
    has_left, has_right = q > 0, q < group - 1
    has_prev, has_next = base > 0, base + group < tm_size
    flanks = [(has_dn, {"space": sp - 1}), (has_up, {"space": sp + 1})]
    beside_has = [has_left, has_right]

    def columns(d):
        return pl.ds(pl.multiple_of(d * width, width), width)

    own_copies = [
        pltpu.make_async_copy(hbm.at[0, 0], r.own.at[f], r.loc_sem.at[f])
        for f, hbm in enumerate((r.state_in, r.source_in))
    ]
    kappa_copy = pltpu.make_async_copy(
        r.kappa_in.at[0, :, :, columns(q)], r.kap.at[:, real, :], r.loc_sem.at[2]
    )

    def beside_copy(side):
        block = r.kappa_in.at[0, :, :, columns(q - 1 + 2 * side)]
        return pltpu.make_async_copy(block, r.beside.at[side], r.loc_sem.at[3 + side])

    own_copies[0].start()
    kappa_copy.start()
    for side in range(2):

        @pl.when(beside_has[side])
        def _():
            beside_copy(side).start()

    own_copies[1].start()

    barrier = pltpu.get_barrier_semaphore()
    for j in range(1, group):
        pl.semaphore_signal(
            barrier, inc=1, device_id={"tm": base + (q + j) % group}, device_id_type=mesh_ids
        )
    greeted = list(flanks)
    if chained:
        greeted += [(has_prev, {"tm": me - group}), (has_next, {"tm": me + group})]
    for has, where in greeted:

        @pl.when(has)
        def _():
            pl.semaphore_signal(barrier, inc=1, device_id=where, device_id_type=mesh_ids)

    expected = group - 1
    for has, _ in greeted:
        expected = expected + jnp.where(has, 1, 0)
    pl.semaphore_wait(barrier, expected)

    def in_copy(a, j):
        d = (q + j) % group
        if a == 0:
            hbm, dst = r.state_in.at[0, 0, :, :, columns(d)], r.u.at[q + 1, planes, real, :]
        else:
            some = pl.ds((a - 1) * piece, piece)
            hbm, dst = r.source_in.at[0, 0, some, :, columns(d)], r.src.at[q, some, real, :]
        if j == 0:
            return pltpu.make_async_copy(hbm, dst, r.in_lsem.at[a])
        return pltpu.make_async_remote_copy(
            src_ref=hbm, dst_ref=dst, send_sem=r.in_ssem.at[a, j - 1],
            recv_sem=r.in_rsem.at[a, j - 1], device_id={"tm": base + d}, device_id_type=mesh_ids,
        )

    def out_copy(a, j, part):
        d = (q + j) % group
        some = pl.ds(part * out_piece, out_piece)
        hbm = (r.res_out, r.new_out)[a].at[0, 0, some, :, columns(q)]
        held = (r.res, r.new)[a].at[d, some, real, :]
        if j == 0:
            return pltpu.make_async_copy(held, hbm, r.out_lsem.at[a, part])
        return pltpu.make_async_remote_copy(
            src_ref=held, dst_ref=hbm, send_sem=r.out_ssem.at[a, part, j - 1],
            recv_sem=r.out_rsem.at[a, part, j - 1], device_id={"tm": base + d},
            device_id_type=mesh_ids,
        )

    def strip_copy(f, j):
        d = (q + j) % group
        return pltpu.make_async_remote_copy(
            src_ref=r.strip_send.at[f, d], dst_ref=r.strip_in.at[f, q, :, real, :],
            send_sem=r.strip_ssem.at[f, j - 1], recv_sem=r.strip_rsem.at[f, j - 1],
            device_id={"tm": base + d}, device_id_type=mesh_ids,
        )

    def edge_ref(kind, n, where):
        if kind == 0:
            return r.u.at[n + 1, planes, where, :]
        if kind <= parts:
            return r.src.at[n, pl.ds((kind - 1) * piece, piece), where, :]
        if kind <= parts + 2:
            return r.strip_in.at[kind - parts - 1, n, :, where, :]
        if kind == parts + 3:
            return r.kap.at[:, where, :]
        return r.kap_strip.at[:, where, :]

    def edge_copy(kind, n, number):
        if number == 0:
            source, target = pl.ds(pad, halo), pl.ds(pad + tx, halo)
        else:
            source, target = pl.ds(pad + tx - halo, halo), pl.ds(pad - halo, halo)
        return pltpu.make_async_remote_copy(
            src_ref=edge_ref(kind, n, source), dst_ref=edge_ref(kind, n, target),
            send_sem=r.edge_ssem.at[kind, n, number], recv_sem=r.edge_rsem.at[kind, n, number],
            device_id=flanks[number][1], device_id_type=mesh_ids,
        )

    def edge_start(kind, n=0):
        for number in range(2):

            @pl.when(flanks[number][0])
            def _():
                edge_copy(kind, n, number).start()

    def edge_send_wait(kind, n=0):
        for number in range(2):

            @pl.when(flanks[number][0])
            def _():
                edge_copy(kind, n, number).wait_send()

    def edge_recv_wait(kind, n=0):
        for number in range(2):

            @pl.when(flanks[number][0])
            def _():
                edge_copy(kind, n, 1 - number).wait_recv()

    time_refs = [(r.u, group), (r.e1, group), (r.e2, group), (r.me1, 2), (r.me2, 2), (r.te, 1)]
    time_strips = [
        (r.su, group), (r.se1, group), (r.se2, group), (r.sme1, 2), (r.sme2, 2), (r.ste, 1),
    ]

    def time_copies(number):
        made = []
        for kind, (ref, last) in enumerate((time_refs[number], time_strips[number])):
            middle = planes if kind == 0 else pl.ds(0, 2)
            made.append(
                pltpu.make_async_remote_copy(
                    src_ref=ref.at[last, middle, rows(full), :],
                    dst_ref=ref.at[0, middle, rows(full), :],
                    send_sem=r.time_ssem.at[number, kind], recv_sem=r.time_rsem.at[number, kind],
                    device_id={"tm": me + group}, device_id_type=mesh_ids,
                )
            )
        return made

    def time_send(number):
        if chained:

            @pl.when(has_next)
            def _():
                for copy in time_copies(number):
                    copy.start()

    def time_wait(number):
        if chained:

            @pl.when(has_prev)
            def _():
                for copy in time_copies(number):
                    copy.wait_recv()

    for j in order:
        in_copy(0, j).start()
    kappa_copy.wait()
    kappa_kind = parts + 3
    edge_start(kappa_kind)

    f32 = jnp.float32
    tall = r.u.shape[2]

    def blank(count):
        return jnp.zeros((count, width), f32)

    for side in range(2):

        @pl.when(jnp.logical_not(beside_has[side]))
        def _():
            def clear_beside(p, carry):
                r.beside[side, p] = blank(tx)
                return carry

            lax.fori_loop(0, nz, clear_beside, 0)

    lane_tx = lax.broadcasted_iota(jnp.int32, (tx, width), 1)
    lane = lax.broadcasted_iota(jnp.int32, (tx + 2 * halo, width), 1)

    def plane_of(side, lanes):
        return ((lanes + (span // 2, 0)[side]) % width) // span

    inside = [plane_of(side, lane_tx) for side in range(2)]

    def put_strip(packed, side, block, p):
        return jnp.where(inside[side] == p, pltpu.roll(block, span * p + 2, 1), packed)

    nothing = blank(tx)

    def pack_own(f):
        def body(p, packed):
            blocks = [r.own[f, p, :, d * width : (d + 1) * width] for d in range(group)]
            made = []
            for d in range(group):
                left, right = packed[2 * d], packed[2 * d + 1]
                turned_left = blocks[d - 1] if d else None
                turned_right = blocks[d + 1] if d < group - 1 else None
                made.append(left if turned_left is None else put_strip(left, 0, turned_left, p))
                made.append(right if turned_right is None else put_strip(right, 1, turned_right, p))
            return tuple(made)

        packed = lax.fori_loop(0, nz, body, (nothing,) * (2 * group), unroll=2)
        for d in range(group):
            for side in range(2):
                r.strip_send[f, d, side] = packed[2 * d + side]
        for side in range(2):
            r.strip_in[f, q, side, real, :] = r.strip_send[f, q, side]

    for f in range(2):
        own_copies[f].wait()
        pack_own(f)
        for j in order[:3]:
            strip_copy(f, j).start()
        for n in range(group):

            @pl.when(q == n)
            def _():
                edge_start(parts + 1 + f, n)

    for part in range(parts):
        for j in order:
            in_copy(1 + part, j).start()

    held = [(ref, 1) for ref, _ in time_refs]
    held += [(ref, 0) for ref in (r.c, r.cu, r.ce1, r.ce2, r.mc, r.cme1, r.cme2, r.tc, r.cte)]
    early = (r.u, r.c, r.cu, r.e1, r.ce1)
    for ref, first in held:
        for n in range(first, ref.shape[0]):
            for plane in (0, nz + 1):
                ref[n, plane] = blank(tall)

    def clear_rows(p, carry):
        for ref, first in held:
            outer = any(ref is one for one in early)
            low, high = (0, tall - halo) if outer else (halo, tall - pad)
            for n in range(first, ref.shape[0]):
                ref[n, p + 1, pl.ds(low, halo), :] = blank(halo)
                ref[n, p + 1, pl.ds(high, halo), :] = blank(halo)
        return carry

    lax.fori_loop(0, nz, clear_rows, 0)
    strips = [(ref, 1) for ref, _ in time_strips]
    strips += [(ref, 0) for ref in (r.sc, r.scu, r.sce1, r.sce2, r.smc, r.scme1, r.scme2, r.stc, r.scte)]
    for ref, first in strips:
        for n in range(first, ref.shape[0]):
            for side in range(2):
                ref[n, side] = blank(tall)
    if chained:

        @pl.when(jnp.logical_not(has_prev))
        def _():
            def clear_first(p, carry):
                for ref, _ in time_refs:
                    ref[0, p + 1] = blank(tall)
                return carry

            lax.fori_loop(0, nz, clear_first, 0)
            for ref, _ in time_strips:
                for side in range(2):
                    ref[0, side] = blank(tall)

    for number, (has, _) in enumerate(flanks):
        edge = pl.ds((pad - halo, pad + tx)[number], halo)

        @pl.when(jnp.logical_not(has))
        def _():
            def clear_edges(p, carry):
                r.kap[p, edge, :] = blank(halo)
                for n in range(group):
                    r.u[n + 1, p + 1, edge, :] = blank(halo)
                    r.src[n, p, edge, :] = blank(halo)
                return carry

            lax.fori_loop(0, nz, clear_edges, 0)
            for side in range(2):
                r.kap_strip[side, edge, :] = blank(halo)
                for f in range(2):
                    for n in range(group):
                        r.strip_in[f, n, side, edge, :] = blank(halo)

    for side in range(2):

        @pl.when(beside_has[side])
        def _():
            beside_copy(side).wait()

    def kappa_body(p, packed):
        return tuple(put_strip(packed[side], side, r.beside[side, p], p) for side in range(2))

    packed = lax.fori_loop(0, nz, kappa_body, (nothing, nothing), unroll=2)
    for side in range(2):
        r.kap_strip[side, real, :] = packed[side]
    strip_kappa = parts + 4
    edge_start(strip_kappa)

    level = lax.broadcasted_iota(jnp.int32, (tx + 2 * halo, width), 0)
    below = jnp.where(has_dn, damping, 0.0)
    above = jnp.where(has_up, damping, 0.0)
    damp = jnp.where(level < halo, below, jnp.where(level < halo + tx, damping, above))
    r.damp[0, rows(full), :] = damp
    for side in range(2):
        r.damp[1 + side, rows(full), :] = damp * jnp.where(beside_has[side], 1.0, 0.0)

    first_plane = [plane_of(side, lane) == 0 for side in range(2)]
    last_plane = [plane_of(side, lane) == nz - 1 for side in range(2)]
    inject = [lane % span == 2, lane % span == 1]
    plane_lane = lane // span
    first_lane = lane == 0
    last_lane = lane == width - 1

    def cut(mask, win):
        return mask[: win[1]]

    def pack(packed, value, p, win):
        return jnp.where(cut(plane_lane, win) == p, pltpu.roll(value, span * p + 2, 1), packed)

    def pack_planes(ref, n, win, packed, first=0, count=None):
        def body(p, packed):
            return pack(packed, ref[n, p + 1, rows(win), :], p, win)

        return planes_loop(body, packed, first, count)

    def ghosts(ref, n, win):
        left = pltpu.roll(ref[n, 0, rows(win), :], 1, 1)
        right = pltpu.roll(ref[n, 1, rows(win), :], width - 1, 1)
        return jnp.where(cut(inject[0], win), left, right)

    def sideways(value, ghost, p, win):
        edge = pltpu.roll(ghost, width - 2 - span * p, 1)
        left = jnp.where(cut(first_lane, win), edge, pltpu.roll(value, 1, 1))
        right = jnp.where(cut(last_lane, win), edge, pltpu.roll(value, width - 1, 1))
        return left, right

    def across(ref, n, p, win):
        return (
            (ref[n, p + 1, rows(win, -1), :] + ref[n, p + 1, rows(win, 1), :])
            + (ref[n, p, rows(win), :] + ref[n, p + 2, rows(win), :])
        )

    def planes_loop(body, init, first=0, count=None):
        count = nz if count is None else count
        return lax.fori_loop(first, first + count, body, init, unroll=min(unroll, count))

    def earlier(ref, n, middle, win):
        if n == 0 and not chained:
            return None
        return ref[n, middle, rows(win), :]

    def pull(v_ref, cv_ref, w, n, ghost, p, win, first):
        v = v_ref[first + n, p + 1, rows(win), :]
        left, right = sideways(v, ghost, p, win)
        total = w.l[n, p, rows(win), :] * left + w.r[n, p, rows(win), :] * right
        total = total + w.c[n, p + 1, rows(win), :] * across(v_ref, first + n, p, win)
        total = total + across(cv_ref, n, p, win)
        before = earlier(v_ref, n, p + 1, win)
        if before is not None:
            total = total + before
        return v, total - w.a[n, p, rows(win), :] * v

    def strip_pull(v_ref, cv_ref, w, n, side, win, first):
        v = v_ref[first + n, side, rows(win), :]
        total = w.sl[n, side, rows(win), :] * pltpu.roll(v, 1, 1)
        total = total + w.sr[n, side, rows(win), :] * pltpu.roll(v, width - 1, 1)
        total = total + w.sd[n, side, rows(win), :] * pltpu.roll(v, span, 1)
        total = total + w.su[n, side, rows(win), :] * pltpu.roll(v, width - span, 1)
        beside = v_ref[first + n, side, rows(win, -1), :] + v_ref[first + n, side, rows(win, 1), :]
        total = total + w.sc[n, side, rows(win), :] * beside
        total = total + (cv_ref[n, side, rows(win, -1), :] + cv_ref[n, side, rows(win, 1), :])
        before = earlier(v_ref, n, side, win)
        if before is not None:
            total = total + before
        return v, total - w.sa[n, side, rows(win), :] * v

    def put_values(v_ref, cv_ref, w, n, side, win, value, packed, first):
        value = jnp.where(cut(inject[side], win), packed, value)
        v_ref[first + n, side, rows(win), :] = value
        cv_ref[n, side, rows(win), :] = w.sc[n, side, rows(win), :] * value

    fine = types.SimpleNamespace(
        l=r.wl, r=r.wr, a=r.wa, c=r.c, d=r.rd, sl=r.swl, sr=r.swr, sd=r.swd, su=r.swu, sa=r.swa, sc=r.sc, sg=r.srd
    )
    mid = types.SimpleNamespace(
        l=r.mwl, r=r.mwr, a=r.mwa, c=r.mc, d=r.mrd, sl=r.smwl, sr=r.smwr, sd=r.smwd, su=r.smwu, sa=r.smwa,
        sc=r.smc, sg=r.smrd,
    )
    top = types.SimpleNamespace(
        l=r.twl, r=r.twr, a=r.twa, c=r.tc, d=r.trd, sl=r.stwl, sr=r.stwr, sd=r.stwd, su=r.stwu, sa=r.stwa,
        sc=r.stc, sg=r.strd,
    )

    wide = blank(full[1])
    edge_recv_wait(kappa_kind)
    edge_recv_wait(strip_kappa)
    kappa_edge = planes_loop(lambda p, packed: pack(packed, r.kap[p, rows(full), :], p, full), wide)

    def arrived(a):
        in_copy(a, 0).wait()
        for j in order[:3]:
            in_copy(a, j).wait_recv()
        for n in range(group):
            edge_start(a, n)

    arrived(0)
    for f in range(2):
        for j in order[:3]:
            strip_copy(f, j).wait_recv()
        for n in range(group):

            @pl.when(q != n)
            def _():
                edge_start(parts + 1 + f, n)

    for n in range(group):
        edge_recv_wait(0, n)
        edge_recv_wait(parts + 1, n)

        def body(p, carry):
            v = r.u[n + 1, p + 1, rows(full), :]
            cc = (half * r.kap[p, rows(full), :]) * (1.0 + v * v)
            r.c[n, p + 1, rows(full), :] = cc
            r.cu[n, p + 1, rows(full), :] = cc * v
            return carry

        planes_loop(body, 0)
        packed = pack_planes(r.u, n + 1, full, wide)
        for side in range(2):
            v = jnp.where(inject[side], packed, r.strip_in[0, n, side, rows(full), :])
            kk = jnp.where(inject[side], kappa_edge, r.kap_strip[side, rows(full), :])
            cc = (half * kk) * (1.0 + v * v)
            r.su[n + 1, side, rows(full), :] = v
            r.sc[n, side, rows(full), :] = cc
            r.scu[n, side, rows(full), :] = cc * v
    time_send(0)
    time_wait(0)

    for n in range(group):
        for side in range(2):
            cc = r.sc[n, side, rows(full), :]
            total = r.sc[n, side, rows(full, -1), :] + r.sc[n, side, rows(full, 1), :]
            for ref, shift, off in (
                (r.swl, 1, None), (r.swr, width - 1, None),
                (r.swd, span, first_plane[side]), (r.swu, width - span, last_plane[side]),
            ):
                near = pltpu.roll(cc, shift, 1)
                weight = cc + near
                if off is not None:
                    near, weight = jnp.where(off, 0.0, near), jnp.where(off, 0.0, weight)
                ref[n, side, rows(full), :] = weight
                total = total + near
            diagonal = 1.0 + (6.0 * cc + total)
            r.swa[n, side, rows(full), :] = diagonal
            r.srd[n, side, rows(full), :] = r.damp[1 + side, rows(full), :] / diagonal
        ghost_c, ghost_u = ghosts(r.sc, n, full), ghosts(r.su, n + 1, full)

        def body(p, carry):
            cc = r.c[n, p + 1, rows(full), :]
            left, right = sideways(cc, ghost_c, p, full)
            left, right = cc + left, cc + right
            r.wl[n, p, rows(full), :] = left
            r.wr[n, p, rows(full), :] = right
            diagonal = 1.0 + ((4.0 * cc + left) + (right + across(r.c, n, p, full)))
            r.wa[n, p, rows(full), :] = diagonal
            r.rd[n, p, rows(full), :] = r.damp[0, rows(full), :] / diagonal
            _, total = pull(r.u, r.cu, fine, n, ghost_u, p, full, 1)
            r.res[n, p, rows(full), :] = total
            return carry

        planes_loop(body, 0)
        for side in range(2):
            _, total = strip_pull(r.su, r.scu, fine, n, side, full, 1)
            r.sres[n, side, rows(full), :] = total
        if n == 1:
            arrived(1)
    arrived(2)

    pairs = ((mid, fine, 2), (top, mid, 1))
    for to, of, count in pairs:
        for n in range(count):

            def body(p, carry):
                to.c[n, p + 1, rows(full), :] = of.c[2 * n, p + 1, rows(full), :] + of.c[2 * n + 1, p + 1, rows(full), :]
                for one, two in ((to.l, of.l), (to.r, of.r)):
                    one[n, p, rows(full), :] = two[2 * n, p, rows(full), :] + two[2 * n + 1, p, rows(full), :]
                diagonal = (of.a[2 * n, p, rows(full), :] - 1.0) + of.a[2 * n + 1, p, rows(full), :]
                to.a[n, p, rows(full), :] = diagonal
                to.d[n, p, rows(full), :] = r.damp[0, rows(full), :] / diagonal
                return carry

            planes_loop(body, 0)
            for side in range(2):
                for one, two in (
                    (to.sc, of.sc), (to.sl, of.sl), (to.sr, of.sr), (to.sd, of.sd), (to.su, of.su),
                ):
                    one[n, side, rows(full), :] = two[2 * n, side, rows(full), :] + two[2 * n + 1, side, rows(full), :]
                diagonal = (of.sa[2 * n, side, rows(full), :] - 1.0) + of.sa[2 * n + 1, side, rows(full), :]
                to.sa[n, side, rows(full), :] = diagonal
                to.sg[n, side, rows(full), :] = r.damp[1 + side, rows(full), :] / diagonal

    for n in range(group):
        edge_recv_wait(parts + 2, n)

    def first_update(n, part, win):
        def body(p, carry):
            left = r.src[n, p, rows(win), :] + r.res[n, p, rows(win), :]
            r.res[n, p, rows(win), :] = left
            update = left * r.rd[n, p, rows(win), :]
            r.e1[n + 1, p + 1, rows(win), :] = update
            r.ce1[n, p + 1, rows(win), :] = r.c[n, p + 1, rows(win), :] * update
            return carry

        planes_loop(body, 0, part * piece, piece)

    outer = [(pad - halo, halo), (pad + tx, halo)]

    def inner_update(part):
        for n in range(group):
            first_update(n, part, core)
        if (part + 1) * piece % out_piece == 0:
            for j in order:
                out_copy(0, j, (part + 1) * piece // out_piece - 1).start()

    def outer_update(part):
        for n in range(group):
            edge_recv_wait(1 + part, n)
            for win in outer:
                first_update(n, part, win)
            packed = r.packed_one[n, rows(full), :] if part else wide
            r.packed_one[n, rows(full), :] = pack_planes(r.e1, n + 1, full, packed, part * piece, piece)

    for part in range(parts):
        if part > 1:
            arrived(1 + part)
        inner_update(part)
        if part:
            outer_update(part - 1)
    outer_update(parts - 1)
    for n in range(group):
        for side in range(2):
            left = r.strip_in[1, n, side, rows(full), :] + r.sres[n, side, rows(full), :]
            r.sres[n, side, rows(full), :] = left
            put_values(
                r.se1, r.sce1, fine, n, side, full, left * r.srd[n, side, rows(full), :],
                r.packed_one[n, rows(full), :], 1,
            )
    time_send(1)
    time_wait(1)

    narrow = blank(trim[1])

    def again(w, v, cv, sv, scv, b, sb, to_v, to_cv, to_sv, to_scv, count):
        for n in range(count):
            ghost = ghosts(sv, n + 1, trim)

            def body(p, carry):
                value, total = pull(v, cv, w, n, ghost, p, trim, 1)
                left = b[n, p, rows(trim), :] + total
                update = value + left * w.d[n, p, rows(trim), :]
                to_v[n + 1, p + 1, rows(trim), :] = update
                to_cv[n, p + 1, rows(trim), :] = w.c[n, p + 1, rows(trim), :] * update
                return carry

            planes_loop(body, 0)
            packed = pack_planes(to_v, n + 1, trim, narrow)
            for side in range(2):
                value, total = strip_pull(sv, scv, w, n, side, trim, 1)
                left = sb[n, side, rows(trim), :] + total
                update = value + left * w.sg[n, side, rows(trim), :]
                put_values(to_sv, to_scv, w, n, side, trim, update, packed, 1)

    def coarsen(w, to, v, cv, sv, scv, b, sb, to_b, to_sb, to_v, to_cv, to_sv, to_scv, count):
        for n in range(count):
            pair = [ghosts(sv, 2 * n + i + 1, trim) for i in range(2)]

            def body(p, carry):
                rhs = None
                for i in range(2):
                    _, total = pull(v, cv, w, 2 * n + i, pair[i], p, trim, 1)
                    left = b[2 * n + i, p, rows(trim), :] + total
                    rhs = left if rhs is None else rhs + left
                to_b[n, p, rows(trim), :] = rhs
                update = rhs * to.d[n, p, rows(trim), :]
                to_v[n + 1, p + 1, rows(trim), :] = update
                to_cv[n, p + 1, rows(trim), :] = to.c[n, p + 1, rows(trim), :] * update
                return carry

            planes_loop(body, 0)
            packed = pack_planes(to_v, n + 1, trim, narrow)
            for side in range(2):
                rhs = None
                for i in range(2):
                    _, total = strip_pull(sv, scv, w, 2 * n + i, side, trim, 1)
                    left = sb[2 * n + i, side, rows(trim), :] + total
                    rhs = left if rhs is None else rhs + left
                to_sb[n, side, rows(trim), :] = rhs
                update = rhs * to.sg[n, side, rows(trim), :]
                put_values(to_sv, to_scv, to, n, side, trim, update, packed, 1)

    again(fine, r.e1, r.ce1, r.se1, r.sce1, r.res, r.sres, r.e2, r.ce2, r.se2, r.sce2, group)
    time_send(2)
    time_wait(2)
    coarsen(
        fine, mid, r.e2, r.ce2, r.se2, r.sce2, r.res, r.sres, r.mb, r.smb, r.me1, r.cme1, r.sme1, r.scme1, 2
    )
    time_send(3)
    time_wait(3)
    again(mid, r.me1, r.cme1, r.sme1, r.scme1, r.mb, r.smb, r.me2, r.cme2, r.sme2, r.scme2, 2)
    time_send(4)
    time_wait(4)
    coarsen(
        mid, top, r.me2, r.cme2, r.sme2, r.scme2, r.mb, r.smb, r.tb, r.stb, r.te, r.cte, r.ste, r.scte, 1
    )
    time_send(5)
    time_wait(5)
    ghost = ghosts(r.ste, 1, core)

    def body(p, carry):
        value, total = pull(r.te, r.cte, top, 0, ghost, p, core, 1)
        update = value + (r.tb[0, p, real, :] + total) * r.trd[0, p, real, :]
        for n in range(group):
            middle = r.me2[n // 2 + 1, p + 1, real, :] + update
            r.new[n, p, real, :] = r.u[n + 1, p + 1, real, :] + (r.e2[n + 1, p + 1, real, :] + middle)
        return carry

    for part in range(out_parts):
        planes_loop(body, 0, part * out_piece, out_piece)
        for j in order:
            out_copy(1, j, part).start()

    for f in range(2):
        for j in order[:3]:
            strip_copy(f, j).wait_send()
    for a in range(1 + parts):
        for j in order[:3]:
            in_copy(a, j).wait_send()
    for kind in range(parts + 3):
        for n in range(group):
            edge_send_wait(kind, n)
    edge_send_wait(kappa_kind)
    edge_send_wait(strip_kappa)
    if chained:

        @pl.when(has_next)
        def _():
            for number in range(len(time_refs)):
                for copy in time_copies(number):
                    copy.wait_send()

    for a in range(2):
        for part in range(out_parts):
            for j in order:
                if j == 0:
                    out_copy(a, j, part).wait()
                else:
                    out_copy(a, j, part).wait_send()
                    out_copy(a, j, part).wait_recv()


def shards(tm_size, space_size, iterate, source_term, conductivity):
    _, nz, tx, ty = conductivity.shape
    width = ty // group
    tall = tx + 2 * pad
    f32 = jnp.float32
    dma = pltpu.SemaphoreType.DMA
    kinds = parts + 5

    def padded(count):
        return pltpu.VMEM((count, nz + 2, tall, width), f32)

    def plain(*lead):
        return pltpu.VMEM((*lead, nz, tall, width), f32)

    def strip(*lead):
        return pltpu.VMEM((*lead, 2, tall, width), f32)

    scratch = {}
    scratch |= {name: padded(count) for name, count in (
        ("u", 5), ("c", 4), ("cu", 4), ("e1", 5), ("ce1", 4), ("e2", 5), ("ce2", 4), ("mc", 2), ("me1", 3),
        ("cme1", 2), ("me2", 3), ("cme2", 2), ("tc", 1), ("te", 2), ("cte", 1),
    )}
    scratch |= {name: plain(count) for name, count in (
        ("src", 4), ("res", 4), ("wl", 4), ("wr", 4), ("wa", 4), ("rd", 4), ("mwl", 2), ("mwr", 2), ("mwa", 2),
        ("mrd", 2), ("mb", 2), ("twl", 1), ("twr", 1), ("twa", 1), ("trd", 1), ("tb", 1), ("new", 4),
    )}
    scratch["kap"] = plain()
    scratch |= {name: strip(count) for name, count in (
        ("su", 5), ("sc", 4), ("scu", 4), ("se1", 5), ("sce1", 4), ("se2", 5), ("sce2", 4), ("smc", 2),
        ("sme1", 3), ("scme1", 2), ("sme2", 3), ("scme2", 2), ("stc", 1), ("ste", 2), ("scte", 1),
        ("swl", 4), ("swr", 4), ("swd", 4), ("swu", 4), ("swa", 4), ("srd", 4), ("sres", 4),
        ("smwl", 2), ("smwr", 2), ("smwd", 2), ("smwu", 2), ("smwa", 2), ("smrd", 2), ("smb", 2),
        ("stwl", 1), ("stwr", 1), ("stwd", 1), ("stwu", 1), ("stwa", 1), ("strd", 1), ("stb", 1),
    )}
    scratch["kap_strip"] = strip()
    scratch["strip_in"] = strip(2, group)
    scratch["strip_send"] = pltpu.VMEM((2, group, 2, tx, width), f32)
    scratch["own"] = pltpu.VMEM((2, nz, tx, ty), f32)
    scratch["beside"] = pltpu.VMEM((2, nz, tx, width), f32)
    scratch["packed_one"] = pltpu.VMEM((group, tall, width), f32)
    scratch["damp"] = pltpu.VMEM((3, tall, width), f32)
    for name, shape in (
        ("loc_sem", (5,)), ("in_lsem", (1 + parts,)), ("in_ssem", (1 + parts, group - 1)),
        ("in_rsem", (1 + parts, group - 1)), ("out_lsem", (2, out_parts)), ("out_ssem", (2, out_parts, group - 1)),
        ("out_rsem", (2, out_parts, group - 1)), ("strip_ssem", (2, group - 1)), ("strip_rsem", (2, group - 1)),
        ("edge_ssem", (kinds, group, 2)), ("edge_rsem", (kinds, group, 2)), ("time_ssem", (6, 2)),
        ("time_rsem", (6, 2)),
    ):
        scratch[name] = dma(shape)
    names = ("state_in", "source_in", "kappa_in", "new_out", "res_out", *scratch)
    out = jax.ShapeDtypeStruct(iterate.shape, f32)
    hbm = pl.BlockSpec(memory_space=pltpu.HBM)
    return pl.pallas_call(
        functools.partial(kernel, tm_size, space_size, names),
        out_shape=(out, out),
        in_specs=[hbm] * 3,
        out_specs=(hbm, hbm),
        scratch_shapes=list(scratch.values()),
        compiler_params=pltpu.CompilerParams(
            collective_id=0, has_side_effects=True, vmem_limit_bytes=67043328
        ),
    )(iterate, source_term, conductivity)


def solution(mesh):
    tiled = P("tm", "space", None, None, None)
    in_specs = (tiled, tiled, P("space", None, None, None))
    body = functools.partial(shards, mesh.shape["tm"], mesh.shape["space"])
    return jax.shard_map(
        body, mesh=mesh, in_specs=in_specs, out_specs=(tiled, tiled), check_vma=False
    )
```

```python
import functools
import types

import jax
import jax.numpy as jnp
from jax import lax
from jax.experimental import pallas as pl
from jax.experimental.pallas import tpu as pltpu
from jax.sharding import PartitionSpec as P

tau_step = 0.08
damping = 0.7
group = 4
halo = 8
pad = 2 * halo
u_parts = 2
parts = 4
out_parts = 2
mesh_ids = pl.DeviceIdType.MESH
order = (2, 1, 3, 0)
unroll = 8


def kernel(tm_size, space_size, names, *refs):
    r = types.SimpleNamespace(**dict(zip(names, refs)))
    _, nz, tx, _ = r.kappa_in.shape
    width = r.kap.shape[-1]
    span = width // nz
    chained = tm_size > group
    half = 0.5 * tau_step
    piece, u_piece, out_piece = nz // parts, nz // u_parts, nz // out_parts

    full = (pad - halo, tx + 2 * halo)
    trim = (pad - halo // 2, tx + halo)
    core = (pad, tx)

    def rows(win, shift=0):
        return pl.ds(win[0] + shift, win[1])

    real = rows(core)
    planes = pl.ds(1, nz)
    me = lax.axis_index("tm")
    sp = lax.axis_index("space")
    q = me % group
    base = me - q
    has_dn, has_up = sp > 0, sp < space_size - 1
    has_left, has_right = q > 0, q < group - 1
    has_prev, has_next = base > 0, base + group < tm_size
    pair = group // 2
    lower = q < pair
    own_work = q != pair
    far_block = jnp.where(lower, pair, 0)
    near_block = jnp.where(lower, pair - 1, 0)
    has_before = jnp.logical_and(own_work, me > 0)
    has_after = jnp.logical_and(q != pair - 1, me + 1 < tm_size)
    flanks = [(has_dn, {"space": sp - 1}), (has_up, {"space": sp + 1})]
    beside_has = [has_left, has_right]

    def columns(d):
        return pl.ds(pl.multiple_of(d * width, width), width)

    own_copies = [
        pltpu.make_async_copy(hbm.at[0, 0], r.own.at[f], r.loc_sem.at[f])
        for f, hbm in enumerate((r.state_in, r.source_in))
    ]
    kappa_copy = pltpu.make_async_copy(
        r.kappa_in.at[0, :, :, columns(q)], r.kap.at[:, real, :], r.loc_sem.at[2]
    )

    def beside_copy(side):
        block = r.kappa_in.at[0, :, :, columns(q - 1 + 2 * side)]
        return pltpu.make_async_copy(block, r.beside.at[side], r.loc_sem.at[3 + side])

    own_copies[0].start()
    kappa_copy.start()
    for side in range(2):

        @pl.when(beside_has[side])
        def _():
            beside_copy(side).start()

    own_copies[1].start()

    def wide_columns(first, count):
        return pl.ds(pl.multiple_of(first * width, width), count * width)

    def far_copies():
        made = []
        for k in range(pair + 1):
            made.append(
                pltpu.make_async_copy(
                    r.state_in.at[0, 0, :, :, columns(near_block + k)],
                    r.lu.at[1 + k, pl.ds(1, nz), pl.ds(halo, tx), :], r.far_sem.at[0, k],
                )
            )
            made.append(
                pltpu.make_async_copy(
                    r.kappa_in.at[0, :, :, columns(near_block + k)], r.lkap.at[1 + k], r.far_sem.at[1, k]
                )
            )
        return made

    @pl.when(own_work)
    def _():
        for copy in far_copies():
            copy.start()

    def before_copy():
        first = jnp.where((q + 1) % group < pair, pair, 0)
        return pltpu.make_async_remote_copy(
            src_ref=r.state_in.at[0, 0, :, :, wide_columns(first, pair)], dst_ref=r.before,
            send_sem=r.before_sem.at[0], recv_sem=r.before_sem.at[1], device_id={"tm": me + 1},
            device_id_type=mesh_ids,
        )

    def row_copy(number):
        return pltpu.make_async_remote_copy(
            src_ref=r.row_send.at[number], dst_ref=r.row_in.at[1 - number],
            send_sem=r.row_sem.at[0, number], recv_sem=r.row_sem.at[1, 1 - number],
            device_id=flanks[number][1], device_id_type=mesh_ids,
        )

    barrier = pltpu.get_barrier_semaphore()
    for j in range(1, group):
        pl.semaphore_signal(
            barrier, inc=1, device_id={"tm": base + (q + j) % group}, device_id_type=mesh_ids
        )
    greeted = list(flanks)
    if chained:
        greeted += [(has_prev, {"tm": me - group}), (has_next, {"tm": me + group})]
        greeted += [(jnp.logical_and(has_prev, q == 0), {"tm": me - 1})]
        greeted += [(jnp.logical_and(has_next, q == group - 1), {"tm": me + 1})]
    for has, where in greeted:

        @pl.when(has)
        def _():
            pl.semaphore_signal(barrier, inc=1, device_id=where, device_id_type=mesh_ids)

    expected = group - 1
    for has, _ in greeted:
        expected = expected + jnp.where(has, 1, 0)
    pl.semaphore_wait(barrier, expected)

    def in_copy(a, j):
        d = (q + j) % group
        if a < u_parts:
            some = pl.ds(a * u_piece, u_piece)
            hbm = r.state_in.at[0, 0, some, :, columns(d)]
            dst = r.u.at[q + 1, pl.ds(1 + a * u_piece, u_piece), real, :]
        else:
            some = pl.ds((a - u_parts) * piece, piece)
            hbm, dst = r.source_in.at[0, 0, some, :, columns(d)], r.src.at[q, some, real, :]
        if j == 0:
            return pltpu.make_async_copy(hbm, dst, r.in_lsem.at[a])
        return pltpu.make_async_remote_copy(
            src_ref=hbm, dst_ref=dst, send_sem=r.in_ssem.at[a, j - 1],
            recv_sem=r.in_rsem.at[a, j - 1], device_id={"tm": base + d}, device_id_type=mesh_ids,
        )

    def out_copy(a, j, part):
        d = (q + j) % group
        some = pl.ds(part * out_piece, out_piece)
        hbm = (r.res_out, r.new_out)[a].at[0, 0, some, :, columns(q)]
        held = (r.res, r.new)[a].at[d, some, real, :]
        if j == 0:
            return pltpu.make_async_copy(held, hbm, r.out_lsem.at[a, part])
        return pltpu.make_async_remote_copy(
            src_ref=held, dst_ref=hbm, send_sem=r.out_ssem.at[a, part, j - 1],
            recv_sem=r.out_rsem.at[a, part, j - 1], device_id={"tm": base + d},
            device_id_type=mesh_ids,
        )

    def out_each(a, part, receiving, act):
        for j in order[:3]:
            one, two = ((q - j) % group, q) if receiving else (q, (q + j) % group)
            if a == 0:
                wanted = jnp.logical_or(one // pair == two // pair, jnp.logical_and(two == pair, one < pair))

                @pl.when(wanted)
                def _():
                    act(out_copy(a, j, part))
            else:
                act(out_copy(a, j, part))

    def strip_copy(j, side):
        d = (q + j) % group
        return pltpu.make_async_remote_copy(
            src_ref=r.strip_send.at[d, side], dst_ref=r.strip_in.at[q, side, :, real, :],
            send_sem=r.strip_ssem.at[j - 1, side], recv_sem=r.strip_rsem.at[j - 1, side],
            device_id={"tm": base + d}, device_id_type=mesh_ids,
        )

    def strip_each(receiving, act):
        for j in order[:3]:
            d = q if receiving else (q + j) % group
            for side, has in enumerate((d > 0, d < group - 1)):

                @pl.when(has)
                def _():
                    act(strip_copy(j, side))


    strip_kind = u_parts + parts
    kappa_kind, kappa_strip_kind = strip_kind + 1, strip_kind + 2

    def edge_ref(kind, where):
        if kind < u_parts:
            return r.u.at[pl.ds(1, group), pl.ds(1 + kind * u_piece, u_piece), where, :]
        if kind < strip_kind:
            return r.src.at[:, pl.ds((kind - u_parts) * piece, piece), where, :]
        if kind == strip_kind:
            return r.strip_in.at[:, :, :, where, :]
        if kind == kappa_kind:
            return r.kap.at[:, where, :]
        return r.kap_strip.at[:, where, :]

    def edge_copy(kind, number):
        if number == 0:
            source, target = pl.ds(pad, halo), pl.ds(pad + tx, halo)
        else:
            source, target = pl.ds(pad + tx - halo, halo), pl.ds(pad - halo, halo)
        return pltpu.make_async_remote_copy(
            src_ref=edge_ref(kind, source), dst_ref=edge_ref(kind, target),
            send_sem=r.edge_ssem.at[kind, number], recv_sem=r.edge_rsem.at[kind, number],
            device_id=flanks[number][1], device_id_type=mesh_ids,
        )

    def edge_start(kind):
        for number in range(2):

            @pl.when(flanks[number][0])
            def _():
                edge_copy(kind, number).start()

    def edge_send_wait(kind):
        for number in range(2):

            @pl.when(flanks[number][0])
            def _():
                edge_copy(kind, number).wait_send()

    def edge_recv_wait(kind):
        for number in range(2):

            @pl.when(flanks[number][0])
            def _():
                edge_copy(kind, 1 - number).wait_recv()

    time_refs = [(r.u, group), (r.e1, group), (r.e2, group), (r.me1, 2), (r.me2, 2), (r.te, 1)]
    time_strips = [
        (r.su, group), (r.se1, group), (r.se2, group), (r.sme1, 2), (r.sme2, 2), (r.ste, 1),
    ]

    def time_copies(number):
        made = []
        for kind, (ref, last) in enumerate((time_refs[number], time_strips[number])):
            middle = planes if kind == 0 else pl.ds(0, 2)
            made.append(
                pltpu.make_async_remote_copy(
                    src_ref=ref.at[last, middle, rows(full), :],
                    dst_ref=ref.at[0, middle, rows(full), :],
                    send_sem=r.time_ssem.at[number, kind], recv_sem=r.time_rsem.at[number, kind],
                    device_id={"tm": me + group}, device_id_type=mesh_ids,
                )
            )
        return made

    def time_send(number):
        if chained:

            @pl.when(has_next)
            def _():
                for copy in time_copies(number):
                    copy.start()

    def time_wait(number):
        if chained:

            @pl.when(has_prev)
            def _():
                for copy in time_copies(number):
                    copy.wait_recv()

    for a in range(u_parts):
        for j in order:
            in_copy(a, j).start()
    kappa_copy.wait()
    edge_start(kappa_kind)

    f32 = jnp.float32
    tall = r.u.shape[2]

    def blank(count):
        return jnp.zeros((count, width), f32)

    for side in range(2):

        @pl.when(jnp.logical_not(beside_has[side]))
        def _():
            def clear_beside(p, carry):
                r.beside[side, p] = blank(tx)
                return carry

            lax.fori_loop(0, nz, clear_beside, 0)
            for n in range(group):
                for f in range(2):
                    r.strip_in[n, side, f, real, :] = blank(tx)

    lane_tx = lax.broadcasted_iota(jnp.int32, (tx, width), 1)
    lane = lax.broadcasted_iota(jnp.int32, (tx + 2 * halo, width), 1)

    def plane_of(side, lanes):
        return ((lanes + (span // 2, 0)[side]) % width) // span

    inside = [plane_of(side, lane_tx) for side in range(2)]

    def put_strip(packed, side, block, p):
        return jnp.where(inside[side] == p, pltpu.roll(block, span * p + 2, 1), packed)

    nothing = blank(tx)

    def pack_own(f):
        def body(p, packed):
            blocks = [r.own[f, p, :, d * width : (d + 1) * width] for d in range(group)]
            made = []
            for d in range(group):
                left, right = packed[2 * d], packed[2 * d + 1]
                turned_left = blocks[d - 1] if d else None
                turned_right = blocks[d + 1] if d < group - 1 else None
                made.append(left if turned_left is None else put_strip(left, 0, turned_left, p))
                made.append(right if turned_right is None else put_strip(right, 1, turned_right, p))
            return tuple(made)

        packed = lax.fori_loop(0, nz, body, (nothing,) * (2 * group), unroll=2)
        for d in range(group):
            for side in range(2):
                r.strip_send[d, side, f] = packed[2 * d + side]
        for side in range(2):
            r.strip_in[q, side, f, real, :] = r.strip_send[q, side, f]

    for f in range(2):
        own_copies[f].wait()
        pack_own(f)
    strip_each(False, lambda copy: copy.start())
    for part in range(parts):
        for j in order:
            in_copy(u_parts + part, j).start()

    @pl.when(has_after)
    def _():
        before_copy().start()

    @pl.when(own_work)
    def _():
        for copy in far_copies():
            copy.wait()

        def far_rows(p, carry):
            for i in range(pair):
                k = far_block - near_block + i
                for number, row in enumerate((0, tx - 1)):
                    r.row_send[number, 0, i, pl.ds(p, 1), :] = r.lu[1 + k, p + 1, pl.ds(halo + row, 1), :]
                    r.row_send[number, 1, i, pl.ds(p, 1), :] = r.lkap[1 + k, p, pl.ds(row, 1), :]
            return carry

        lax.fori_loop(0, nz, far_rows, 0, unroll=4)
        for number in range(2):

            @pl.when(flanks[number][0])
            def _():
                row_copy(number).start()

            @pl.when(jnp.logical_not(flanks[number][0]))
            def _():
                for f in range(2):
                    for i in range(pair):
                        r.row_in[number, f, i] = blank(nz)

    held = [(ref, 1) for ref, _ in time_refs]
    held += [(ref, 0) for ref in (r.c, r.cu, r.ce1, r.ce2, r.mc, r.cme1, r.cme2, r.tc, r.cte)]
    early = (r.u, r.c, r.cu, r.e1, r.ce1)
    for ref, first in held:
        for n in range(first, ref.shape[0]):
            for plane in (0, nz + 1):
                ref[n, plane] = blank(tall)

    def clear_rows(p, carry):
        for ref, first in held:
            outer = any(ref is one for one in early)
            low, high = (0, tall - halo) if outer else (halo, tall - pad)
            for n in range(first, ref.shape[0]):
                ref[n, p + 1, pl.ds(low, halo), :] = blank(halo)
                ref[n, p + 1, pl.ds(high, halo), :] = blank(halo)
        return carry

    lax.fori_loop(0, nz, clear_rows, 0)
    strips = [(ref, 1) for ref, _ in time_strips]
    strips += [(ref, 0) for ref in (r.sc, r.scu, r.sce1, r.sce2, r.smc, r.scme1, r.scme2, r.stc, r.scte)]
    for ref, first in strips:
        for n in range(first, ref.shape[0]):
            for side in range(2):
                ref[n, side] = blank(tall)
    if chained:

        @pl.when(jnp.logical_not(has_prev))
        def _():
            def clear_first(p, carry):
                for ref, _ in time_refs:
                    ref[0, p + 1] = blank(tall)
                return carry

            lax.fori_loop(0, nz, clear_first, 0)
            for ref, _ in time_strips:
                for side in range(2):
                    ref[0, side] = blank(tall)

    for number, (has, _) in enumerate(flanks):
        edge = pl.ds((pad - halo, pad + tx)[number], halo)

        @pl.when(jnp.logical_not(has))
        def _():
            def clear_edges(p, carry):
                r.kap[p, edge, :] = blank(halo)
                for n in range(group):
                    r.u[n + 1, p + 1, edge, :] = blank(halo)
                    r.src[n, p, edge, :] = blank(halo)
                return carry

            lax.fori_loop(0, nz, clear_edges, 0)
            for side in range(2):
                r.kap_strip[side, edge, :] = blank(halo)
                for f in range(2):
                    for n in range(group):
                        r.strip_in[n, side, f, edge, :] = blank(halo)

    for side in range(2):

        @pl.when(beside_has[side])
        def _():
            beside_copy(side).wait()

    def kappa_body(p, packed):
        return tuple(put_strip(packed[side], side, r.beside[side, p], p) for side in range(2))

    packed = lax.fori_loop(0, nz, kappa_body, (nothing, nothing), unroll=2)
    for side in range(2):
        r.kap_strip[side, real, :] = packed[side]
    edge_start(kappa_strip_kind)

    level = lax.broadcasted_iota(jnp.int32, (tx + 2 * halo, width), 0)
    below = jnp.where(has_dn, damping, 0.0)
    above = jnp.where(has_up, damping, 0.0)
    damp = jnp.where(level < halo, below, jnp.where(level < halo + tx, damping, above))
    r.damp[0, rows(full), :] = damp
    for side in range(2):
        r.damp[1 + side, rows(full), :] = damp * jnp.where(beside_has[side], 1.0, 0.0)

    first_plane = [plane_of(side, lane) == 0 for side in range(2)]
    last_plane = [plane_of(side, lane) == nz - 1 for side in range(2)]
    inject = [lane % span == 2, lane % span == 1]
    plane_lane = lane // span
    first_lane = lane == 0
    last_lane = lane == width - 1

    def cut(mask, win):
        return mask[: win[1]]

    def pack(packed, value, p, win):
        return jnp.where(cut(plane_lane, win) == p, pltpu.roll(value, span * p + 2, 1), packed)

    def pack_planes(ref, n, win, packed, first=0, count=None):
        def body(p, packed):
            return pack(packed, ref[n, p + 1, rows(win), :], p, win)

        return planes_loop(body, packed, first, count)

    def ghosts(ref, n, win):
        left = pltpu.roll(ref[n, 0, rows(win), :], 1, 1)
        right = pltpu.roll(ref[n, 1, rows(win), :], width - 1, 1)
        return jnp.where(cut(inject[0], win), left, right)

    def sideways(value, ghost, p, win):
        edge = pltpu.roll(ghost, width - 2 - span * p, 1)
        left = jnp.where(cut(first_lane, win), edge, pltpu.roll(value, 1, 1))
        right = jnp.where(cut(last_lane, win), edge, pltpu.roll(value, width - 1, 1))
        return left, right

    def across(ref, n, p, win):
        return (
            (ref[n, p + 1, rows(win, -1), :] + ref[n, p + 1, rows(win, 1), :])
            + (ref[n, p, rows(win), :] + ref[n, p + 2, rows(win), :])
        )

    def planes_loop(body, init, first=0, count=None):
        count = nz if count is None else count
        return lax.fori_loop(first, first + count, body, init, unroll=min(unroll, count))

    def earlier(ref, n, middle, win):
        if n == 0 and not chained:
            return None
        return ref[n, middle, rows(win), :]

    def pull(v_ref, cv_ref, w, n, ghost, p, win, first):
        v = v_ref[first + n, p + 1, rows(win), :]
        left, right = sideways(v, ghost, p, win)
        total = w.l[n, p, rows(win), :] * left + w.r[n, p, rows(win), :] * right
        total = total + w.c[n, p + 1, rows(win), :] * across(v_ref, first + n, p, win)
        total = total + across(cv_ref, n, p, win)
        before = earlier(v_ref, n, p + 1, win)
        if before is not None:
            total = total + before
        return v, total - w.a[n, p, rows(win), :] * v

    def strip_pull(v_ref, cv_ref, w, n, side, win, first):
        v = v_ref[first + n, side, rows(win), :]
        total = w.sl[n, side, rows(win), :] * pltpu.roll(v, 1, 1)
        total = total + w.sr[n, side, rows(win), :] * pltpu.roll(v, width - 1, 1)
        total = total + w.sd[n, side, rows(win), :] * pltpu.roll(v, span, 1)
        total = total + w.su[n, side, rows(win), :] * pltpu.roll(v, width - span, 1)
        beside = v_ref[first + n, side, rows(win, -1), :] + v_ref[first + n, side, rows(win, 1), :]
        total = total + w.sc[n, side, rows(win), :] * beside
        total = total + (cv_ref[n, side, rows(win, -1), :] + cv_ref[n, side, rows(win, 1), :])
        before = earlier(v_ref, n, side, win)
        if before is not None:
            total = total + before
        return v, total - w.sa[n, side, rows(win), :] * v

    def put_values(v_ref, cv_ref, w, n, side, win, value, packed, first):
        value = jnp.where(cut(inject[side], win), packed, value)
        v_ref[first + n, side, rows(win), :] = value
        cv_ref[n, side, rows(win), :] = w.sc[n, side, rows(win), :] * value

    fine = types.SimpleNamespace(
        l=r.wl, r=r.wr, a=r.wa, c=r.c, d=r.rd, sl=r.swl, sr=r.swr, sd=r.swd, su=r.swu, sa=r.swa, sc=r.sc, sg=r.srd
    )
    mid = types.SimpleNamespace(
        l=r.mwl, r=r.mwr, a=r.mwa, c=r.mc, d=r.mrd, sl=r.smwl, sr=r.smwr, sd=r.smwd, su=r.smwu, sa=r.smwa,
        sc=r.smc, sg=r.smrd,
    )
    top = types.SimpleNamespace(
        l=r.twl, r=r.twr, a=r.twa, c=r.tc, d=r.trd, sl=r.stwl, sr=r.stwr, sd=r.stwd, su=r.stwu, sa=r.stwa,
        sc=r.stc, sg=r.strd,
    )

    wide = blank(full[1])
    edge_recv_wait(kappa_kind)
    edge_recv_wait(kappa_strip_kind)
    kappa_edge = planes_loop(lambda p, packed: pack(packed, r.kap[p, rows(full), :], p, full), wide)

    def arrived(a):
        in_copy(a, 0).wait()
        for j in order[:3]:
            in_copy(a, j).wait_recv()
        edge_start(a)

    for a in range(u_parts):
        arrived(a)
    strip_each(True, lambda copy: copy.wait_recv())
    edge_start(strip_kind)

    for a in range(u_parts):
        edge_recv_wait(a)
    edge_recv_wait(strip_kind)
    for n in range(group):
        def body(p, carry):
            v = r.u[n + 1, p + 1, rows(full), :]
            cc = (half * r.kap[p, rows(full), :]) * (1.0 + v * v)
            r.c[n, p + 1, rows(full), :] = cc
            r.cu[n, p + 1, rows(full), :] = cc * v
            return carry

        planes_loop(body, 0)
        packed = pack_planes(r.u, n + 1, full, wide)
        for side in range(2):
            v = jnp.where(inject[side], packed, r.strip_in[n, side, 0, rows(full), :])
            kk = jnp.where(inject[side], kappa_edge, r.kap_strip[side, rows(full), :])
            cc = (half * kk) * (1.0 + v * v)
            r.su[n + 1, side, rows(full), :] = v
            r.sc[n, side, rows(full), :] = cc
            r.scu[n, side, rows(full), :] = cc * v
    time_send(0)
    time_wait(0)

    for n in range(group):
        for side in range(2):
            cc = r.sc[n, side, rows(full), :]
            total = r.sc[n, side, rows(full, -1), :] + r.sc[n, side, rows(full, 1), :]
            for ref, shift, off in (
                (r.swl, 1, None), (r.swr, width - 1, None),
                (r.swd, span, first_plane[side]), (r.swu, width - span, last_plane[side]),
            ):
                near = pltpu.roll(cc, shift, 1)
                weight = cc + near
                if off is not None:
                    near, weight = jnp.where(off, 0.0, near), jnp.where(off, 0.0, weight)
                ref[n, side, rows(full), :] = weight
                total = total + near
            diagonal = 1.0 + (6.0 * cc + total)
            r.swa[n, side, rows(full), :] = diagonal
            r.srd[n, side, rows(full), :] = r.damp[1 + side, rows(full), :] / diagonal
        ghost_c, ghost_u = ghosts(r.sc, n, full), ghosts(r.su, n + 1, full)

        def body(p, carry):
            cc = r.c[n, p + 1, rows(full), :]
            left, right = sideways(cc, ghost_c, p, full)
            left, right = cc + left, cc + right
            r.wl[n, p, rows(full), :] = left
            r.wr[n, p, rows(full), :] = right
            diagonal = 1.0 + ((4.0 * cc + left) + (right + across(r.c, n, p, full)))
            r.wa[n, p, rows(full), :] = diagonal
            r.rd[n, p, rows(full), :] = r.damp[0, rows(full), :] / diagonal
            _, total = pull(r.u, r.cu, fine, n, ghost_u, p, full, 1)
            r.res[n, p, rows(full), :] = total
            return carry

        planes_loop(body, 0)
        for side in range(2):
            _, total = strip_pull(r.su, r.scu, fine, n, side, full, 1)
            r.sres[n, side, rows(full), :] = total
        if n == 1:
            arrived(u_parts)
    arrived(u_parts + 1)

    pairs = ((mid, fine, 2), (top, mid, 1))
    for to, of, count in pairs:
        for n in range(count):

            def body(p, carry):
                to.c[n, p + 1, rows(full), :] = of.c[2 * n, p + 1, rows(full), :] + of.c[2 * n + 1, p + 1, rows(full), :]
                for one, two in ((to.l, of.l), (to.r, of.r)):
                    one[n, p, rows(full), :] = two[2 * n, p, rows(full), :] + two[2 * n + 1, p, rows(full), :]
                diagonal = (of.a[2 * n, p, rows(full), :] - 1.0) + of.a[2 * n + 1, p, rows(full), :]
                to.a[n, p, rows(full), :] = diagonal
                to.d[n, p, rows(full), :] = r.damp[0, rows(full), :] / diagonal
                return carry

            planes_loop(body, 0)
            for side in range(2):
                for one, two in (
                    (to.sc, of.sc), (to.sl, of.sl), (to.sr, of.sr), (to.sd, of.sd), (to.su, of.su),
                ):
                    one[n, side, rows(full), :] = two[2 * n, side, rows(full), :] + two[2 * n + 1, side, rows(full), :]
                diagonal = (of.sa[2 * n, side, rows(full), :] - 1.0) + of.sa[2 * n + 1, side, rows(full), :]
                to.sa[n, side, rows(full), :] = diagonal
                to.sg[n, side, rows(full), :] = r.damp[1 + side, rows(full), :] / diagonal

    def first_update(n, part, win):
        def body(p, carry):
            left = r.src[n, p, rows(win), :] + r.res[n, p, rows(win), :]
            r.res[n, p, rows(win), :] = left
            update = left * r.rd[n, p, rows(win), :]
            r.e1[n + 1, p + 1, rows(win), :] = update
            r.ce1[n, p + 1, rows(win), :] = r.c[n, p + 1, rows(win), :] * update
            return carry

        planes_loop(body, 0, part * piece, piece)

    outer = [(pad - halo, halo), (pad + tx, halo)]

    def inner_update(part):
        for n in range(group):
            first_update(n, part, core)
        if (part + 1) * piece % out_piece == 0:
            ready = (part + 1) * piece // out_piece - 1
            out_each(0, ready, False, lambda copy: copy.start())
            out_copy(0, 0, ready).start()

    def outer_update(part):
        edge_recv_wait(u_parts + part)
        for n in range(group):
            for win in outer:
                first_update(n, part, win)
            packed = r.packed_one[n, rows(full), :] if part else wide
            r.packed_one[n, rows(full), :] = pack_planes(r.e1, n + 1, full, packed, part * piece, piece)

    for part in range(parts):
        if part > 1:
            arrived(u_parts + part)
        inner_update(part)
        if part:
            outer_update(part - 1)
    outer_update(parts - 1)
    for n in range(group):
        for side in range(2):
            left = r.strip_in[n, side, 1, rows(full), :] + r.sres[n, side, rows(full), :]
            r.sres[n, side, rows(full), :] = left
            put_values(
                r.se1, r.sce1, fine, n, side, full, left * r.srd[n, side, rows(full), :],
                r.packed_one[n, rows(full), :], 1,
            )
    time_send(1)
    time_wait(1)

    narrow = blank(trim[1])

    def again(w, v, cv, sv, scv, b, sb, to_v, to_cv, to_sv, to_scv, count):
        for n in range(count):
            ghost = ghosts(sv, n + 1, trim)

            def body(p, carry):
                value, total = pull(v, cv, w, n, ghost, p, trim, 1)
                left = b[n, p, rows(trim), :] + total
                update = value + left * w.d[n, p, rows(trim), :]
                to_v[n + 1, p + 1, rows(trim), :] = update
                to_cv[n, p + 1, rows(trim), :] = w.c[n, p + 1, rows(trim), :] * update
                return carry

            planes_loop(body, 0)
            packed = pack_planes(to_v, n + 1, trim, narrow)
            for side in range(2):
                value, total = strip_pull(sv, scv, w, n, side, trim, 1)
                left = sb[n, side, rows(trim), :] + total
                update = value + left * w.sg[n, side, rows(trim), :]
                put_values(to_sv, to_scv, w, n, side, trim, update, packed, 1)

    def coarsen(w, to, v, cv, sv, scv, b, sb, to_b, to_sb, to_v, to_cv, to_sv, to_scv, count):
        for n in range(count):
            pair = [ghosts(sv, 2 * n + i + 1, trim) for i in range(2)]

            def body(p, carry):
                rhs = None
                for i in range(2):
                    _, total = pull(v, cv, w, 2 * n + i, pair[i], p, trim, 1)
                    left = b[2 * n + i, p, rows(trim), :] + total
                    rhs = left if rhs is None else rhs + left
                to_b[n, p, rows(trim), :] = rhs
                update = rhs * to.d[n, p, rows(trim), :]
                to_v[n + 1, p + 1, rows(trim), :] = update
                to_cv[n, p + 1, rows(trim), :] = to.c[n, p + 1, rows(trim), :] * update
                return carry

            planes_loop(body, 0)
            packed = pack_planes(to_v, n + 1, trim, narrow)
            for side in range(2):
                rhs = None
                for i in range(2):
                    _, total = strip_pull(sv, scv, w, 2 * n + i, side, trim, 1)
                    left = sb[2 * n + i, side, rows(trim), :] + total
                    rhs = left if rhs is None else rhs + left
                to_sb[n, side, rows(trim), :] = rhs
                update = rhs * to.sg[n, side, rows(trim), :]
                put_values(to_sv, to_scv, to, n, side, trim, update, packed, 1)

    again(fine, r.e1, r.ce1, r.se1, r.sce1, r.res, r.sres, r.e2, r.ce2, r.se2, r.sce2, group)
    time_send(2)
    time_wait(2)
    coarsen(
        fine, mid, r.e2, r.ce2, r.se2, r.sce2, r.res, r.sres, r.mb, r.smb, r.me1, r.cme1, r.sme1, r.scme1, 2
    )
    time_send(3)
    time_wait(3)
    again(mid, r.me1, r.cme1, r.sme1, r.scme1, r.mb, r.smb, r.me2, r.cme2, r.sme2, r.scme2, 2)
    time_send(4)
    time_wait(4)
    coarsen(
        mid, top, r.me2, r.cme2, r.sme2, r.scme2, r.mb, r.smb, r.tb, r.stb, r.te, r.cte, r.ste, r.scte, 1
    )
    time_send(5)
    time_wait(5)
    ghost = ghosts(r.ste, 1, core)

    def body(p, carry):
        value, total = pull(r.te, r.cte, top, 0, ghost, p, core, 1)
        update = value + (r.tb[0, p, real, :] + total) * r.trd[0, p, real, :]
        for n in range(group):
            middle = r.me2[n // 2 + 1, p + 1, real, :] + update
            r.new[n, p, real, :] = r.u[n + 1, p + 1, real, :] + (r.e2[n + 1, p + 1, real, :] + middle)
        return carry

    for part in range(out_parts):
        planes_loop(body, 0, part * out_piece, out_piece)
        for j in order:
            out_copy(1, j, part).start()

    @pl.when(jnp.logical_not(has_before))
    def _():
        def clear_before(p, carry):
            for i in range(pair):
                r.before[p, :, i * width : (i + 1) * width] = nothing
            return carry

        lax.fori_loop(0, nz, clear_before, 0)

    @pl.when(has_before)
    def _():
        pltpu.make_async_remote_copy(
            src_ref=r.before, dst_ref=r.before, send_sem=r.before_sem.at[0], recv_sem=r.before_sem.at[1],
            device_id={"tm": me}, device_id_type=mesh_ids,
        ).wait_recv()

    far_real = pl.ds(halo, tx)
    bare = (halo, tx)

    def far_out(i):
        return pltpu.make_async_copy(
            r.far_res.at[i], r.res_out.at[0, 0, :, :, columns(far_block + i)], r.far_sem.at[2, i]
        )

    @pl.when(own_work)
    def _():
        for number in range(2):

            @pl.when(flanks[number][0])
            def _():
                row_copy(1 - number).wait_recv()

            for i in range(pair):
                value = r.row_in[number, 0, i]
                r.row_c[number, i] = (half * r.row_in[number, 1, i]) * (1.0 + value * value)
        for ref in (r.lu, r.lc):
            for k in range(pair + 3):
                for plane in (0, nz + 1):
                    ref[k, plane] = blank(tx + pad)

            def clear_outer(p, carry):
                for k in (0, pair + 2):
                    ref[k, p + 1, far_real, :] = nothing
                return carry

            lax.fori_loop(0, nz, clear_outer, 0)

        def far_coefficient(p, carry):
            for k in range(pair + 1):
                value = r.lu[1 + k, p + 1, far_real, :]
                r.lc[1 + k, p + 1, far_real, :] = (half * r.lkap[1 + k, p]) * (1.0 + value * value)
            for i in range(pair):
                k = far_block - near_block + i
                for number, row in enumerate((halo - 1, halo + tx)):
                    r.lu[1 + k, p + 1, pl.ds(row, 1), :] = r.row_in[number, 0, i, pl.ds(p, 1), :]
                    r.lc[1 + k, p + 1, pl.ds(row, 1), :] = r.row_c[number, i, pl.ds(p, 1), :]
            return carry

        lax.fori_loop(0, nz, far_coefficient, 0, unroll=2)
        first_tx, last_tx = lane_tx == 0, lane_tx == width - 1
        for i in range(pair):
            k = 1 + far_block - near_block + i
            own_columns = columns(far_block + i)

            def body(p, carry):
                def near_of(ref):
                    here = ref[k, p + 1, far_real, :]
                    before, after = ref[k - 1, p + 1, far_real, :], ref[k + 1, p + 1, far_real, :]
                    return here, (
                        jnp.where(first_tx, pltpu.roll(before, 1, 1), pltpu.roll(here, 1, 1)),
                        jnp.where(last_tx, pltpu.roll(after, width - 1, 1), pltpu.roll(here, width - 1, 1)),
                        ref[k, p + 1, pl.ds(halo - 1, tx), :], ref[k, p + 1, pl.ds(halo + 1, tx), :],
                        ref[k, p, far_real, :], ref[k, p + 2, far_real, :],
                    )

                value, value_near = near_of(r.lu)
                cc, c_near = near_of(r.lc)
                left = r.own[1, p, :, own_columns] - value + r.before[p, :, i * width : (i + 1) * width]
                for one, two in zip(value_near, c_near):
                    left = left - (cc + two) * (value - one)
                r.far_res[i, p] = left
                return carry

            lax.fori_loop(0, nz, body, 0, unroll=4)
            far_out(i).start()
        for i in range(pair):
            far_out(i).wait()
        for number in range(2):

            @pl.when(flanks[number][0])
            def _():
                row_copy(number).wait_send()

    @pl.when(has_after)
    def _():
        before_copy().wait_send()

    strip_each(False, lambda copy: copy.wait_send())
    for a in range(u_parts + parts):
        for j in order[:3]:
            in_copy(a, j).wait_send()
    for kind in range(u_parts + parts + 3):
        edge_send_wait(kind)
    if chained:

        @pl.when(has_next)
        def _():
            for number in range(len(time_refs)):
                for copy in time_copies(number):
                    copy.wait_send()

    for a in range(2):
        for part in range(out_parts):
            out_copy(a, 0, part).wait()
            out_each(a, part, False, lambda copy: copy.wait_send())
            out_each(a, part, True, lambda copy: copy.wait_recv())


def shards(tm_size, space_size, iterate, source_term, conductivity):
    _, nz, tx, ty = conductivity.shape
    width = ty // group
    tall = tx + 2 * pad
    f32 = jnp.float32
    dma = pltpu.SemaphoreType.DMA
    kinds = u_parts + parts + 3

    def padded(count):
        return pltpu.VMEM((count, nz + 2, tall, width), f32)

    def plain(*lead):
        return pltpu.VMEM((*lead, nz, tall, width), f32)

    def strip(*lead):
        return pltpu.VMEM((*lead, 2, tall, width), f32)

    scratch = {}
    scratch |= {name: padded(count) for name, count in (
        ("u", 5), ("c", 4), ("cu", 4), ("e1", 5), ("ce1", 4), ("e2", 5), ("ce2", 4), ("mc", 2), ("me1", 3),
        ("cme1", 2), ("me2", 3), ("cme2", 2), ("tc", 1), ("te", 2), ("cte", 1),
    )}
    scratch |= {name: plain(count) for name, count in (
        ("src", 4), ("res", 4), ("wl", 4), ("wr", 4), ("wa", 4), ("rd", 4), ("mwl", 2), ("mwr", 2), ("mwa", 2),
        ("mrd", 2), ("mb", 2), ("twl", 1), ("twr", 1), ("twa", 1), ("trd", 1), ("tb", 1), ("new", 4),
    )}
    scratch["kap"] = plain()
    scratch |= {name: strip(count) for name, count in (
        ("su", 5), ("sc", 4), ("scu", 4), ("se1", 5), ("sce1", 4), ("se2", 5), ("sce2", 4), ("smc", 2),
        ("sme1", 3), ("scme1", 2), ("sme2", 3), ("scme2", 2), ("stc", 1), ("ste", 2), ("scte", 1),
        ("swl", 4), ("swr", 4), ("swd", 4), ("swu", 4), ("swa", 4), ("srd", 4), ("sres", 4),
        ("smwl", 2), ("smwr", 2), ("smwd", 2), ("smwu", 2), ("smwa", 2), ("smrd", 2), ("smb", 2),
        ("stwl", 1), ("stwr", 1), ("stwd", 1), ("stwu", 1), ("stwa", 1), ("strd", 1), ("stb", 1),
    )}
    scratch["kap_strip"] = strip()
    scratch["strip_in"] = strip(group, 2)
    scratch["strip_send"] = pltpu.VMEM((group, 2, 2, tx, width), f32)
    scratch["own"] = pltpu.VMEM((2, nz, tx, ty), f32)
    scratch["beside"] = pltpu.VMEM((2, nz, tx, width), f32)
    pair = group // 2
    scratch["lu"] = pltpu.VMEM((pair + 3, nz + 2, tx + pad, width), f32)
    scratch["lc"] = pltpu.VMEM((pair + 3, nz + 2, tx + pad, width), f32)
    scratch["lkap"] = pltpu.VMEM((pair + 2, nz, tx, width), f32)
    scratch["before"] = pltpu.VMEM((nz, tx, pair * width), f32)
    scratch["far_res"] = pltpu.VMEM((pair, nz, tx, width), f32)
    scratch["row_send"] = pltpu.VMEM((2, 2, pair, nz, width), f32)
    scratch["row_in"] = pltpu.VMEM((2, 2, pair, nz, width), f32)
    scratch["row_c"] = pltpu.VMEM((2, pair, nz, width), f32)
    scratch["packed_one"] = pltpu.VMEM((group, tall, width), f32)
    scratch["damp"] = pltpu.VMEM((3, tall, width), f32)
    for name, shape in (
        ("loc_sem", (5,)), ("in_lsem", (u_parts + parts,)), ("in_ssem", (u_parts + parts, group - 1)),
        ("in_rsem", (u_parts + parts, group - 1)), ("out_lsem", (2, out_parts)), ("out_ssem", (2, out_parts, group - 1)),
        ("out_rsem", (2, out_parts, group - 1)), ("strip_ssem", (group - 1, 2)), ("strip_rsem", (group - 1, 2)),
        ("edge_ssem", (kinds, 2)), ("edge_rsem", (kinds, 2)), ("time_ssem", (6, 2)), ("far_sem", (3, pair + 1)),
        ("before_sem", (2,)), ("row_sem", (2, 2)),
        ("time_rsem", (6, 2)),
    ):
        scratch[name] = dma(shape)
    names = ("state_in", "source_in", "kappa_in", "new_out", "res_out", *scratch)
    out = jax.ShapeDtypeStruct(iterate.shape, f32)
    hbm = pl.BlockSpec(memory_space=pltpu.HBM)
    return pl.pallas_call(
        functools.partial(kernel, tm_size, space_size, names),
        out_shape=(out, out),
        in_specs=[hbm] * 3,
        out_specs=(hbm, hbm),
        scratch_shapes=list(scratch.values()),
        compiler_params=pltpu.CompilerParams(
            collective_id=0, has_side_effects=True, vmem_limit_bytes=67043328
        ),
    )(iterate, source_term, conductivity)


def solution(mesh):
    tiled = P("tm", "space", None, None, None)
    in_specs = (tiled, tiled, P("space", None, None, None))
    body = functools.partial(shards, mesh.shape["tm"], mesh.shape["space"])
    return jax.shard_map(
        body, mesh=mesh, in_specs=in_specs, out_specs=(tiled, tiled), check_vma=False
    )
```

```python
import functools
import types

import jax
import jax.numpy as jnp
from jax import lax
from jax.experimental import pallas as pl
from jax.experimental.pallas import tpu as pltpu
from jax.sharding import PartitionSpec as P

tau_step = 0.08
damping = 0.7
group = 4
halo = 8
pad = 2 * halo
u_parts = 2
parts = 4
passes = (2, 3, 4)
stages = 5
mesh_ids = pl.DeviceIdType.MESH
order = (2, 1, 3, 0)
unroll = 8


def kernel(tm_size, space_size, names, *refs):
    r = types.SimpleNamespace(**dict(zip(names, refs)))
    _, nz, tx, _ = r.kappa_in.shape
    width = r.kap.shape[-1]
    span = width // nz
    chained = tm_size > group
    half = 0.5 * tau_step
    piece, u_piece = nz // parts, nz // u_parts

    def reach(number, stage):
        bounds = [0] + [known * piece - stage if known < parts else nz for known in passes]
        return max(bounds[number], 0), bounds[number + 1]

    pieces = [[(0, nz // 2), (nz // 2, nz // 2)], []]
    for number in range(len(passes)):
        first, last = reach(number, stages)
        pieces[1].append((first, last - first))

    full = (pad - halo, tx + 2 * halo)
    trim = (pad - halo // 2, tx + halo)
    core = (pad, tx)

    def rows(win, shift=0):
        return pl.ds(win[0] + shift, win[1])

    real = rows(core)
    planes = pl.ds(1, nz)
    me = lax.axis_index("tm")
    sp = lax.axis_index("space")
    q = me % group
    base = me - q
    has_dn, has_up = sp > 0, sp < space_size - 1
    has_left, has_right = q > 0, q < group - 1
    has_prev, has_next = base > 0, base + group < tm_size
    pair = group // 2
    lower = q < pair
    own_work = q != pair
    far_block = jnp.where(lower, pair, 0)
    near_block = jnp.where(lower, pair - 1, 0)
    has_before = jnp.logical_and(own_work, me > 0)
    has_after = jnp.logical_and(q != pair - 1, me + 1 < tm_size)
    flanks = [(has_dn, {"space": sp - 1}), (has_up, {"space": sp + 1})]
    beside_has = [has_left, has_right]

    def columns(d):
        return pl.ds(pl.multiple_of(d * width, width), width)

    own_copies = [
        pltpu.make_async_copy(hbm.at[0, 0], r.own.at[f], r.loc_sem.at[f])
        for f, hbm in enumerate((r.state_in, r.source_in))
    ]
    kappa_copy = pltpu.make_async_copy(
        r.kappa_in.at[0, :, :, columns(q)], r.kap.at[:, real, :], r.loc_sem.at[2]
    )

    def beside_copy(side):
        block = r.kappa_in.at[0, :, :, columns(q - 1 + 2 * side)]
        return pltpu.make_async_copy(block, r.beside.at[side], r.loc_sem.at[3 + side])

    own_copies[0].start()
    kappa_copy.start()
    for side in range(2):

        @pl.when(beside_has[side])
        def _():
            beside_copy(side).start()

    own_copies[1].start()

    def wide_columns(first, count):
        return pl.ds(pl.multiple_of(first * width, width), count * width)

    def far_copies():
        made = []
        for k in range(pair + 1):
            made.append(
                pltpu.make_async_copy(
                    r.state_in.at[0, 0, :, :, columns(near_block + k)],
                    r.lu.at[1 + k, pl.ds(1, nz), pl.ds(halo, tx), :], r.far_sem.at[0, k],
                )
            )
            made.append(
                pltpu.make_async_copy(
                    r.kappa_in.at[0, :, :, columns(near_block + k)], r.lkap.at[1 + k], r.far_sem.at[1, k]
                )
            )
        return made

    @pl.when(own_work)
    def _():
        for copy in far_copies():
            copy.start()

    def before_copy():
        first = jnp.where((q + 1) % group < pair, pair, 0)
        return pltpu.make_async_remote_copy(
            src_ref=r.state_in.at[0, 0, :, :, wide_columns(first, pair)], dst_ref=r.before,
            send_sem=r.before_sem.at[0], recv_sem=r.before_sem.at[1], device_id={"tm": me + 1},
            device_id_type=mesh_ids,
        )

    def row_copy(number):
        return pltpu.make_async_remote_copy(
            src_ref=r.row_send.at[number], dst_ref=r.row_in.at[1 - number],
            send_sem=r.row_sem.at[0, number], recv_sem=r.row_sem.at[1, 1 - number],
            device_id=flanks[number][1], device_id_type=mesh_ids,
        )

    barrier = pltpu.get_barrier_semaphore()
    for j in range(1, group):
        pl.semaphore_signal(
            barrier, inc=1, device_id={"tm": base + (q + j) % group}, device_id_type=mesh_ids
        )
    greeted = list(flanks)
    if chained:
        greeted += [(has_prev, {"tm": me - group}), (has_next, {"tm": me + group})]
        greeted += [(jnp.logical_and(has_prev, q == 0), {"tm": me - 1})]
        greeted += [(jnp.logical_and(has_next, q == group - 1), {"tm": me + 1})]
    for has, where in greeted:

        @pl.when(has)
        def _():
            pl.semaphore_signal(barrier, inc=1, device_id=where, device_id_type=mesh_ids)

    expected = group - 1
    for has, _ in greeted:
        expected = expected + jnp.where(has, 1, 0)
    pl.semaphore_wait(barrier, expected)

    def in_copy(a, j):
        d = (q + j) % group
        if a < u_parts:
            some = pl.ds(a * u_piece, u_piece)
            hbm = r.state_in.at[0, 0, some, :, columns(d)]
            dst = r.u.at[q + 1, pl.ds(1 + a * u_piece, u_piece), real, :]
        else:
            some = pl.ds((a - u_parts) * piece, piece)
            hbm, dst = r.source_in.at[0, 0, some, :, columns(d)], r.src.at[q, some, real, :]
        if j == 0:
            return pltpu.make_async_copy(hbm, dst, r.in_lsem.at[a])
        return pltpu.make_async_remote_copy(
            src_ref=hbm, dst_ref=dst, send_sem=r.in_ssem.at[a, j - 1],
            recv_sem=r.in_rsem.at[a, j - 1], device_id={"tm": base + d}, device_id_type=mesh_ids,
        )

    def out_copy(a, j, part):
        d = (q + j) % group
        some = pl.ds(*pieces[a][part])
        hbm = (r.res_out, r.new_out)[a].at[0, 0, some, :, columns(q)]
        held = (r.res, r.new)[a].at[d, some, real, :]
        if j == 0:
            return pltpu.make_async_copy(held, hbm, r.out_lsem.at[a, part])
        return pltpu.make_async_remote_copy(
            src_ref=held, dst_ref=hbm, send_sem=r.out_ssem.at[a, part, j - 1],
            recv_sem=r.out_rsem.at[a, part, j - 1], device_id={"tm": base + d},
            device_id_type=mesh_ids,
        )

    def out_each(a, part, receiving, act):
        for j in order[:3]:
            one, two = ((q - j) % group, q) if receiving else (q, (q + j) % group)
            if a == 0:
                wanted = jnp.logical_or(one // pair == two // pair, jnp.logical_and(two == pair, one < pair))

                @pl.when(wanted)
                def _():
                    act(out_copy(a, j, part))
            else:
                act(out_copy(a, j, part))

    def strip_copy(j, side):
        d = (q + j) % group
        return pltpu.make_async_remote_copy(
            src_ref=r.strip_send.at[d, side], dst_ref=r.strip_in.at[q, side, :, real, :],
            send_sem=r.strip_ssem.at[j - 1, side], recv_sem=r.strip_rsem.at[j - 1, side],
            device_id={"tm": base + d}, device_id_type=mesh_ids,
        )

    def strip_each(receiving, act):
        for j in order[:3]:
            d = q if receiving else (q + j) % group
            for side, has in enumerate((d > 0, d < group - 1)):

                @pl.when(has)
                def _():
                    act(strip_copy(j, side))


    strip_kind = u_parts + parts
    kappa_kind, kappa_strip_kind = strip_kind + 1, strip_kind + 2

    def edge_ref(kind, where):
        if kind < u_parts:
            return r.u.at[pl.ds(1, group), pl.ds(1 + kind * u_piece, u_piece), where, :]
        if kind < strip_kind:
            return r.src.at[:, pl.ds((kind - u_parts) * piece, piece), where, :]
        if kind == strip_kind:
            return r.strip_in.at[:, :, :, where, :]
        if kind == kappa_kind:
            return r.kap.at[:, where, :]
        return r.kap_strip.at[:, where, :]

    def edge_copy(kind, number):
        if number == 0:
            source, target = pl.ds(pad, halo), pl.ds(pad + tx, halo)
        else:
            source, target = pl.ds(pad + tx - halo, halo), pl.ds(pad - halo, halo)
        return pltpu.make_async_remote_copy(
            src_ref=edge_ref(kind, source), dst_ref=edge_ref(kind, target),
            send_sem=r.edge_ssem.at[kind, number], recv_sem=r.edge_rsem.at[kind, number],
            device_id=flanks[number][1], device_id_type=mesh_ids,
        )

    def edge_start(kind):
        for number in range(2):

            @pl.when(flanks[number][0])
            def _():
                edge_copy(kind, number).start()

    def edge_send_wait(kind):
        for number in range(2):

            @pl.when(flanks[number][0])
            def _():
                edge_copy(kind, number).wait_send()

    def edge_recv_wait(kind):
        for number in range(2):

            @pl.when(flanks[number][0])
            def _():
                edge_copy(kind, 1 - number).wait_recv()

    time_refs = [(r.u, group), (r.e1, group), (r.e2, group), (r.me1, 2), (r.me2, 2), (r.te, 1)]
    time_strips = [
        (r.su, group), (r.se1, group), (r.se2, group), (r.sme1, 2), (r.sme2, 2), (r.ste, 1),
    ]

    def time_copies(number):
        made = []
        for kind, (ref, last) in enumerate((time_refs[number], time_strips[number])):
            middle = planes if kind == 0 else pl.ds(0, 2)
            made.append(
                pltpu.make_async_remote_copy(
                    src_ref=ref.at[last, middle, rows(full), :],
                    dst_ref=ref.at[0, middle, rows(full), :],
                    send_sem=r.time_ssem.at[number, kind], recv_sem=r.time_rsem.at[number, kind],
                    device_id={"tm": me + group}, device_id_type=mesh_ids,
                )
            )
        return made

    def time_send(number):
        if chained:

            @pl.when(has_next)
            def _():
                for copy in time_copies(number):
                    copy.start()

    def time_wait(number):
        if chained:

            @pl.when(has_prev)
            def _():
                for copy in time_copies(number):
                    copy.wait_recv()

    for a in range(u_parts):
        for j in order:
            in_copy(a, j).start()
    kappa_copy.wait()
    edge_start(kappa_kind)

    f32 = jnp.float32
    tall = r.u.shape[2]

    def blank(count):
        return jnp.zeros((count, width), f32)

    for side in range(2):

        @pl.when(jnp.logical_not(beside_has[side]))
        def _():
            def clear_beside(p, carry):
                r.beside[side, p] = blank(tx)
                return carry

            lax.fori_loop(0, nz, clear_beside, 0)
            for n in range(group):
                for f in range(2):
                    r.strip_in[n, side, f, real, :] = blank(tx)

    lane_tx = lax.broadcasted_iota(jnp.int32, (tx, width), 1)
    lane = lax.broadcasted_iota(jnp.int32, (tx + 2 * halo, width), 1)

    def plane_of(side, lanes):
        return ((lanes + (span // 2, 0)[side]) % width) // span

    inside = [plane_of(side, lane_tx) for side in range(2)]

    def put_strip(packed, side, block, p):
        return jnp.where(inside[side] == p, pltpu.roll(block, span * p + 2, 1), packed)

    nothing = blank(tx)

    def pack_own(f):
        def body(p, packed):
            blocks = [r.own[f, p, :, d * width : (d + 1) * width] for d in range(group)]
            made = []
            for d in range(group):
                left, right = packed[2 * d], packed[2 * d + 1]
                turned_left = blocks[d - 1] if d else None
                turned_right = blocks[d + 1] if d < group - 1 else None
                made.append(left if turned_left is None else put_strip(left, 0, turned_left, p))
                made.append(right if turned_right is None else put_strip(right, 1, turned_right, p))
            return tuple(made)

        packed = lax.fori_loop(0, nz, body, (nothing,) * (2 * group), unroll=2)
        for d in range(group):
            for side in range(2):
                r.strip_send[d, side, f] = packed[2 * d + side]
        for side in range(2):
            r.strip_in[q, side, f, real, :] = r.strip_send[q, side, f]

    for f in range(2):
        own_copies[f].wait()
        pack_own(f)
    strip_each(False, lambda copy: copy.start())
    for part in range(parts):
        for j in order:
            in_copy(u_parts + part, j).start()

    @pl.when(has_after)
    def _():
        before_copy().start()

    @pl.when(own_work)
    def _():
        for copy in far_copies():
            copy.wait()

        def far_rows(p, carry):
            for i in range(pair):
                k = far_block - near_block + i
                for number, row in enumerate((0, tx - 1)):
                    r.row_send[number, 0, i, pl.ds(p, 1), :] = r.lu[1 + k, p + 1, pl.ds(halo + row, 1), :]
                    r.row_send[number, 1, i, pl.ds(p, 1), :] = r.lkap[1 + k, p, pl.ds(row, 1), :]
            return carry

        lax.fori_loop(0, nz, far_rows, 0, unroll=4)
        for number in range(2):

            @pl.when(flanks[number][0])
            def _():
                row_copy(number).start()

            @pl.when(jnp.logical_not(flanks[number][0]))
            def _():
                for f in range(2):
                    for i in range(pair):
                        r.row_in[number, f, i] = blank(nz)

    held = [(ref, 1) for ref, _ in time_refs]
    held += [(ref, 0) for ref in (r.c, r.cu, r.ce1, r.ce2, r.mc, r.cme1, r.cme2, r.tc, r.cte)]
    early = (r.u, r.c, r.cu, r.e1, r.ce1)
    for ref, first in held:
        for n in range(first, ref.shape[0]):
            for plane in (0, nz + 1):
                ref[n, plane] = blank(tall)

    def clear_rows(p, carry):
        for ref, first in held:
            outer = any(ref is one for one in early)
            low, high = (0, tall - halo) if outer else (halo, tall - pad)
            for n in range(first, ref.shape[0]):
                ref[n, p + 1, pl.ds(low, halo), :] = blank(halo)
                ref[n, p + 1, pl.ds(high, halo), :] = blank(halo)
        return carry

    lax.fori_loop(0, nz, clear_rows, 0)
    strips = [(ref, 1) for ref, _ in time_strips]
    strips += [(ref, 0) for ref in (r.sc, r.scu, r.sce1, r.sce2, r.smc, r.scme1, r.scme2, r.stc, r.scte)]
    for ref, first in strips:
        for n in range(first, ref.shape[0]):
            for side in range(2):
                ref[n, side] = blank(tall)
    if chained:

        @pl.when(jnp.logical_not(has_prev))
        def _():
            def clear_first(p, carry):
                for ref, _ in time_refs:
                    ref[0, p + 1] = blank(tall)
                return carry

            lax.fori_loop(0, nz, clear_first, 0)
            for ref, _ in time_strips:
                for side in range(2):
                    ref[0, side] = blank(tall)

    for number, (has, _) in enumerate(flanks):
        edge = pl.ds((pad - halo, pad + tx)[number], halo)

        @pl.when(jnp.logical_not(has))
        def _():
            def clear_edges(p, carry):
                r.kap[p, edge, :] = blank(halo)
                for n in range(group):
                    r.u[n + 1, p + 1, edge, :] = blank(halo)
                    r.src[n, p, edge, :] = blank(halo)
                return carry

            lax.fori_loop(0, nz, clear_edges, 0)
            for side in range(2):
                r.kap_strip[side, edge, :] = blank(halo)
                for f in range(2):
                    for n in range(group):
                        r.strip_in[n, side, f, edge, :] = blank(halo)

    for side in range(2):

        @pl.when(beside_has[side])
        def _():
            beside_copy(side).wait()

    def kappa_body(p, packed):
        return tuple(put_strip(packed[side], side, r.beside[side, p], p) for side in range(2))

    packed = lax.fori_loop(0, nz, kappa_body, (nothing, nothing), unroll=2)
    for side in range(2):
        r.kap_strip[side, real, :] = packed[side]
    edge_start(kappa_strip_kind)

    level = lax.broadcasted_iota(jnp.int32, (tx + 2 * halo, width), 0)
    below = jnp.where(has_dn, damping, 0.0)
    above = jnp.where(has_up, damping, 0.0)
    damp = jnp.where(level < halo, below, jnp.where(level < halo + tx, damping, above))
    r.damp[0, rows(full), :] = damp
    for side in range(2):
        r.damp[1 + side, rows(full), :] = damp * jnp.where(beside_has[side], 1.0, 0.0)

    first_plane = [plane_of(side, lane) == 0 for side in range(2)]
    last_plane = [plane_of(side, lane) == nz - 1 for side in range(2)]
    inject = [lane % span == 2, lane % span == 1]
    plane_lane = lane // span
    first_lane = lane == 0
    last_lane = lane == width - 1

    def cut(mask, win):
        return mask[: win[1]]

    def pack(packed, value, p, win):
        return jnp.where(cut(plane_lane, win) == p, pltpu.roll(value, span * p + 2, 1), packed)

    def pack_planes(ref, n, win, packed, first=0, count=None):
        def body(p, packed):
            return pack(packed, ref[n, p + 1, rows(win), :], p, win)

        return planes_loop(body, packed, first, count)

    def ghosts(ref, n, win):
        left = pltpu.roll(ref[n, 0, rows(win), :], 1, 1)
        right = pltpu.roll(ref[n, 1, rows(win), :], width - 1, 1)
        return jnp.where(cut(inject[0], win), left, right)

    def sideways(value, ghost, p, win):
        edge = pltpu.roll(ghost, width - 2 - span * p, 1)
        left = jnp.where(cut(first_lane, win), edge, pltpu.roll(value, 1, 1))
        right = jnp.where(cut(last_lane, win), edge, pltpu.roll(value, width - 1, 1))
        return left, right

    def across(ref, n, p, win):
        return (
            (ref[n, p + 1, rows(win, -1), :] + ref[n, p + 1, rows(win, 1), :])
            + (ref[n, p, rows(win), :] + ref[n, p + 2, rows(win), :])
        )

    def planes_loop(body, init, first=0, count=None):
        count = nz if count is None else count
        return lax.fori_loop(first, first + count, body, init, unroll=min(unroll, count))

    def earlier(ref, n, middle, win):
        if n == 0 and not chained:
            return None
        return ref[n, middle, rows(win), :]

    def pull(v_ref, cv_ref, w, n, ghost, p, win, first):
        v = v_ref[first + n, p + 1, rows(win), :]
        left, right = sideways(v, ghost, p, win)
        total = w.l[n, p, rows(win), :] * left + w.r[n, p, rows(win), :] * right
        total = total + w.c[n, p + 1, rows(win), :] * across(v_ref, first + n, p, win)
        total = total + across(cv_ref, n, p, win)
        before = earlier(v_ref, n, p + 1, win)
        if before is not None:
            total = total + before
        return v, total - w.a[n, p, rows(win), :] * v

    def strip_pull(v_ref, cv_ref, w, n, side, win, first):
        v = v_ref[first + n, side, rows(win), :]
        total = w.sl[n, side, rows(win), :] * pltpu.roll(v, 1, 1)
        total = total + w.sr[n, side, rows(win), :] * pltpu.roll(v, width - 1, 1)
        total = total + w.sd[n, side, rows(win), :] * pltpu.roll(v, span, 1)
        total = total + w.su[n, side, rows(win), :] * pltpu.roll(v, width - span, 1)
        beside = v_ref[first + n, side, rows(win, -1), :] + v_ref[first + n, side, rows(win, 1), :]
        total = total + w.sc[n, side, rows(win), :] * beside
        total = total + (cv_ref[n, side, rows(win, -1), :] + cv_ref[n, side, rows(win, 1), :])
        before = earlier(v_ref, n, side, win)
        if before is not None:
            total = total + before
        return v, total - w.sa[n, side, rows(win), :] * v

    def put_values(v_ref, cv_ref, w, n, side, win, value, packed, first):
        value = jnp.where(cut(inject[side], win), packed, value)
        v_ref[first + n, side, rows(win), :] = value
        cv_ref[n, side, rows(win), :] = w.sc[n, side, rows(win), :] * value

    fine = types.SimpleNamespace(
        l=r.wl, r=r.wr, a=r.wa, c=r.c, d=r.rd, sl=r.swl, sr=r.swr, sd=r.swd, su=r.swu, sa=r.swa, sc=r.sc, sg=r.srd
    )
    mid = types.SimpleNamespace(
        l=r.mwl, r=r.mwr, a=r.mwa, c=r.mc, d=r.mrd, sl=r.smwl, sr=r.smwr, sd=r.smwd, su=r.smwu, sa=r.smwa,
        sc=r.smc, sg=r.smrd,
    )
    top = types.SimpleNamespace(
        l=r.twl, r=r.twr, a=r.twa, c=r.tc, d=r.trd, sl=r.stwl, sr=r.stwr, sd=r.stwd, su=r.stwu, sa=r.stwa,
        sc=r.stc, sg=r.strd,
    )

    wide = blank(full[1])
    edge_recv_wait(kappa_kind)
    edge_recv_wait(kappa_strip_kind)
    kappa_edge = planes_loop(lambda p, packed: pack(packed, r.kap[p, rows(full), :], p, full), wide)

    def arrived(a):
        in_copy(a, 0).wait()
        for j in order[:3]:
            in_copy(a, j).wait_recv()
        edge_start(a)

    for a in range(u_parts):
        arrived(a)
    strip_each(True, lambda copy: copy.wait_recv())
    edge_start(strip_kind)

    for a in range(u_parts):
        edge_recv_wait(a)
    edge_recv_wait(strip_kind)
    for n in range(group):
        def body(p, carry):
            v = r.u[n + 1, p + 1, rows(full), :]
            cc = (half * r.kap[p, rows(full), :]) * (1.0 + v * v)
            r.c[n, p + 1, rows(full), :] = cc
            r.cu[n, p + 1, rows(full), :] = cc * v
            return carry

        planes_loop(body, 0)
        packed = pack_planes(r.u, n + 1, full, wide)
        for side in range(2):
            v = jnp.where(inject[side], packed, r.strip_in[n, side, 0, rows(full), :])
            kk = jnp.where(inject[side], kappa_edge, r.kap_strip[side, rows(full), :])
            cc = (half * kk) * (1.0 + v * v)
            r.su[n + 1, side, rows(full), :] = v
            r.sc[n, side, rows(full), :] = cc
            r.scu[n, side, rows(full), :] = cc * v
    time_send(0)
    time_wait(0)

    for n in range(group):
        for side in range(2):
            cc = r.sc[n, side, rows(full), :]
            total = r.sc[n, side, rows(full, -1), :] + r.sc[n, side, rows(full, 1), :]
            for ref, shift, off in (
                (r.swl, 1, None), (r.swr, width - 1, None),
                (r.swd, span, first_plane[side]), (r.swu, width - span, last_plane[side]),
            ):
                near = pltpu.roll(cc, shift, 1)
                weight = cc + near
                if off is not None:
                    near, weight = jnp.where(off, 0.0, near), jnp.where(off, 0.0, weight)
                ref[n, side, rows(full), :] = weight
                total = total + near
            diagonal = 1.0 + (6.0 * cc + total)
            r.swa[n, side, rows(full), :] = diagonal
            r.srd[n, side, rows(full), :] = r.damp[1 + side, rows(full), :] / diagonal
        ghost_c, ghost_u = ghosts(r.sc, n, full), ghosts(r.su, n + 1, full)

        def body(p, carry):
            cc = r.c[n, p + 1, rows(full), :]
            left, right = sideways(cc, ghost_c, p, full)
            left, right = cc + left, cc + right
            r.wl[n, p, rows(full), :] = left
            r.wr[n, p, rows(full), :] = right
            diagonal = 1.0 + ((4.0 * cc + left) + (right + across(r.c, n, p, full)))
            r.wa[n, p, rows(full), :] = diagonal
            r.rd[n, p, rows(full), :] = r.damp[0, rows(full), :] / diagonal
            _, total = pull(r.u, r.cu, fine, n, ghost_u, p, full, 1)
            r.res[n, p, rows(full), :] = total
            return carry

        planes_loop(body, 0)
        for side in range(2):
            _, total = strip_pull(r.su, r.scu, fine, n, side, full, 1)
            r.sres[n, side, rows(full), :] = total
        if n == 1:
            arrived(u_parts)
    arrived(u_parts + 1)

    pairs = ((mid, fine, 2), (top, mid, 1))
    for to, of, count in pairs:
        for n in range(count):

            def body(p, carry):
                to.c[n, p + 1, rows(full), :] = of.c[2 * n, p + 1, rows(full), :] + of.c[2 * n + 1, p + 1, rows(full), :]
                for one, two in ((to.l, of.l), (to.r, of.r)):
                    one[n, p, rows(full), :] = two[2 * n, p, rows(full), :] + two[2 * n + 1, p, rows(full), :]
                diagonal = (of.a[2 * n, p, rows(full), :] - 1.0) + of.a[2 * n + 1, p, rows(full), :]
                to.a[n, p, rows(full), :] = diagonal
                to.d[n, p, rows(full), :] = r.damp[0, rows(full), :] / diagonal
                return carry

            planes_loop(body, 0)
            for side in range(2):
                for one, two in (
                    (to.sc, of.sc), (to.sl, of.sl), (to.sr, of.sr), (to.sd, of.sd), (to.su, of.su),
                ):
                    one[n, side, rows(full), :] = two[2 * n, side, rows(full), :] + two[2 * n + 1, side, rows(full), :]
                diagonal = (of.sa[2 * n, side, rows(full), :] - 1.0) + of.sa[2 * n + 1, side, rows(full), :]
                to.sa[n, side, rows(full), :] = diagonal
                to.sg[n, side, rows(full), :] = r.damp[1 + side, rows(full), :] / diagonal

    def first_update(n, part, win):
        def body(p, carry):
            left = r.src[n, p, rows(win), :] + r.res[n, p, rows(win), :]
            r.res[n, p, rows(win), :] = left
            update = left * r.rd[n, p, rows(win), :]
            r.e1[n + 1, p + 1, rows(win), :] = update
            r.ce1[n, p + 1, rows(win), :] = r.c[n, p + 1, rows(win), :] * update
            return carry

        planes_loop(body, 0, part * piece, piece)

    outer = [(pad - halo, halo), (pad + tx, halo)]

    def inner_update(part):
        for n in range(group):
            first_update(n, part, core)
        for number, (first, count) in enumerate(pieces[0]):
            if first + count == (part + 1) * piece:
                out_each(0, number, False, lambda copy: copy.start())
                out_copy(0, 0, number).start()

    def outer_update(part):
        edge_recv_wait(u_parts + part)
        for n in range(group):
            for win in outer:
                first_update(n, part, win)
            packed = r.packed_one[n, rows(full), :] if part else wide
            r.packed_one[n, rows(full), :] = pack_planes(r.e1, n + 1, full, packed, part * piece, piece)

    narrow = blank(trim[1])

    def pack_more(stage, ref, n, number):
        first, last = reach(number, stage)
        packed = r.packs[stage - 1, n, rows(trim), :] if number else narrow
        packed = pack_planes(ref, n + 1, trim, packed, first, last - first)
        if number < len(passes) - 1:
            r.packs[stage - 1, n, rows(trim), :] = packed
        return packed

    def again(number, stage, w, v, cv, sv, scv, b, sb, to_v, to_cv, to_sv, to_scv, count):
        first, last = reach(number, stage)
        for n in range(count):
            ghost = ghosts(sv, n + 1, trim)

            def body(p, carry):
                value, total = pull(v, cv, w, n, ghost, p, trim, 1)
                left = b[n, p, rows(trim), :] + total
                update = value + left * w.d[n, p, rows(trim), :]
                to_v[n + 1, p + 1, rows(trim), :] = update
                to_cv[n, p + 1, rows(trim), :] = w.c[n, p + 1, rows(trim), :] * update
                return carry

            planes_loop(body, 0, first, last - first)
            packed = pack_more(stage, to_v, n, number)
            for side in range(2):
                value, total = strip_pull(sv, scv, w, n, side, trim, 1)
                left = sb[n, side, rows(trim), :] + total
                update = value + left * w.sg[n, side, rows(trim), :]
                put_values(to_sv, to_scv, w, n, side, trim, update, packed, 1)

    def coarsen(number, stage, w, to, v, cv, sv, scv, b, sb, to_b, to_sb, to_v, to_cv, to_sv, to_scv, count):
        first, last = reach(number, stage)
        for n in range(count):
            both = [ghosts(sv, 2 * n + i + 1, trim) for i in range(2)]

            def body(p, carry):
                rhs = None
                for i in range(2):
                    _, total = pull(v, cv, w, 2 * n + i, both[i], p, trim, 1)
                    left = b[2 * n + i, p, rows(trim), :] + total
                    rhs = left if rhs is None else rhs + left
                to_b[n, p, rows(trim), :] = rhs
                update = rhs * to.d[n, p, rows(trim), :]
                to_v[n + 1, p + 1, rows(trim), :] = update
                to_cv[n, p + 1, rows(trim), :] = to.c[n, p + 1, rows(trim), :] * update
                return carry

            planes_loop(body, 0, first, last - first)
            packed = pack_more(stage, to_v, n, number)
            for side in range(2):
                rhs = None
                for i in range(2):
                    _, total = strip_pull(sv, scv, w, 2 * n + i, side, trim, 1)
                    left = sb[2 * n + i, side, rows(trim), :] + total
                    rhs = left if rhs is None else rhs + left
                to_sb[n, side, rows(trim), :] = rhs
                update = rhs * to.sg[n, side, rows(trim), :]
                put_values(to_sv, to_scv, to, n, side, trim, update, packed, 1)

    def run_pass(number):
        started, ended = number == 0, number == len(passes) - 1

        def meet(level):
            if ended:
                time_send(level)
            if started:
                time_wait(level)

        for n in range(group):
            for side in range(2):
                put_values(
                    r.se1, r.sce1, fine, n, side, full, r.sres[n, side, rows(full), :] * r.srd[n, side, rows(full), :],
                    r.packed_one[n, rows(full), :], 1,
                )
        meet(1)
        again(number, 1, fine, r.e1, r.ce1, r.se1, r.sce1, r.res, r.sres, r.e2, r.ce2, r.se2, r.sce2, group)
        meet(2)
        coarsen(
            number, 2, fine, mid, r.e2, r.ce2, r.se2, r.sce2, r.res, r.sres, r.mb, r.smb, r.me1, r.cme1, r.sme1,
            r.scme1, 2,
        )
        meet(3)
        again(number, 3, mid, r.me1, r.cme1, r.sme1, r.scme1, r.mb, r.smb, r.me2, r.cme2, r.sme2, r.scme2, 2)
        meet(4)
        coarsen(
            number, 4, mid, top, r.me2, r.cme2, r.sme2, r.scme2, r.mb, r.smb, r.tb, r.stb, r.te, r.cte, r.ste, r.scte,
            1,
        )
        meet(5)
        ghost = ghosts(r.ste, 1, core)

        def body(p, carry):
            value, total = pull(r.te, r.cte, top, 0, ghost, p, core, 1)
            update = value + (r.tb[0, p, real, :] + total) * r.trd[0, p, real, :]
            for n in range(group):
                middle = r.me2[n // 2 + 1, p + 1, real, :] + update
                r.new[n, p, real, :] = r.u[n + 1, p + 1, real, :] + (r.e2[n + 1, p + 1, real, :] + middle)
            return carry

        first, last = reach(number, stages)
        planes_loop(body, 0, first, last - first)
        out_each(1, number, False, lambda copy: copy.start())
        out_copy(1, 0, number).start()

    for n in range(group):
        for side in range(2):
            r.sres[n, side, rows(full), :] = (
                r.strip_in[n, side, 1, rows(full), :] + r.sres[n, side, rows(full), :]
            )
    for part in range(parts):
        if part > 1:
            arrived(u_parts + part)
        inner_update(part)
        if part:
            outer_update(part - 1)
            if part in passes:
                run_pass(passes.index(part))
    outer_update(parts - 1)
    run_pass(len(passes) - 1)

    @pl.when(jnp.logical_not(has_before))
    def _():
        def clear_before(p, carry):
            for i in range(pair):
                r.before[p, :, i * width : (i + 1) * width] = nothing
            return carry

        lax.fori_loop(0, nz, clear_before, 0)

    @pl.when(has_before)
    def _():
        pltpu.make_async_remote_copy(
            src_ref=r.before, dst_ref=r.before, send_sem=r.before_sem.at[0], recv_sem=r.before_sem.at[1],
            device_id={"tm": me}, device_id_type=mesh_ids,
        ).wait_recv()

    far_real = pl.ds(halo, tx)
    bare = (halo, tx)

    def far_out(i):
        return pltpu.make_async_copy(
            r.far_res.at[i], r.res_out.at[0, 0, :, :, columns(far_block + i)], r.far_sem.at[2, i]
        )

    @pl.when(own_work)
    def _():
        for number in range(2):

            @pl.when(flanks[number][0])
            def _():
                row_copy(1 - number).wait_recv()

            for i in range(pair):
                value = r.row_in[number, 0, i]
                r.row_c[number, i] = (half * r.row_in[number, 1, i]) * (1.0 + value * value)
        for ref in (r.lu, r.lc):
            for k in range(pair + 3):
                for plane in (0, nz + 1):
                    ref[k, plane] = blank(tx + pad)

            def clear_outer(p, carry):
                for k in (0, pair + 2):
                    ref[k, p + 1, far_real, :] = nothing
                return carry

            lax.fori_loop(0, nz, clear_outer, 0)

        def far_coefficient(p, carry):
            for k in range(pair + 1):
                value = r.lu[1 + k, p + 1, far_real, :]
                r.lc[1 + k, p + 1, far_real, :] = (half * r.lkap[1 + k, p]) * (1.0 + value * value)
            for i in range(pair):
                k = far_block - near_block + i
                for number, row in enumerate((halo - 1, halo + tx)):
                    r.lu[1 + k, p + 1, pl.ds(row, 1), :] = r.row_in[number, 0, i, pl.ds(p, 1), :]
                    r.lc[1 + k, p + 1, pl.ds(row, 1), :] = r.row_c[number, i, pl.ds(p, 1), :]
            return carry

        lax.fori_loop(0, nz, far_coefficient, 0, unroll=2)
        first_tx, last_tx = lane_tx == 0, lane_tx == width - 1
        for i in range(pair):
            k = 1 + far_block - near_block + i
            own_columns = columns(far_block + i)

            def body(p, carry):
                def near_of(ref):
                    here = ref[k, p + 1, far_real, :]
                    before, after = ref[k - 1, p + 1, far_real, :], ref[k + 1, p + 1, far_real, :]
                    return here, (
                        jnp.where(first_tx, pltpu.roll(before, 1, 1), pltpu.roll(here, 1, 1)),
                        jnp.where(last_tx, pltpu.roll(after, width - 1, 1), pltpu.roll(here, width - 1, 1)),
                        ref[k, p + 1, pl.ds(halo - 1, tx), :], ref[k, p + 1, pl.ds(halo + 1, tx), :],
                        ref[k, p, far_real, :], ref[k, p + 2, far_real, :],
                    )

                value, value_near = near_of(r.lu)
                cc, c_near = near_of(r.lc)
                left = r.own[1, p, :, own_columns] - value + r.before[p, :, i * width : (i + 1) * width]
                for one, two in zip(value_near, c_near):
                    left = left - (cc + two) * (value - one)
                r.far_res[i, p] = left
                return carry

            lax.fori_loop(0, nz, body, 0, unroll=4)
            far_out(i).start()
        for i in range(pair):
            far_out(i).wait()
        for number in range(2):

            @pl.when(flanks[number][0])
            def _():
                row_copy(number).wait_send()

    @pl.when(has_after)
    def _():
        before_copy().wait_send()

    strip_each(False, lambda copy: copy.wait_send())
    for a in range(u_parts + parts):
        for j in order[:3]:
            in_copy(a, j).wait_send()
    for kind in range(u_parts + parts + 3):
        edge_send_wait(kind)
    if chained:

        @pl.when(has_next)
        def _():
            for number in range(len(time_refs)):
                for copy in time_copies(number):
                    copy.wait_send()

    for a in range(2):
        for part in range(len(pieces[a])):
            out_copy(a, 0, part).wait()
            out_each(a, part, False, lambda copy: copy.wait_send())
            out_each(a, part, True, lambda copy: copy.wait_recv())


def shards(tm_size, space_size, iterate, source_term, conductivity):
    _, nz, tx, ty = conductivity.shape
    width = ty // group
    tall = tx + 2 * pad
    f32 = jnp.float32
    dma = pltpu.SemaphoreType.DMA
    kinds = u_parts + parts + 3

    def padded(count):
        return pltpu.VMEM((count, nz + 2, tall, width), f32)

    def plain(*lead):
        return pltpu.VMEM((*lead, nz, tall, width), f32)

    def strip(*lead):
        return pltpu.VMEM((*lead, 2, tall, width), f32)

    scratch = {}
    scratch |= {name: padded(count) for name, count in (
        ("u", 5), ("c", 4), ("cu", 4), ("e1", 5), ("ce1", 4), ("e2", 5), ("ce2", 4), ("mc", 2), ("me1", 3),
        ("cme1", 2), ("me2", 3), ("cme2", 2), ("tc", 1), ("te", 2), ("cte", 1),
    )}
    scratch |= {name: plain(count) for name, count in (
        ("src", 4), ("res", 4), ("wl", 4), ("wr", 4), ("wa", 4), ("rd", 4), ("mwl", 2), ("mwr", 2), ("mwa", 2),
        ("mrd", 2), ("mb", 2), ("twl", 1), ("twr", 1), ("twa", 1), ("trd", 1), ("tb", 1), ("new", 4),
    )}
    scratch["kap"] = plain()
    scratch |= {name: strip(count) for name, count in (
        ("su", 5), ("sc", 4), ("scu", 4), ("se1", 5), ("sce1", 4), ("se2", 5), ("sce2", 4), ("smc", 2),
        ("sme1", 3), ("scme1", 2), ("sme2", 3), ("scme2", 2), ("stc", 1), ("ste", 2), ("scte", 1),
        ("swl", 4), ("swr", 4), ("swd", 4), ("swu", 4), ("swa", 4), ("srd", 4), ("sres", 4),
        ("smwl", 2), ("smwr", 2), ("smwd", 2), ("smwu", 2), ("smwa", 2), ("smrd", 2), ("smb", 2),
        ("stwl", 1), ("stwr", 1), ("stwd", 1), ("stwu", 1), ("stwa", 1), ("strd", 1), ("stb", 1),
    )}
    scratch["kap_strip"] = strip()
    scratch["strip_in"] = strip(group, 2)
    scratch["strip_send"] = pltpu.VMEM((group, 2, 2, tx, width), f32)
    scratch["own"] = pltpu.VMEM((2, nz, tx, ty), f32)
    scratch["beside"] = pltpu.VMEM((2, nz, tx, width), f32)
    pair = group // 2
    scratch["lu"] = pltpu.VMEM((pair + 3, nz + 2, tx + pad, width), f32)
    scratch["lc"] = pltpu.VMEM((pair + 3, nz + 2, tx + pad, width), f32)
    scratch["lkap"] = pltpu.VMEM((pair + 2, nz, tx, width), f32)
    scratch["before"] = pltpu.VMEM((nz, tx, pair * width), f32)
    scratch["far_res"] = pltpu.VMEM((pair, nz, tx, width), f32)
    scratch["row_send"] = pltpu.VMEM((2, 2, pair, nz, width), f32)
    scratch["row_in"] = pltpu.VMEM((2, 2, pair, nz, width), f32)
    scratch["row_c"] = pltpu.VMEM((2, pair, nz, width), f32)
    scratch["packs"] = pltpu.VMEM((stages - 1, group, tall, width), f32)
    scratch["packed_one"] = pltpu.VMEM((group, tall, width), f32)
    scratch["damp"] = pltpu.VMEM((3, tall, width), f32)
    for name, shape in (
        ("loc_sem", (5,)), ("in_lsem", (u_parts + parts,)), ("in_ssem", (u_parts + parts, group - 1)),
        ("in_rsem", (u_parts + parts, group - 1)), ("out_lsem", (2, len(passes) + 1)), ("out_ssem", (2, len(passes) + 1, group - 1)),
        ("out_rsem", (2, len(passes) + 1, group - 1)), ("strip_ssem", (group - 1, 2)), ("strip_rsem", (group - 1, 2)),
        ("edge_ssem", (kinds, 2)), ("edge_rsem", (kinds, 2)), ("time_ssem", (6, 2)), ("far_sem", (3, pair + 1)),
        ("before_sem", (2,)), ("row_sem", (2, 2)),
        ("time_rsem", (6, 2)),
    ):
        scratch[name] = dma(shape)
    names = ("state_in", "source_in", "kappa_in", "new_out", "res_out", *scratch)
    out = jax.ShapeDtypeStruct(iterate.shape, f32)
    hbm = pl.BlockSpec(memory_space=pltpu.HBM)
    return pl.pallas_call(
        functools.partial(kernel, tm_size, space_size, names),
        out_shape=(out, out),
        in_specs=[hbm] * 3,
        out_specs=(hbm, hbm),
        scratch_shapes=list(scratch.values()),
        compiler_params=pltpu.CompilerParams(
            collective_id=0, has_side_effects=True, vmem_limit_bytes=67043328
        ),
    )(iterate, source_term, conductivity)


def solution(mesh):
    tiled = P("tm", "space", None, None, None)
    in_specs = (tiled, tiled, P("space", None, None, None))
    body = functools.partial(shards, mesh.shape["tm"], mesh.shape["space"])
    return jax.shard_map(
        body, mesh=mesh, in_specs=in_specs, out_specs=(tiled, tiled), check_vma=False
    )
```

```python
import functools
import types

import jax
import jax.numpy as jnp
from jax import lax
from jax.experimental import pallas as pl
from jax.experimental.pallas import tpu as pltpu
from jax.sharding import PartitionSpec as P

tau_step = 0.08
damping = 0.7
group = 4
halo = 8
pad = 2 * halo
u_parts = 2
shares = (6, 6, 4)
parts = len(shares)
passes = (1, 2, 3)
stages = 5
mesh_ids = pl.DeviceIdType.MESH
order = (2, 1, 3, 0)
unroll = 8


def kernel(tm_size, space_size, names, *refs):
    r = types.SimpleNamespace(**dict(zip(names, refs)))
    _, nz, tx, _ = r.kappa_in.shape
    width = r.kap.shape[-1]
    span = width // nz
    chained = tm_size > group
    half = 0.5 * tau_step
    u_piece = nz // u_parts
    cuts = [nz * sum(shares[:k]) // sum(shares) for k in range(parts + 1)]
    spans = [(cuts[k], cuts[k + 1] - cuts[k]) for k in range(parts)]

    def reach(number, stage):
        bounds = [0] + [cuts[known] - stage if known < parts else nz for known in passes]
        return max(bounds[number], 0), bounds[number + 1]

    pieces = [[(0, cuts[-2]), spans[-1]], []]
    for number in range(len(passes)):
        first, last = reach(number, stages)
        pieces[1].append((first, last - first))

    full = (pad - halo, tx + 2 * halo)
    trim = (pad - halo // 2, tx + halo)
    core = (pad, tx)

    def rows(win, shift=0):
        return pl.ds(win[0] + shift, win[1])

    real = rows(core)
    planes = pl.ds(1, nz)
    me = lax.axis_index("tm")
    sp = lax.axis_index("space")
    q = me % group
    base = me - q
    has_dn, has_up = sp > 0, sp < space_size - 1
    has_left, has_right = q > 0, q < group - 1
    has_prev, has_next = base > 0, base + group < tm_size
    pair = group // 2
    lower = q < pair
    own_work = q != pair
    far_block = jnp.where(lower, pair, 0)
    near_block = jnp.where(lower, pair - 1, 0)
    has_before = jnp.logical_and(own_work, me > 0)
    has_after = jnp.logical_and(q != pair - 1, me + 1 < tm_size)
    flanks = [(has_dn, {"space": sp - 1}), (has_up, {"space": sp + 1})]
    beside_has = [has_left, has_right]

    def columns(d):
        return pl.ds(pl.multiple_of(d * width, width), width)

    own_copies = [
        pltpu.make_async_copy(hbm.at[0, 0], r.own.at[f], r.loc_sem.at[f])
        for f, hbm in enumerate((r.state_in, r.source_in))
    ]
    kappa_copy = pltpu.make_async_copy(
        r.kappa_in.at[0, :, :, columns(q)], r.kap.at[:, real, :], r.loc_sem.at[2]
    )

    def beside_copy(side):
        block = r.kappa_in.at[0, :, :, columns(q - 1 + 2 * side)]
        return pltpu.make_async_copy(block, r.beside.at[side], r.loc_sem.at[3 + side])

    own_copies[0].start()
    kappa_copy.start()
    for side in range(2):

        @pl.when(beside_has[side])
        def _():
            beside_copy(side).start()

    own_copies[1].start()

    def wide_columns(first, count):
        return pl.ds(pl.multiple_of(first * width, width), count * width)

    def far_copies():
        made = []
        for k in range(pair + 1):
            made.append(
                pltpu.make_async_copy(
                    r.state_in.at[0, 0, :, :, columns(near_block + k)],
                    r.lu.at[1 + k, pl.ds(1, nz), pl.ds(halo, tx), :], r.far_sem.at[0, k],
                )
            )
            made.append(
                pltpu.make_async_copy(
                    r.kappa_in.at[0, :, :, columns(near_block + k)], r.lkap.at[1 + k], r.far_sem.at[1, k]
                )
            )
        return made

    @pl.when(own_work)
    def _():
        for copy in far_copies():
            copy.start()

    def before_copy():
        first = jnp.where((q + 1) % group < pair, pair, 0)
        return pltpu.make_async_remote_copy(
            src_ref=r.state_in.at[0, 0, :, :, wide_columns(first, pair)], dst_ref=r.before,
            send_sem=r.before_sem.at[0], recv_sem=r.before_sem.at[1], device_id={"tm": me + 1},
            device_id_type=mesh_ids,
        )

    def row_copy(number):
        return pltpu.make_async_remote_copy(
            src_ref=r.row_send.at[number], dst_ref=r.row_in.at[1 - number],
            send_sem=r.row_sem.at[0, number], recv_sem=r.row_sem.at[1, 1 - number],
            device_id=flanks[number][1], device_id_type=mesh_ids,
        )

    barrier = pltpu.get_barrier_semaphore()
    for j in range(1, group):
        pl.semaphore_signal(
            barrier, inc=1, device_id={"tm": base + (q + j) % group}, device_id_type=mesh_ids
        )
    greeted = list(flanks)
    if chained:
        greeted += [(has_prev, {"tm": me - group}), (has_next, {"tm": me + group})]
        greeted += [(jnp.logical_and(has_prev, q == 0), {"tm": me - 1})]
        greeted += [(jnp.logical_and(has_next, q == group - 1), {"tm": me + 1})]
    for has, where in greeted:

        @pl.when(has)
        def _():
            pl.semaphore_signal(barrier, inc=1, device_id=where, device_id_type=mesh_ids)

    expected = group - 1
    for has, _ in greeted:
        expected = expected + jnp.where(has, 1, 0)
    pl.semaphore_wait(barrier, expected)

    def in_copy(a, j):
        d = (q + j) % group
        if a < u_parts:
            some = pl.ds(a * u_piece, u_piece)
            hbm = r.state_in.at[0, 0, some, :, columns(d)]
            dst = r.u.at[q + 1, pl.ds(1 + a * u_piece, u_piece), real, :]
        else:
            some = pl.ds(*spans[a - u_parts])
            hbm, dst = r.source_in.at[0, 0, some, :, columns(d)], r.src.at[q, some, real, :]
        if j == 0:
            return pltpu.make_async_copy(hbm, dst, r.in_lsem.at[a])
        return pltpu.make_async_remote_copy(
            src_ref=hbm, dst_ref=dst, send_sem=r.in_ssem.at[a, j - 1],
            recv_sem=r.in_rsem.at[a, j - 1], device_id={"tm": base + d}, device_id_type=mesh_ids,
        )

    def out_copy(a, j, part):
        d = (q + j) % group
        some = pl.ds(*pieces[a][part])
        hbm = (r.res_out, r.new_out)[a].at[0, 0, some, :, columns(q)]
        held = (r.res, r.new)[a].at[d, some, real, :]
        if j == 0:
            return pltpu.make_async_copy(held, hbm, r.out_lsem.at[a, part])
        return pltpu.make_async_remote_copy(
            src_ref=held, dst_ref=hbm, send_sem=r.out_ssem.at[a, part, j - 1],
            recv_sem=r.out_rsem.at[a, part, j - 1], device_id={"tm": base + d},
            device_id_type=mesh_ids,
        )

    def out_each(a, part, receiving, act):
        for j in order[:3]:
            one, two = ((q - j) % group, q) if receiving else (q, (q + j) % group)
            if a == 0:
                wanted = jnp.logical_or(one // pair == two // pair, jnp.logical_and(two == pair, one < pair))

                @pl.when(wanted)
                def _():
                    act(out_copy(a, j, part))
            else:
                act(out_copy(a, j, part))

    def strip_copy(j, side):
        d = (q + j) % group
        return pltpu.make_async_remote_copy(
            src_ref=r.strip_send.at[d, side], dst_ref=r.strip_in.at[q, side, :, real, :],
            send_sem=r.strip_ssem.at[j - 1, side], recv_sem=r.strip_rsem.at[j - 1, side],
            device_id={"tm": base + d}, device_id_type=mesh_ids,
        )

    def strip_each(receiving, act):
        for j in order[:3]:
            d = q if receiving else (q + j) % group
            for side, has in enumerate((d > 0, d < group - 1)):

                @pl.when(has)
                def _():
                    act(strip_copy(j, side))


    strip_kind = u_parts + parts
    kappa_kind, kappa_strip_kind = strip_kind + 1, strip_kind + 2

    def edge_ref(kind, where):
        if kind < u_parts:
            return r.u.at[pl.ds(1, group), pl.ds(1 + kind * u_piece, u_piece), where, :]
        if kind < strip_kind:
            return r.src.at[:, pl.ds(*spans[kind - u_parts]), where, :]
        if kind == strip_kind:
            return r.strip_in.at[:, :, :, where, :]
        if kind == kappa_kind:
            return r.kap.at[:, where, :]
        return r.kap_strip.at[:, where, :]

    def edge_copy(kind, number):
        if number == 0:
            source, target = pl.ds(pad, halo), pl.ds(pad + tx, halo)
        else:
            source, target = pl.ds(pad + tx - halo, halo), pl.ds(pad - halo, halo)
        return pltpu.make_async_remote_copy(
            src_ref=edge_ref(kind, source), dst_ref=edge_ref(kind, target),
            send_sem=r.edge_ssem.at[kind, number], recv_sem=r.edge_rsem.at[kind, number],
            device_id=flanks[number][1], device_id_type=mesh_ids,
        )

    def edge_start(kind):
        for number in range(2):

            @pl.when(flanks[number][0])
            def _():
                edge_copy(kind, number).start()

    def edge_send_wait(kind):
        for number in range(2):

            @pl.when(flanks[number][0])
            def _():
                edge_copy(kind, number).wait_send()

    def edge_recv_wait(kind):
        for number in range(2):

            @pl.when(flanks[number][0])
            def _():
                edge_copy(kind, 1 - number).wait_recv()

    time_refs = [(r.u, group), (r.e1, group), (r.e2, group), (r.me1, 2), (r.me2, 2), (r.te, 1)]
    time_strips = [
        (r.su, group), (r.se1, group), (r.se2, group), (r.sme1, 2), (r.sme2, 2), (r.ste, 1),
    ]

    def time_copies(number):
        made = []
        for kind, (ref, last) in enumerate((time_refs[number], time_strips[number])):
            middle = planes if kind == 0 else pl.ds(0, 2)
            made.append(
                pltpu.make_async_remote_copy(
                    src_ref=ref.at[last, middle, rows(full), :],
                    dst_ref=ref.at[0, middle, rows(full), :],
                    send_sem=r.time_ssem.at[number, kind], recv_sem=r.time_rsem.at[number, kind],
                    device_id={"tm": me + group}, device_id_type=mesh_ids,
                )
            )
        return made

    def time_send(number):
        if chained:

            @pl.when(has_next)
            def _():
                for copy in time_copies(number):
                    copy.start()

    def time_wait(number):
        if chained:

            @pl.when(has_prev)
            def _():
                for copy in time_copies(number):
                    copy.wait_recv()

    for j in order:
        in_copy(0, j).start()
    kappa_copy.wait()
    edge_start(kappa_kind)

    f32 = jnp.float32
    tall = r.u.shape[2]

    def blank(count):
        return jnp.zeros((count, width), f32)

    for side in range(2):

        @pl.when(jnp.logical_not(beside_has[side]))
        def _():
            def clear_beside(p, carry):
                r.beside[side, p] = blank(tx)
                return carry

            lax.fori_loop(0, nz, clear_beside, 0)
            for n in range(group):
                for f in range(2):
                    r.strip_in[n, side, f, real, :] = blank(tx)

    lane_tx = lax.broadcasted_iota(jnp.int32, (tx, width), 1)
    lane = lax.broadcasted_iota(jnp.int32, (tx + 2 * halo, width), 1)

    def plane_of(side, lanes):
        return ((lanes + (span // 2, 0)[side]) % width) // span

    inside = [plane_of(side, lane_tx) for side in range(2)]

    def put_strip(packed, side, block, p):
        return jnp.where(inside[side] == p, pltpu.roll(block, span * p + 2, 1), packed)

    nothing = blank(tx)

    def pack_own(f):
        def body(p, packed):
            blocks = [r.own[f, p, :, d * width : (d + 1) * width] for d in range(group)]
            made = []
            for d in range(group):
                left, right = packed[2 * d], packed[2 * d + 1]
                turned_left = blocks[d - 1] if d else None
                turned_right = blocks[d + 1] if d < group - 1 else None
                made.append(left if turned_left is None else put_strip(left, 0, turned_left, p))
                made.append(right if turned_right is None else put_strip(right, 1, turned_right, p))
            return tuple(made)

        packed = lax.fori_loop(0, nz, body, (nothing,) * (2 * group), unroll=2)
        for d in range(group):
            for side in range(2):
                r.strip_send[d, side, f] = packed[2 * d + side]
        for side in range(2):
            r.strip_in[q, side, f, real, :] = r.strip_send[q, side, f]

    for f in range(2):
        own_copies[f].wait()
        pack_own(f)
    strip_each(False, lambda copy: copy.start())
    for a in range(1, u_parts + parts):
        for j in order:
            in_copy(a, j).start()

    @pl.when(has_after)
    def _():
        before_copy().start()

    @pl.when(own_work)
    def _():
        for copy in far_copies():
            copy.wait()

        def far_rows(p, carry):
            for i in range(pair):
                k = far_block - near_block + i
                for number, row in enumerate((0, tx - 1)):
                    r.row_send[number, 0, i, pl.ds(p, 1), :] = r.lu[1 + k, p + 1, pl.ds(halo + row, 1), :]
                    r.row_send[number, 1, i, pl.ds(p, 1), :] = r.lkap[1 + k, p, pl.ds(row, 1), :]
            return carry

        lax.fori_loop(0, nz, far_rows, 0, unroll=4)
        for number in range(2):

            @pl.when(flanks[number][0])
            def _():
                row_copy(number).start()

            @pl.when(jnp.logical_not(flanks[number][0]))
            def _():
                for f in range(2):
                    for i in range(pair):
                        r.row_in[number, f, i] = blank(nz)

    held = [(ref, 1) for ref, _ in time_refs]
    held += [(ref, 0) for ref in (r.c, r.cu, r.ce1, r.ce2, r.mc, r.cme1, r.cme2, r.tc, r.cte)]
    early = (r.u, r.c, r.cu, r.e1, r.ce1)
    for ref, first in held:
        for n in range(first, ref.shape[0]):
            for plane in (0, nz + 1):
                ref[n, plane] = blank(tall)

    def clear_rows(p, carry):
        for ref, first in held:
            outer = any(ref is one for one in early)
            low, high = (0, tall - halo) if outer else (halo, tall - pad)
            for n in range(first, ref.shape[0]):
                ref[n, p + 1, pl.ds(low, halo), :] = blank(halo)
                ref[n, p + 1, pl.ds(high, halo), :] = blank(halo)
        return carry

    lax.fori_loop(0, nz, clear_rows, 0)
    strips = [(ref, 1) for ref, _ in time_strips]
    strips += [(ref, 0) for ref in (r.sc, r.scu, r.sce1, r.sce2, r.smc, r.scme1, r.scme2, r.stc, r.scte)]
    for ref, first in strips:
        for n in range(first, ref.shape[0]):
            for side in range(2):
                ref[n, side] = blank(tall)
    if chained:

        @pl.when(jnp.logical_not(has_prev))
        def _():
            def clear_first(p, carry):
                for ref, _ in time_refs:
                    ref[0, p + 1] = blank(tall)
                return carry

            lax.fori_loop(0, nz, clear_first, 0)
            for ref, _ in time_strips:
                for side in range(2):
                    ref[0, side] = blank(tall)

    for number, (has, _) in enumerate(flanks):
        edge = pl.ds((pad - halo, pad + tx)[number], halo)

        @pl.when(jnp.logical_not(has))
        def _():
            def clear_edges(p, carry):
                r.kap[p, edge, :] = blank(halo)
                for n in range(group):
                    r.u[n + 1, p + 1, edge, :] = blank(halo)
                    r.src[n, p, edge, :] = blank(halo)
                return carry

            lax.fori_loop(0, nz, clear_edges, 0)
            for side in range(2):
                r.kap_strip[side, edge, :] = blank(halo)
                for f in range(2):
                    for n in range(group):
                        r.strip_in[n, side, f, edge, :] = blank(halo)

    for side in range(2):

        @pl.when(beside_has[side])
        def _():
            beside_copy(side).wait()

    def kappa_body(p, packed):
        return tuple(put_strip(packed[side], side, r.beside[side, p], p) for side in range(2))

    packed = lax.fori_loop(0, nz, kappa_body, (nothing, nothing), unroll=2)
    for side in range(2):
        r.kap_strip[side, real, :] = packed[side]
    edge_start(kappa_strip_kind)

    level = lax.broadcasted_iota(jnp.int32, (tx + 2 * halo, width), 0)
    below = jnp.where(has_dn, damping, 0.0)
    above = jnp.where(has_up, damping, 0.0)
    damp = jnp.where(level < halo, below, jnp.where(level < halo + tx, damping, above))
    r.damp[0, rows(full), :] = damp
    for side in range(2):
        r.damp[1 + side, rows(full), :] = damp * jnp.where(beside_has[side], 1.0, 0.0)

    first_plane = [plane_of(side, lane) == 0 for side in range(2)]
    last_plane = [plane_of(side, lane) == nz - 1 for side in range(2)]
    inject = [lane % span == 2, lane % span == 1]
    plane_lane = lane // span
    first_lane = lane == 0
    last_lane = lane == width - 1

    def cut(mask, win):
        return mask[: win[1]]

    def pack(packed, value, p, win):
        return jnp.where(cut(plane_lane, win) == p, pltpu.roll(value, span * p + 2, 1), packed)

    def pack_planes(ref, count, win, packed, first=0, planes_count=None):
        def body(p, packed):
            return tuple(pack(packed[n], ref[n + 1, p + 1, rows(win), :], p, win) for n in range(count))

        return planes_loop(body, tuple(packed), first, planes_count)

    def ghosts(ref, n, win):
        left = pltpu.roll(ref[n, 0, rows(win), :], 1, 1)
        right = pltpu.roll(ref[n, 1, rows(win), :], width - 1, 1)
        return jnp.where(cut(inject[0], win), left, right)

    def sideways(value, ghost, p, win):
        edge = pltpu.roll(ghost, width - 2 - span * p, 1)
        left = jnp.where(cut(first_lane, win), edge, pltpu.roll(value, 1, 1))
        right = jnp.where(cut(last_lane, win), edge, pltpu.roll(value, width - 1, 1))
        return left, right

    def across(ref, n, p, win):
        return (
            (ref[n, p + 1, rows(win, -1), :] + ref[n, p + 1, rows(win, 1), :])
            + (ref[n, p, rows(win), :] + ref[n, p + 2, rows(win), :])
        )

    def planes_loop(body, init, first=0, count=None):
        count = nz if count is None else count
        return lax.fori_loop(first, first + count, body, init, unroll=min(unroll, count))

    def earlier(ref, n, middle, win):
        if n == 0 and not chained:
            return None
        return ref[n, middle, rows(win), :]

    def pull(v_ref, cv_ref, w, n, ghost, p, win, first):
        v = v_ref[first + n, p + 1, rows(win), :]
        left, right = sideways(v, ghost, p, win)
        total = w.l[n, p, rows(win), :] * left + w.r[n, p, rows(win), :] * right
        total = total + w.c[n, p + 1, rows(win), :] * across(v_ref, first + n, p, win)
        total = total + across(cv_ref, n, p, win)
        before = earlier(v_ref, n, p + 1, win)
        if before is not None:
            total = total + before
        return v, total - w.a[n, p, rows(win), :] * v

    def strip_pull(v_ref, cv_ref, w, n, side, win, first):
        v = v_ref[first + n, side, rows(win), :]
        total = w.sl[n, side, rows(win), :] * pltpu.roll(v, 1, 1)
        total = total + w.sr[n, side, rows(win), :] * pltpu.roll(v, width - 1, 1)
        total = total + w.sd[n, side, rows(win), :] * pltpu.roll(v, span, 1)
        total = total + w.su[n, side, rows(win), :] * pltpu.roll(v, width - span, 1)
        beside = v_ref[first + n, side, rows(win, -1), :] + v_ref[first + n, side, rows(win, 1), :]
        total = total + w.sc[n, side, rows(win), :] * beside
        total = total + (cv_ref[n, side, rows(win, -1), :] + cv_ref[n, side, rows(win, 1), :])
        before = earlier(v_ref, n, side, win)
        if before is not None:
            total = total + before
        return v, total - w.sa[n, side, rows(win), :] * v

    def put_values(v_ref, cv_ref, w, n, side, win, value, packed, first):
        value = jnp.where(cut(inject[side], win), packed, value)
        v_ref[first + n, side, rows(win), :] = value
        cv_ref[n, side, rows(win), :] = w.sc[n, side, rows(win), :] * value

    fine = types.SimpleNamespace(
        l=r.wl, r=r.wr, a=r.wa, c=r.c, d=r.rd, sl=r.swl, sr=r.swr, sd=r.swd, su=r.swu, sa=r.swa, sc=r.sc, sg=r.srd
    )
    mid = types.SimpleNamespace(
        l=r.mwl, r=r.mwr, a=r.mwa, c=r.mc, d=r.mrd, sl=r.smwl, sr=r.smwr, sd=r.smwd, su=r.smwu, sa=r.smwa,
        sc=r.smc, sg=r.smrd,
    )
    top = types.SimpleNamespace(
        l=r.twl, r=r.twr, a=r.twa, c=r.tc, d=r.trd, sl=r.stwl, sr=r.stwr, sd=r.stwd, su=r.stwu, sa=r.stwa,
        sc=r.stc, sg=r.strd,
    )

    wide = blank(full[1])
    edge_recv_wait(kappa_kind)
    edge_recv_wait(kappa_strip_kind)
    kappa_edge = planes_loop(lambda p, packed: pack(packed, r.kap[p, rows(full), :], p, full), wide)

    def arrived(a):
        in_copy(a, 0).wait()
        for j in order[:3]:
            in_copy(a, j).wait_recv()
        edge_start(a)

    def coefficients(p, carry):
        scaled = half * r.kap[p, rows(full), :]
        for n in range(group):
            v = r.u[n + 1, p + 1, rows(full), :]
            cc = scaled * (1.0 + v * v)
            r.c[n, p + 1, rows(full), :] = cc
            r.cu[n, p + 1, rows(full), :] = cc * v
        return carry

    def strip_coefficients(packed):
        for n in range(group):
            for side in range(2):
                v = jnp.where(inject[side], packed[n], r.strip_in[n, side, 0, rows(full), :])
                kk = jnp.where(inject[side], kappa_edge, r.kap_strip[side, rows(full), :])
                cc = (half * kk) * (1.0 + v * v)
                r.su[n + 1, side, rows(full), :] = v
                r.sc[n, side, rows(full), :] = cc
                r.scu[n, side, rows(full), :] = cc * v

    def weights(first, count):
        for n in range(group):
            ghost_c, ghost_u = ghosts(r.sc, n, full), ghosts(r.su, n + 1, full)

            def body(p, carry):
                cc = r.c[n, p + 1, rows(full), :]
                left, right = sideways(cc, ghost_c, p, full)
                left, right = cc + left, cc + right
                r.wl[n, p, rows(full), :] = left
                r.wr[n, p, rows(full), :] = right
                diagonal = 1.0 + ((4.0 * cc + left) + (right + across(r.c, n, p, full)))
                r.wa[n, p, rows(full), :] = diagonal
                r.rd[n, p, rows(full), :] = r.damp[0, rows(full), :] / diagonal
                _, total = pull(r.u, r.cu, fine, n, ghost_u, p, full, 1)
                r.res[n, p, rows(full), :] = total
                return carry

            planes_loop(body, 0, first, count)

    def coarser(first, count):
        for to, of, slices in ((mid, fine, 2), (top, mid, 1)):

            def body(p, carry):
                for n in range(slices):
                    to.c[n, p + 1, rows(full), :] = of.c[2 * n, p + 1, rows(full), :] + of.c[2 * n + 1, p + 1, rows(full), :]
                    for one, two in ((to.l, of.l), (to.r, of.r)):
                        one[n, p, rows(full), :] = two[2 * n, p, rows(full), :] + two[2 * n + 1, p, rows(full), :]
                    diagonal = (of.a[2 * n, p, rows(full), :] - 1.0) + of.a[2 * n + 1, p, rows(full), :]
                    to.a[n, p, rows(full), :] = diagonal
                    to.d[n, p, rows(full), :] = r.damp[0, rows(full), :] / diagonal
                return carry

            lax.fori_loop(first, first + count, body, 0, unroll=min(4, count))

    arrived(0)
    strip_each(True, lambda copy: copy.wait_recv())
    edge_start(strip_kind)
    edge_recv_wait(0)
    edge_recv_wait(strip_kind)
    strip_coefficients((wide,) * group)
    lax.fori_loop(0, u_piece, coefficients, 0, unroll=4)
    time_wait(0)
    known = u_piece - 1
    weights(0, known)
    for a in range(1, u_parts):
        arrived(a)
    coarser(0, known)
    packed_u = pack_planes(r.u, group, full, (wide,) * group, 0, u_piece)
    for a in range(1, u_parts):
        edge_recv_wait(a)
    lax.fori_loop(u_piece, nz, coefficients, 0, unroll=4)
    packed_u = pack_planes(r.u, group, full, packed_u, u_piece, nz - u_piece)
    strip_coefficients(packed_u)
    time_send(0)
    for n in range(group):
        for side in range(2):
            cc = r.sc[n, side, rows(full), :]
            total = r.sc[n, side, rows(full, -1), :] + r.sc[n, side, rows(full, 1), :]
            for ref, shift, off in (
                (r.swl, 1, None), (r.swr, width - 1, None),
                (r.swd, span, first_plane[side]), (r.swu, width - span, last_plane[side]),
            ):
                beside = pltpu.roll(cc, shift, 1)
                weight = cc + beside
                if off is not None:
                    beside, weight = jnp.where(off, 0.0, beside), jnp.where(off, 0.0, weight)
                ref[n, side, rows(full), :] = weight
                total = total + beside
            diagonal = 1.0 + (6.0 * cc + total)
            r.swa[n, side, rows(full), :] = diagonal
            r.srd[n, side, rows(full), :] = r.damp[1 + side, rows(full), :] / diagonal
    weights(known, nz - known)
    arrived(u_parts)
    for n in range(group):
        for side in range(2):
            _, total = strip_pull(r.su, r.scu, fine, n, side, full, 1)
            r.sres[n, side, rows(full), :] = total
    for to, of, slices in ((mid, fine, 2), (top, mid, 1)):
        for n in range(slices):
            for side in range(2):
                for one, two in (
                    (to.sc, of.sc), (to.sl, of.sl), (to.sr, of.sr), (to.sd, of.sd), (to.su, of.su),
                ):
                    one[n, side, rows(full), :] = two[2 * n, side, rows(full), :] + two[2 * n + 1, side, rows(full), :]
                diagonal = (of.sa[2 * n, side, rows(full), :] - 1.0) + of.sa[2 * n + 1, side, rows(full), :]
                to.sa[n, side, rows(full), :] = diagonal
                to.sg[n, side, rows(full), :] = r.damp[1 + side, rows(full), :] / diagonal
    coarser(known, nz - known)

    def first_update(part, wins):
        def body(p, carry):
            for n in range(group):
                for win in wins:
                    left = r.src[n, p, rows(win), :] + r.res[n, p, rows(win), :]
                    r.res[n, p, rows(win), :] = left
                    update = left * r.rd[n, p, rows(win), :]
                    r.e1[n + 1, p + 1, rows(win), :] = update
                    r.ce1[n, p + 1, rows(win), :] = r.c[n, p + 1, rows(win), :] * update
            return carry

        planes_loop(body, 0, *spans[part])

    def inner_update(part):
        first_update(part, [core])
        for number, (first, count) in enumerate(pieces[0]):
            if first + count == cuts[part + 1]:
                out_each(0, number, False, lambda copy: copy.start())
                out_copy(0, 0, number).start()

    def outer_update(part):
        edge_recv_wait(u_parts + part)
        first_update(part, [(pad - halo, halo), (pad + tx, halo)])
        packed = [r.packed_one[n, rows(full), :] if part else wide for n in range(group)]
        packed = pack_planes(r.e1, group, full, packed, *spans[part])
        for n in range(group):
            r.packed_one[n, rows(full), :] = packed[n]

    narrow = blank(trim[1])

    def pack_more(stage, ref, count, number):
        first, last = reach(number, stage)
        packed = [r.packs[stage - 1, n, rows(trim), :] if number else narrow for n in range(count)]
        packed = pack_planes(ref, count, trim, packed, first, last - first)
        if number < len(passes) - 1:
            for n in range(count):
                r.packs[stage - 1, n, rows(trim), :] = packed[n]
        return packed

    def again(number, stage, w, v, cv, sv, scv, b, sb, to_v, to_cv, to_sv, to_scv, count):
        first, last = reach(number, stage)
        ghost = [ghosts(sv, n + 1, trim) for n in range(count)]

        def body(p, carry):
            for n in range(count):
                value, total = pull(v, cv, w, n, ghost[n], p, trim, 1)
                left = b[n, p, rows(trim), :] + total
                update = value + left * w.d[n, p, rows(trim), :]
                to_v[n + 1, p + 1, rows(trim), :] = update
                to_cv[n, p + 1, rows(trim), :] = w.c[n, p + 1, rows(trim), :] * update
            return carry

        planes_loop(body, 0, first, last - first)
        packed = pack_more(stage, to_v, count, number)
        for n in range(count):
            for side in range(2):
                value, total = strip_pull(sv, scv, w, n, side, trim, 1)
                left = sb[n, side, rows(trim), :] + total
                update = value + left * w.sg[n, side, rows(trim), :]
                put_values(to_sv, to_scv, w, n, side, trim, update, packed[n], 1)

    def coarsen(number, stage, w, to, v, cv, sv, scv, b, sb, to_b, to_sb, to_v, to_cv, to_sv, to_scv, count):
        first, last = reach(number, stage)
        ghost = [ghosts(sv, n + 1, trim) for n in range(2 * count)]

        def body(p, carry):
            for n in range(count):
                rhs = None
                for m in (2 * n, 2 * n + 1):
                    _, total = pull(v, cv, w, m, ghost[m], p, trim, 1)
                    left = b[m, p, rows(trim), :] + total
                    rhs = left if rhs is None else rhs + left
                to_b[n, p, rows(trim), :] = rhs
                update = rhs * to.d[n, p, rows(trim), :]
                to_v[n + 1, p + 1, rows(trim), :] = update
                to_cv[n, p + 1, rows(trim), :] = to.c[n, p + 1, rows(trim), :] * update
            return carry

        planes_loop(body, 0, first, last - first)
        packed = pack_more(stage, to_v, count, number)
        for n in range(count):
            for side in range(2):
                rhs = None
                for m in (2 * n, 2 * n + 1):
                    _, total = strip_pull(sv, scv, w, m, side, trim, 1)
                    left = sb[m, side, rows(trim), :] + total
                    rhs = left if rhs is None else rhs + left
                to_sb[n, side, rows(trim), :] = rhs
                update = rhs * to.sg[n, side, rows(trim), :]
                put_values(to_sv, to_scv, to, n, side, trim, update, packed[n], 1)

    def run_pass(number):
        started, ended = number == 0, number == len(passes) - 1

        def meet(level):
            if ended:
                time_send(level)
            if started:
                time_wait(level)

        for n in range(group):
            for side in range(2):
                put_values(
                    r.se1, r.sce1, fine, n, side, full, r.sres[n, side, rows(full), :] * r.srd[n, side, rows(full), :],
                    r.packed_one[n, rows(full), :], 1,
                )
        meet(1)
        again(number, 1, fine, r.e1, r.ce1, r.se1, r.sce1, r.res, r.sres, r.e2, r.ce2, r.se2, r.sce2, group)
        meet(2)
        coarsen(
            number, 2, fine, mid, r.e2, r.ce2, r.se2, r.sce2, r.res, r.sres, r.mb, r.smb, r.me1, r.cme1, r.sme1,
            r.scme1, 2,
        )
        meet(3)
        again(number, 3, mid, r.me1, r.cme1, r.sme1, r.scme1, r.mb, r.smb, r.me2, r.cme2, r.sme2, r.scme2, 2)
        meet(4)
        coarsen(
            number, 4, mid, top, r.me2, r.cme2, r.sme2, r.scme2, r.mb, r.smb, r.tb, r.stb, r.te, r.cte, r.ste, r.scte,
            1,
        )
        meet(5)
        ghost = ghosts(r.ste, 1, core)

        def body(p, carry):
            value, total = pull(r.te, r.cte, top, 0, ghost, p, core, 1)
            update = value + (r.tb[0, p, real, :] + total) * r.trd[0, p, real, :]
            for n in range(group):
                middle = r.me2[n // 2 + 1, p + 1, real, :] + update
                r.new[n, p, real, :] = r.u[n + 1, p + 1, real, :] + (r.e2[n + 1, p + 1, real, :] + middle)
            return carry

        first, last = reach(number, stages)
        planes_loop(body, 0, first, last - first)
        out_each(1, number, False, lambda copy: copy.start())
        out_copy(1, 0, number).start()

    for n in range(group):
        for side in range(2):
            r.sres[n, side, rows(full), :] = (
                r.strip_in[n, side, 1, rows(full), :] + r.sres[n, side, rows(full), :]
            )
    for part in range(parts):
        if part:
            arrived(u_parts + part)
        inner_update(part)
        if part:
            outer_update(part - 1)
            if part in passes:
                run_pass(passes.index(part))
    outer_update(parts - 1)
    run_pass(len(passes) - 1)

    @pl.when(jnp.logical_not(has_before))
    def _():
        def clear_before(p, carry):
            for i in range(pair):
                r.before[p, :, i * width : (i + 1) * width] = nothing
            return carry

        lax.fori_loop(0, nz, clear_before, 0)

    @pl.when(has_before)
    def _():
        pltpu.make_async_remote_copy(
            src_ref=r.before, dst_ref=r.before, send_sem=r.before_sem.at[0], recv_sem=r.before_sem.at[1],
            device_id={"tm": me}, device_id_type=mesh_ids,
        ).wait_recv()

    far_real = pl.ds(halo, tx)
    bare = (halo, tx)

    def far_out(i):
        return pltpu.make_async_copy(
            r.far_res.at[i], r.res_out.at[0, 0, :, :, columns(far_block + i)], r.far_sem.at[2, i]
        )

    @pl.when(own_work)
    def _():
        for number in range(2):

            @pl.when(flanks[number][0])
            def _():
                row_copy(1 - number).wait_recv()

            for i in range(pair):
                value = r.row_in[number, 0, i]
                r.row_c[number, i] = (half * r.row_in[number, 1, i]) * (1.0 + value * value)
        for ref in (r.lu, r.lc):
            for k in range(pair + 3):
                for plane in (0, nz + 1):
                    ref[k, plane] = blank(tx + pad)

            def clear_outer(p, carry):
                for k in (0, pair + 2):
                    ref[k, p + 1, far_real, :] = nothing
                return carry

            lax.fori_loop(0, nz, clear_outer, 0)

        def far_coefficient(p, carry):
            for k in range(pair + 1):
                value = r.lu[1 + k, p + 1, far_real, :]
                r.lc[1 + k, p + 1, far_real, :] = (half * r.lkap[1 + k, p]) * (1.0 + value * value)
            for i in range(pair):
                k = far_block - near_block + i
                for number, row in enumerate((halo - 1, halo + tx)):
                    r.lu[1 + k, p + 1, pl.ds(row, 1), :] = r.row_in[number, 0, i, pl.ds(p, 1), :]
                    r.lc[1 + k, p + 1, pl.ds(row, 1), :] = r.row_c[number, i, pl.ds(p, 1), :]
            return carry

        lax.fori_loop(0, nz, far_coefficient, 0, unroll=2)
        first_tx, last_tx = lane_tx == 0, lane_tx == width - 1
        for i in range(pair):
            k = 1 + far_block - near_block + i
            own_columns = columns(far_block + i)

            def body(p, carry):
                def near_of(ref):
                    here = ref[k, p + 1, far_real, :]
                    before, after = ref[k - 1, p + 1, far_real, :], ref[k + 1, p + 1, far_real, :]
                    return here, (
                        jnp.where(first_tx, pltpu.roll(before, 1, 1), pltpu.roll(here, 1, 1)),
                        jnp.where(last_tx, pltpu.roll(after, width - 1, 1), pltpu.roll(here, width - 1, 1)),
                        ref[k, p + 1, pl.ds(halo - 1, tx), :], ref[k, p + 1, pl.ds(halo + 1, tx), :],
                        ref[k, p, far_real, :], ref[k, p + 2, far_real, :],
                    )

                value, value_near = near_of(r.lu)
                cc, c_near = near_of(r.lc)
                left = r.own[1, p, :, own_columns] - value + r.before[p, :, i * width : (i + 1) * width]
                for one, two in zip(value_near, c_near):
                    left = left - (cc + two) * (value - one)
                r.far_res[i, p] = left
                return carry

            lax.fori_loop(0, nz, body, 0, unroll=4)
            far_out(i).start()
        for i in range(pair):
            far_out(i).wait()
        for number in range(2):

            @pl.when(flanks[number][0])
            def _():
                row_copy(number).wait_send()

    @pl.when(has_after)
    def _():
        before_copy().wait_send()

    strip_each(False, lambda copy: copy.wait_send())
    for a in range(u_parts + parts):
        for j in order[:3]:
            in_copy(a, j).wait_send()
    for kind in range(u_parts + parts + 3):
        edge_send_wait(kind)
    if chained:

        @pl.when(has_next)
        def _():
            for number in range(len(time_refs)):
                for copy in time_copies(number):
                    copy.wait_send()

    for a in range(2):
        for part in range(len(pieces[a])):
            out_copy(a, 0, part).wait()
            out_each(a, part, False, lambda copy: copy.wait_send())
            out_each(a, part, True, lambda copy: copy.wait_recv())


def shards(tm_size, space_size, iterate, source_term, conductivity):
    _, nz, tx, ty = conductivity.shape
    width = ty // group
    tall = tx + 2 * pad
    f32 = jnp.float32
    dma = pltpu.SemaphoreType.DMA
    kinds = u_parts + parts + 3

    def padded(count):
        return pltpu.VMEM((count, nz + 2, tall, width), f32)

    def plain(*lead):
        return pltpu.VMEM((*lead, nz, tall, width), f32)

    def strip(*lead):
        return pltpu.VMEM((*lead, 2, tall, width), f32)

    scratch = {}
    scratch |= {name: padded(count) for name, count in (
        ("u", 5), ("c", 4), ("cu", 4), ("e1", 5), ("ce1", 4), ("e2", 5), ("ce2", 4), ("mc", 2), ("me1", 3),
        ("cme1", 2), ("me2", 3), ("cme2", 2), ("tc", 1), ("te", 2), ("cte", 1),
    )}
    scratch |= {name: plain(count) for name, count in (
        ("src", 4), ("res", 4), ("wl", 4), ("wr", 4), ("wa", 4), ("rd", 4), ("mwl", 2), ("mwr", 2), ("mwa", 2),
        ("mrd", 2), ("mb", 2), ("twl", 1), ("twr", 1), ("twa", 1), ("trd", 1), ("tb", 1), ("new", 4),
    )}
    scratch["kap"] = plain()
    scratch |= {name: strip(count) for name, count in (
        ("su", 5), ("sc", 4), ("scu", 4), ("se1", 5), ("sce1", 4), ("se2", 5), ("sce2", 4), ("smc", 2),
        ("sme1", 3), ("scme1", 2), ("sme2", 3), ("scme2", 2), ("stc", 1), ("ste", 2), ("scte", 1),
        ("swl", 4), ("swr", 4), ("swd", 4), ("swu", 4), ("swa", 4), ("srd", 4), ("sres", 4),
        ("smwl", 2), ("smwr", 2), ("smwd", 2), ("smwu", 2), ("smwa", 2), ("smrd", 2), ("smb", 2),
        ("stwl", 1), ("stwr", 1), ("stwd", 1), ("stwu", 1), ("stwa", 1), ("strd", 1), ("stb", 1),
    )}
    scratch["kap_strip"] = strip()
    scratch["strip_in"] = strip(group, 2)
    scratch["strip_send"] = pltpu.VMEM((group, 2, 2, tx, width), f32)
    scratch["own"] = pltpu.VMEM((2, nz, tx, ty), f32)
    scratch["beside"] = pltpu.VMEM((2, nz, tx, width), f32)
    pair = group // 2
    scratch["lu"] = pltpu.VMEM((pair + 3, nz + 2, tx + pad, width), f32)
    scratch["lc"] = pltpu.VMEM((pair + 3, nz + 2, tx + pad, width), f32)
    scratch["lkap"] = pltpu.VMEM((pair + 2, nz, tx, width), f32)
    scratch["before"] = pltpu.VMEM((nz, tx, pair * width), f32)
    scratch["far_res"] = pltpu.VMEM((pair, nz, tx, width), f32)
    scratch["row_send"] = pltpu.VMEM((2, 2, pair, nz, width), f32)
    scratch["row_in"] = pltpu.VMEM((2, 2, pair, nz, width), f32)
    scratch["row_c"] = pltpu.VMEM((2, pair, nz, width), f32)
    scratch["packs"] = pltpu.VMEM((stages - 1, group, tall, width), f32)
    scratch["packed_one"] = pltpu.VMEM((group, tall, width), f32)
    scratch["damp"] = pltpu.VMEM((3, tall, width), f32)
    for name, shape in (
        ("loc_sem", (5,)), ("in_lsem", (u_parts + parts,)), ("in_ssem", (u_parts + parts, group - 1)),
        ("in_rsem", (u_parts + parts, group - 1)), ("out_lsem", (2, len(passes) + 1)), ("out_ssem", (2, len(passes) + 1, group - 1)),
        ("out_rsem", (2, len(passes) + 1, group - 1)), ("strip_ssem", (group - 1, 2)), ("strip_rsem", (group - 1, 2)),
        ("edge_ssem", (kinds, 2)), ("edge_rsem", (kinds, 2)), ("time_ssem", (6, 2)), ("far_sem", (3, pair + 1)),
        ("before_sem", (2,)), ("row_sem", (2, 2)),
        ("time_rsem", (6, 2)),
    ):
        scratch[name] = dma(shape)
    names = ("state_in", "source_in", "kappa_in", "new_out", "res_out", *scratch)
    out = jax.ShapeDtypeStruct(iterate.shape, f32)
    hbm = pl.BlockSpec(memory_space=pltpu.HBM)
    return pl.pallas_call(
        functools.partial(kernel, tm_size, space_size, names),
        out_shape=(out, out),
        in_specs=[hbm] * 3,
        out_specs=(hbm, hbm),
        scratch_shapes=list(scratch.values()),
        compiler_params=pltpu.CompilerParams(
            collective_id=0, has_side_effects=True, vmem_limit_bytes=67043328
        ),
    )(iterate, source_term, conductivity)


def solution(mesh):
    tiled = P("tm", "space", None, None, None)
    in_specs = (tiled, tiled, P("space", None, None, None))
    body = functools.partial(shards, mesh.shape["tm"], mesh.shape["space"])
    return jax.shard_map(
        body, mesh=mesh, in_specs=in_specs, out_specs=(tiled, tiled), check_vma=False
    )
```

```python
import functools
import types

import jax
import jax.numpy as jnp
from jax import lax
from jax.experimental import pallas as pl
from jax.experimental.pallas import tpu as pltpu
from jax.sharding import PartitionSpec as P

tau_step = 0.08
damping = 0.7
group = 4
halo = 8
pad = 2 * halo
u_parts = 2
shares = (6, 6, 4)
parts = len(shares)
passes = (1, 2, 3)
stages = 5
mesh_ids = pl.DeviceIdType.MESH
order = (2, 1, 3, 0)
unroll = 8


def kernel(tm_size, space_size, names, *refs):
    r = types.SimpleNamespace(**dict(zip(names, refs)))
    _, nz, tx, _ = r.kappa_in.shape
    width = r.kap.shape[-1]
    span = width // nz
    chained = tm_size > group
    half = 0.5 * tau_step
    u_piece = nz // u_parts
    cuts = [nz * sum(shares[:k]) // sum(shares) for k in range(parts + 1)]
    spans = [(cuts[k], cuts[k + 1] - cuts[k]) for k in range(parts)]

    def reach(number, stage):
        bounds = [0] + [cuts[known] - stage if known < parts else nz for known in passes]
        return max(bounds[number], 0), bounds[number + 1]

    pieces = [[(0, cuts[-2]), spans[-1]], []]
    for number in range(len(passes)):
        first, last = reach(number, stages)
        pieces[1].append((first, last - first))

    full = (pad - halo, tx + 2 * halo)
    trim = (pad - halo // 2, tx + halo)
    core = (pad, tx)

    def rows(win, shift=0):
        return pl.ds(win[0] + shift, win[1])

    real = rows(core)
    planes = pl.ds(1, nz)
    me = lax.axis_index("tm")
    sp = lax.axis_index("space")
    q = me % group
    base = me - q
    has_dn, has_up = sp > 0, sp < space_size - 1
    has_left, has_right = q > 0, q < group - 1
    has_prev, has_next = base > 0, base + group < tm_size
    pair = group // 2
    lower = q < pair
    own_work = q != pair
    far_block = jnp.where(lower, pair, 0)
    near_block = jnp.where(lower, pair - 1, 0)
    has_before = jnp.logical_and(own_work, me > 0)
    has_after = jnp.logical_and(q != pair - 1, me + 1 < tm_size)
    flanks = [(has_dn, {"space": sp - 1}), (has_up, {"space": sp + 1})]
    beside_has = [has_left, has_right]

    def columns(d):
        return pl.ds(pl.multiple_of(d * width, width), width)

    own_copies = [
        pltpu.make_async_copy(hbm.at[0, 0], r.own.at[f], r.loc_sem.at[f])
        for f, hbm in enumerate((r.state_in, r.source_in))
    ]
    kappa_copy = pltpu.make_async_copy(
        r.kappa_in.at[0, :, :, columns(q)], r.kap.at[:, real, :], r.loc_sem.at[2]
    )

    def beside_copy(side):
        block = r.kappa_in.at[0, :, :, columns(q - 1 + 2 * side)]
        return pltpu.make_async_copy(block, r.beside.at[side], r.loc_sem.at[3 + side])

    own_copies[0].start()
    kappa_copy.start()
    for side in range(2):

        @pl.when(beside_has[side])
        def _():
            beside_copy(side).start()

    own_copies[1].start()

    def wide_columns(first, count):
        return pl.ds(pl.multiple_of(first * width, width), count * width)

    def far_copies():
        made = []
        for k in range(pair + 1):
            made.append(
                pltpu.make_async_copy(
                    r.state_in.at[0, 0, :, :, columns(near_block + k)],
                    r.lu.at[1 + k, pl.ds(1, nz), pl.ds(halo, tx), :], r.far_sem.at[0, k],
                )
            )
            made.append(
                pltpu.make_async_copy(
                    r.kappa_in.at[0, :, :, columns(near_block + k)], r.lkap.at[1 + k], r.far_sem.at[1, k]
                )
            )
        return made

    @pl.when(own_work)
    def _():
        for copy in far_copies():
            copy.start()

    def before_copy():
        first = jnp.where((q + 1) % group < pair, pair, 0)
        return pltpu.make_async_remote_copy(
            src_ref=r.state_in.at[0, 0, :, :, wide_columns(first, pair)], dst_ref=r.before,
            send_sem=r.before_sem.at[0], recv_sem=r.before_sem.at[1], device_id={"tm": me + 1},
            device_id_type=mesh_ids,
        )

    def row_copy(number):
        return pltpu.make_async_remote_copy(
            src_ref=r.row_send.at[number], dst_ref=r.row_in.at[1 - number],
            send_sem=r.row_sem.at[0, number], recv_sem=r.row_sem.at[1, 1 - number],
            device_id=flanks[number][1], device_id_type=mesh_ids,
        )

    barrier = pltpu.get_barrier_semaphore()
    for j in range(1, group):
        pl.semaphore_signal(
            barrier, inc=1, device_id={"tm": base + (q + j) % group}, device_id_type=mesh_ids
        )
    greeted = list(flanks)
    if chained:
        greeted += [(has_prev, {"tm": me - group}), (has_next, {"tm": me + group})]
        greeted += [(jnp.logical_and(has_prev, q == 0), {"tm": me - 1})]
        greeted += [(jnp.logical_and(has_next, q == group - 1), {"tm": me + 1})]
    for has, where in greeted:

        @pl.when(has)
        def _():
            pl.semaphore_signal(barrier, inc=1, device_id=where, device_id_type=mesh_ids)

    expected = group - 1
    for has, _ in greeted:
        expected = expected + jnp.where(has, 1, 0)
    pl.semaphore_wait(barrier, expected)

    def in_copy(a, j):
        d = (q + j) % group
        if a < u_parts:
            some = pl.ds(a * u_piece, u_piece)
            hbm = r.state_in.at[0, 0, some, :, columns(d)]
            dst = r.u.at[q + 1, pl.ds(1 + a * u_piece, u_piece), real, :]
        else:
            some = pl.ds(*spans[a - u_parts])
            hbm, dst = r.source_in.at[0, 0, some, :, columns(d)], r.src.at[q, some, real, :]
        if j == 0:
            return pltpu.make_async_copy(hbm, dst, r.in_lsem.at[a])
        return pltpu.make_async_remote_copy(
            src_ref=hbm, dst_ref=dst, send_sem=r.in_ssem.at[a, j - 1],
            recv_sem=r.in_rsem.at[a, j - 1], device_id={"tm": base + d}, device_id_type=mesh_ids,
        )

    def out_copy(a, j, part):
        d = (q + j) % group
        some = pl.ds(*pieces[a][part])
        hbm = (r.res_out, r.new_out)[a].at[0, 0, some, :, columns(q)]
        held = (r.res, r.new)[a].at[d, some, real, :]
        if j == 0:
            return pltpu.make_async_copy(held, hbm, r.out_lsem.at[a, part])
        return pltpu.make_async_remote_copy(
            src_ref=held, dst_ref=hbm, send_sem=r.out_ssem.at[a, part, j - 1],
            recv_sem=r.out_rsem.at[a, part, j - 1], device_id={"tm": base + d},
            device_id_type=mesh_ids,
        )

    def out_each(a, part, receiving, act):
        for j in order[:3]:
            one, two = ((q - j) % group, q) if receiving else (q, (q + j) % group)
            if a == 0:
                wanted = jnp.logical_or(one // pair == two // pair, jnp.logical_and(two == pair, one < pair))

                @pl.when(wanted)
                def _():
                    act(out_copy(a, j, part))
            else:
                act(out_copy(a, j, part))

    def strip_copy(j, side):
        d = (q + j) % group
        return pltpu.make_async_remote_copy(
            src_ref=r.strip_send.at[d, side], dst_ref=r.strip_in.at[q, side, :, real, :],
            send_sem=r.strip_ssem.at[j - 1, side], recv_sem=r.strip_rsem.at[j - 1, side],
            device_id={"tm": base + d}, device_id_type=mesh_ids,
        )

    def strip_each(receiving, act):
        for j in order[:3]:
            d = q if receiving else (q + j) % group
            for side, has in enumerate((d > 0, d < group - 1)):

                @pl.when(has)
                def _():
                    act(strip_copy(j, side))


    strip_kind = u_parts + parts
    kappa_kind, kappa_strip_kind = strip_kind + 1, strip_kind + 2

    def edge_ref(kind, where):
        if kind < u_parts:
            return r.u.at[pl.ds(1, group), pl.ds(1 + kind * u_piece, u_piece), where, :]
        if kind < strip_kind:
            return r.src.at[:, pl.ds(*spans[kind - u_parts]), where, :]
        if kind == strip_kind:
            return r.strip_in.at[:, :, :, where, :]
        if kind == kappa_kind:
            return r.kap.at[:, where, :]
        return r.kap_strip.at[:, where, :]

    def edge_copy(kind, number):
        if number == 0:
            source, target = pl.ds(pad, halo), pl.ds(pad + tx, halo)
        else:
            source, target = pl.ds(pad + tx - halo, halo), pl.ds(pad - halo, halo)
        return pltpu.make_async_remote_copy(
            src_ref=edge_ref(kind, source), dst_ref=edge_ref(kind, target),
            send_sem=r.edge_ssem.at[kind, number], recv_sem=r.edge_rsem.at[kind, number],
            device_id=flanks[number][1], device_id_type=mesh_ids,
        )

    def edge_start(kind):
        for number in range(2):

            @pl.when(flanks[number][0])
            def _():
                edge_copy(kind, number).start()

    def edge_send_wait(kind):
        for number in range(2):

            @pl.when(flanks[number][0])
            def _():
                edge_copy(kind, number).wait_send()

    def edge_recv_wait(kind):
        for number in range(2):

            @pl.when(flanks[number][0])
            def _():
                edge_copy(kind, 1 - number).wait_recv()

    time_refs = [(r.u, group), (r.e1, group), (r.e2, group), (r.me1, 2), (r.me2, 2), (r.te, 1)]
    time_strips = [
        (r.su, group), (r.se1, group), (r.se2, group), (r.sme1, 2), (r.sme2, 2), (r.ste, 1),
    ]

    def time_copies(number):
        made = []
        for kind, (ref, last) in enumerate((time_refs[number], time_strips[number])):
            middle = planes if kind == 0 else pl.ds(0, 2)
            made.append(
                pltpu.make_async_remote_copy(
                    src_ref=ref.at[last, middle, rows(full), :],
                    dst_ref=ref.at[0, middle, rows(full), :],
                    send_sem=r.time_ssem.at[number, kind], recv_sem=r.time_rsem.at[number, kind],
                    device_id={"tm": me + group}, device_id_type=mesh_ids,
                )
            )
        return made

    def time_send(number):
        if chained:

            @pl.when(has_next)
            def _():
                for copy in time_copies(number):
                    copy.start()

    def time_wait(number):
        if chained:

            @pl.when(has_prev)
            def _():
                for copy in time_copies(number):
                    copy.wait_recv()

    for j in order:
        in_copy(0, j).start()
    kappa_copy.wait()
    edge_start(kappa_kind)

    f32 = jnp.float32
    tall = r.u.shape[2]

    def blank(count):
        return jnp.zeros((count, width), f32)

    for side in range(2):

        @pl.when(jnp.logical_not(beside_has[side]))
        def _():
            def clear_beside(p, carry):
                r.beside[side, p] = blank(tx)
                return carry

            lax.fori_loop(0, nz, clear_beside, 0)
            for n in range(group):
                for f in range(2):
                    r.strip_in[n, side, f, real, :] = blank(tx)

    lane_tx = lax.broadcasted_iota(jnp.int32, (tx, width), 1)
    lane = lax.broadcasted_iota(jnp.int32, (tx + 2 * halo, width), 1)

    def plane_of(side, lanes):
        return ((lanes + (span // 2, 0)[side]) % width) // span

    inside = [plane_of(side, lane_tx) for side in range(2)]

    def put_strip(packed, side, block, p):
        return jnp.where(inside[side] == p, pltpu.roll(block, span * p + 2, 1), packed)

    nothing = blank(tx)

    def pack_own(f):
        def body(p, packed):
            blocks = [r.own[f, p, :, d * width : (d + 1) * width] for d in range(group)]
            made = []
            for d in range(group):
                left, right = packed[2 * d], packed[2 * d + 1]
                turned_left = blocks[d - 1] if d else None
                turned_right = blocks[d + 1] if d < group - 1 else None
                made.append(left if turned_left is None else put_strip(left, 0, turned_left, p))
                made.append(right if turned_right is None else put_strip(right, 1, turned_right, p))
            return tuple(made)

        packed = lax.fori_loop(0, nz, body, (nothing,) * (2 * group), unroll=2)
        for d in range(group):
            for side in range(2):
                r.strip_send[d, side, f] = packed[2 * d + side]
        for side in range(2):
            r.strip_in[q, side, f, real, :] = r.strip_send[q, side, f]

    for f in range(2):
        own_copies[f].wait()
        pack_own(f)
    strip_each(False, lambda copy: copy.start())
    for a in range(1, u_parts + parts):
        for j in order:
            in_copy(a, j).start()

    @pl.when(has_after)
    def _():
        before_copy().start()

    @pl.when(own_work)
    def _():
        for copy in far_copies():
            copy.wait()

        def far_rows(p, carry):
            for i in range(pair):
                k = far_block - near_block + i
                for number, row in enumerate((0, tx - 1)):
                    r.row_send[number, 0, i, pl.ds(p, 1), :] = r.lu[1 + k, p + 1, pl.ds(halo + row, 1), :]
                    r.row_send[number, 1, i, pl.ds(p, 1), :] = r.lkap[1 + k, p, pl.ds(row, 1), :]
            return carry

        lax.fori_loop(0, nz, far_rows, 0, unroll=4)
        for number in range(2):

            @pl.when(flanks[number][0])
            def _():
                row_copy(number).start()

            @pl.when(jnp.logical_not(flanks[number][0]))
            def _():
                for f in range(2):
                    for i in range(pair):
                        r.row_in[number, f, i] = blank(nz)

    held = [(ref, 1) for ref, _ in time_refs]
    held += [(ref, 0) for ref in (r.c, r.cu, r.ce1, r.ce2, r.mc, r.cme1, r.cme2, r.tc, r.cte)]
    early = (r.u, r.c, r.cu, r.e1, r.ce1)
    for ref, first in held:
        for n in range(first, ref.shape[0]):
            for plane in (0, nz + 1):
                ref[n, plane] = blank(tall)

    def clear_rows(p, carry):
        for ref, first in held:
            outer = any(ref is one for one in early)
            low, high = (0, tall - halo) if outer else (halo, tall - pad)
            for n in range(first, ref.shape[0]):
                ref[n, p + 1, pl.ds(low, halo), :] = blank(halo)
                ref[n, p + 1, pl.ds(high, halo), :] = blank(halo)
        return carry

    lax.fori_loop(0, nz, clear_rows, 0)
    strips = [(ref, 1) for ref, _ in time_strips]
    strips += [(ref, 0) for ref in (r.sc, r.scu, r.sce1, r.sce2, r.smc, r.scme1, r.scme2, r.stc, r.scte)]
    for ref, first in strips:
        for n in range(first, ref.shape[0]):
            for side in range(2):
                ref[n, side] = blank(tall)
    if chained:

        @pl.when(jnp.logical_not(has_prev))
        def _():
            def clear_first(p, carry):
                for ref, _ in time_refs:
                    ref[0, p + 1] = blank(tall)
                return carry

            lax.fori_loop(0, nz, clear_first, 0)
            for ref, _ in time_strips:
                for side in range(2):
                    ref[0, side] = blank(tall)

    for number, (has, _) in enumerate(flanks):
        edge = pl.ds((pad - halo, pad + tx)[number], halo)

        @pl.when(jnp.logical_not(has))
        def _():
            def clear_edges(p, carry):
                r.kap[p, edge, :] = blank(halo)
                for n in range(group):
                    r.u[n + 1, p + 1, edge, :] = blank(halo)
                    r.src[n, p, edge, :] = blank(halo)
                return carry

            lax.fori_loop(0, nz, clear_edges, 0)
            for side in range(2):
                r.kap_strip[side, edge, :] = blank(halo)
                for f in range(2):
                    for n in range(group):
                        r.strip_in[n, side, f, edge, :] = blank(halo)

    for side in range(2):

        @pl.when(beside_has[side])
        def _():
            beside_copy(side).wait()

    def kappa_body(p, packed):
        return tuple(put_strip(packed[side], side, r.beside[side, p], p) for side in range(2))

    packed = lax.fori_loop(0, nz, kappa_body, (nothing, nothing), unroll=2)
    for side in range(2):
        r.kap_strip[side, real, :] = packed[side]
    edge_start(kappa_strip_kind)

    level = lax.broadcasted_iota(jnp.int32, (tx + 2 * halo, width), 0)
    below = jnp.where(has_dn, damping, 0.0)
    above = jnp.where(has_up, damping, 0.0)
    damp = jnp.where(level < halo, below, jnp.where(level < halo + tx, damping, above))
    r.damp[0, rows(full), :] = damp
    for side in range(2):
        r.damp[1 + side, rows(full), :] = damp * jnp.where(beside_has[side], 1.0, 0.0)

    first_plane = [plane_of(side, lane) == 0 for side in range(2)]
    last_plane = [plane_of(side, lane) == nz - 1 for side in range(2)]
    inject = [lane % span == 2, lane % span == 1]
    plane_lane = lane // span
    first_lane = lane == 0
    last_lane = lane == width - 1

    def cut(mask, win):
        return mask[: win[1]]

    def pack(packed, value, p, win):
        return jnp.where(cut(plane_lane, win) == p, pltpu.roll(value, span * p + 2, 1), packed)

    def pack_planes(ref, count, win, packed, first=0, planes_count=None):
        def body(p, packed):
            return tuple(pack(packed[n], ref[n + 1, p + 1, rows(win), :], p, win) for n in range(count))

        return planes_loop(body, tuple(packed), first, planes_count)

    def ghosts(ref, n, win):
        left = pltpu.roll(ref[n, 0, rows(win), :], 1, 1)
        right = pltpu.roll(ref[n, 1, rows(win), :], width - 1, 1)
        return jnp.where(cut(inject[0], win), left, right)

    def sideways(value, ghost, p, win):
        edge = pltpu.roll(ghost, width - 2 - span * p, 1)
        left = jnp.where(cut(first_lane, win), edge, pltpu.roll(value, 1, 1))
        right = jnp.where(cut(last_lane, win), edge, pltpu.roll(value, width - 1, 1))
        return left, right

    def across(ref, n, p, win):
        return (
            (ref[n, p + 1, rows(win, -1), :] + ref[n, p + 1, rows(win, 1), :])
            + (ref[n, p, rows(win), :] + ref[n, p + 2, rows(win), :])
        )

    def planes_loop(body, init, first=0, count=None):
        count = nz if count is None else count
        return lax.fori_loop(first, first + count, body, init, unroll=min(unroll, count))

    def earlier(ref, n, middle, win):
        if n == 0 and not chained:
            return None
        return ref[n, middle, rows(win), :]

    def pull(v_ref, cv_ref, w, n, ghost, p, win, first):
        v = v_ref[first + n, p + 1, rows(win), :]
        left, right = sideways(v, ghost, p, win)
        total = w.l[n, p, rows(win), :] * left + w.r[n, p, rows(win), :] * right
        total = total + w.c[n, p + 1, rows(win), :] * across(v_ref, first + n, p, win)
        total = total + across(cv_ref, n, p, win)
        before = earlier(v_ref, n, p + 1, win)
        if before is not None:
            total = total + before
        return v, total - w.a[n, p, rows(win), :] * v

    def strip_pull(v_ref, cv_ref, w, n, side, win, first):
        v = v_ref[first + n, side, rows(win), :]
        total = w.sl[n, side, rows(win), :] * pltpu.roll(v, 1, 1)
        total = total + w.sr[n, side, rows(win), :] * pltpu.roll(v, width - 1, 1)
        total = total + w.sd[n, side, rows(win), :] * pltpu.roll(v, span, 1)
        total = total + w.su[n, side, rows(win), :] * pltpu.roll(v, width - span, 1)
        beside = v_ref[first + n, side, rows(win, -1), :] + v_ref[first + n, side, rows(win, 1), :]
        total = total + w.sc[n, side, rows(win), :] * beside
        total = total + (cv_ref[n, side, rows(win, -1), :] + cv_ref[n, side, rows(win, 1), :])
        before = earlier(v_ref, n, side, win)
        if before is not None:
            total = total + before
        return v, total - w.sa[n, side, rows(win), :] * v

    def put_values(v_ref, cv_ref, w, n, side, win, value, packed, first):
        value = jnp.where(cut(inject[side], win), packed, value)
        v_ref[first + n, side, rows(win), :] = value
        cv_ref[n, side, rows(win), :] = w.sc[n, side, rows(win), :] * value

    fine = types.SimpleNamespace(
        l=r.wl, r=r.wr, a=r.wa, c=r.c, d=r.rd, sl=r.swl, sr=r.swr, sd=r.swd, su=r.swu, sa=r.swa, sc=r.sc, sg=r.srd
    )
    mid = types.SimpleNamespace(
        l=r.mwl, r=r.mwr, a=r.mwa, c=r.mc, d=r.mrd, sl=r.smwl, sr=r.smwr, sd=r.smwd, su=r.smwu, sa=r.smwa,
        sc=r.smc, sg=r.smrd,
    )
    top = types.SimpleNamespace(
        l=r.twl, r=r.twr, a=r.twa, c=r.tc, d=r.trd, sl=r.stwl, sr=r.stwr, sd=r.stwd, su=r.stwu, sa=r.stwa,
        sc=r.stc, sg=r.strd,
    )

    wide = blank(full[1])
    edge_recv_wait(kappa_kind)
    edge_recv_wait(kappa_strip_kind)
    kappa_edge = planes_loop(lambda p, packed: pack(packed, r.kap[p, rows(full), :], p, full), wide)

    def arrived(a):
        in_copy(a, 0).wait()
        for j in order[:3]:
            in_copy(a, j).wait_recv()
        edge_start(a)

    def coefficients(p, carry):
        scaled = half * r.kap[p, rows(full), :]
        for n in range(group):
            v = r.u[n + 1, p + 1, rows(full), :]
            cc = scaled * (1.0 + v * v)
            r.c[n, p + 1, rows(full), :] = cc
            r.cu[n, p + 1, rows(full), :] = cc * v
        return carry

    def strip_coefficients(packed):
        for n in range(group):
            for side in range(2):
                v = jnp.where(inject[side], packed[n], r.strip_in[n, side, 0, rows(full), :])
                kk = jnp.where(inject[side], kappa_edge, r.kap_strip[side, rows(full), :])
                cc = (half * kk) * (1.0 + v * v)
                r.su[n + 1, side, rows(full), :] = v
                r.sc[n, side, rows(full), :] = cc
                r.scu[n, side, rows(full), :] = cc * v

    def weights(first, count):
        for n in range(group):
            ghost_c, ghost_u = ghosts(r.sc, n, full), ghosts(r.su, n + 1, full)

            def body(p, carry):
                cc = r.c[n, p + 1, rows(full), :]
                left, right = sideways(cc, ghost_c, p, full)
                left, right = cc + left, cc + right
                r.wl[n, p, rows(full), :] = left
                r.wr[n, p, rows(full), :] = right
                diagonal = 1.0 + ((4.0 * cc + left) + (right + across(r.c, n, p, full)))
                r.wa[n, p, rows(full), :] = diagonal
                r.rd[n, p, rows(full), :] = r.damp[0, rows(full), :] / diagonal
                _, total = pull(r.u, r.cu, fine, n, ghost_u, p, full, 1)
                r.res[n, p, rows(full), :] = total
                return carry

            planes_loop(body, 0, first, count)

    def coarser(first, count):
        for to, of, slices in ((mid, fine, 2), (top, mid, 1)):

            def body(p, carry):
                for n in range(slices):
                    to.c[n, p + 1, rows(full), :] = of.c[2 * n, p + 1, rows(full), :] + of.c[2 * n + 1, p + 1, rows(full), :]
                    for one, two in ((to.l, of.l), (to.r, of.r)):
                        one[n, p, rows(full), :] = two[2 * n, p, rows(full), :] + two[2 * n + 1, p, rows(full), :]
                    diagonal = (of.a[2 * n, p, rows(full), :] - 1.0) + of.a[2 * n + 1, p, rows(full), :]
                    to.a[n, p, rows(full), :] = diagonal
                    to.d[n, p, rows(full), :] = r.damp[0, rows(full), :] / diagonal
                return carry

            lax.fori_loop(first, first + count, body, 0, unroll=min(4, count))

    arrived(0)
    strip_each(True, lambda copy: copy.wait_recv())
    edge_start(strip_kind)
    edge_recv_wait(0)
    edge_recv_wait(strip_kind)
    strip_coefficients((wide,) * group)
    lax.fori_loop(0, u_piece, coefficients, 0, unroll=4)
    time_wait(0)
    known = u_piece - 1
    weights(0, known)
    for a in range(1, u_parts):
        arrived(a)
    coarser(0, known)
    packed_u = pack_planes(r.u, group, full, (wide,) * group, 0, u_piece)
    for a in range(1, u_parts):
        edge_recv_wait(a)
    lax.fori_loop(u_piece, nz, coefficients, 0, unroll=4)
    packed_u = pack_planes(r.u, group, full, packed_u, u_piece, nz - u_piece)
    strip_coefficients(packed_u)
    time_send(0)
    for n in range(group):
        for side in range(2):
            cc = r.sc[n, side, rows(full), :]
            total = r.sc[n, side, rows(full, -1), :] + r.sc[n, side, rows(full, 1), :]
            for ref, shift, off in (
                (r.swl, 1, None), (r.swr, width - 1, None),
                (r.swd, span, first_plane[side]), (r.swu, width - span, last_plane[side]),
            ):
                beside = pltpu.roll(cc, shift, 1)
                weight = cc + beside
                if off is not None:
                    beside, weight = jnp.where(off, 0.0, beside), jnp.where(off, 0.0, weight)
                ref[n, side, rows(full), :] = weight
                total = total + beside
            diagonal = 1.0 + (6.0 * cc + total)
            r.swa[n, side, rows(full), :] = diagonal
            r.srd[n, side, rows(full), :] = r.damp[1 + side, rows(full), :] / diagonal
    weights(known, nz - known)
    arrived(u_parts)
    for n in range(group):
        for side in range(2):
            _, total = strip_pull(r.su, r.scu, fine, n, side, full, 1)
            r.sres[n, side, rows(full), :] = total
    for to, of, slices in ((mid, fine, 2), (top, mid, 1)):
        for n in range(slices):
            for side in range(2):
                for one, two in (
                    (to.sc, of.sc), (to.sl, of.sl), (to.sr, of.sr), (to.sd, of.sd), (to.su, of.su),
                ):
                    one[n, side, rows(full), :] = two[2 * n, side, rows(full), :] + two[2 * n + 1, side, rows(full), :]
                diagonal = (of.sa[2 * n, side, rows(full), :] - 1.0) + of.sa[2 * n + 1, side, rows(full), :]
                to.sa[n, side, rows(full), :] = diagonal
                to.sg[n, side, rows(full), :] = r.damp[1 + side, rows(full), :] / diagonal
    coarser(known, nz - known)

    def first_update(part, wins):
        def body(p, carry):
            for n in range(group):
                for win in wins:
                    left = r.src[n, p, rows(win), :] + r.res[n, p, rows(win), :]
                    r.res[n, p, rows(win), :] = left
                    update = left * r.rd[n, p, rows(win), :]
                    r.e1[n + 1, p + 1, rows(win), :] = update
                    r.ce1[n, p + 1, rows(win), :] = r.c[n, p + 1, rows(win), :] * update
            return carry

        planes_loop(body, 0, *spans[part])

    def inner_update(part):
        first_update(part, [core])
        for number, (first, count) in enumerate(pieces[0]):
            if first + count == cuts[part + 1]:
                out_each(0, number, False, lambda copy: copy.start())
                out_copy(0, 0, number).start()

    def outer_update(part):
        edge_recv_wait(u_parts + part)
        first_update(part, [(pad - halo, halo), (pad + tx, halo)])
        packed = [r.packed_one[n, rows(full), :] if part else wide for n in range(group)]
        packed = pack_planes(r.e1, group, full, packed, *spans[part])
        for n in range(group):
            r.packed_one[n, rows(full), :] = packed[n]

    narrow = blank(trim[1])

    def pack_more(stage, ref, count, number):
        first, last = reach(number, stage)
        packed = [r.packs[stage - 1, n, rows(trim), :] if number else narrow for n in range(count)]
        packed = pack_planes(ref, count, trim, packed, first, last - first)
        if number < len(passes) - 1:
            for n in range(count):
                r.packs[stage - 1, n, rows(trim), :] = packed[n]
        return packed

    def again(number, stage, w, v, cv, sv, scv, b, sb, to_v, to_cv, to_sv, to_scv, count):
        first, last = reach(number, stage)
        ghost = [ghosts(sv, n + 1, trim) for n in range(count)]

        def body(p, carry):
            for n in range(count):
                value, total = pull(v, cv, w, n, ghost[n], p, trim, 1)
                left = b[n, p, rows(trim), :] + total
                update = value + left * w.d[n, p, rows(trim), :]
                to_v[n + 1, p + 1, rows(trim), :] = update
                to_cv[n, p + 1, rows(trim), :] = w.c[n, p + 1, rows(trim), :] * update
            return carry

        planes_loop(body, 0, first, last - first)
        packed = pack_more(stage, to_v, count, number)
        for n in range(count):
            for side in range(2):
                value, total = strip_pull(sv, scv, w, n, side, trim, 1)
                left = sb[n, side, rows(trim), :] + total
                update = value + left * w.sg[n, side, rows(trim), :]
                put_values(to_sv, to_scv, w, n, side, trim, update, packed[n], 1)

    def coarsen(number, stage, w, to, v, cv, sv, scv, b, sb, to_b, to_sb, to_v, to_cv, to_sv, to_scv, count):
        first, last = reach(number, stage)
        ghost = [ghosts(sv, n + 1, trim) for n in range(2 * count)]

        def body(p, carry):
            for n in range(count):
                rhs = None
                for m in (2 * n, 2 * n + 1):
                    _, total = pull(v, cv, w, m, ghost[m], p, trim, 1)
                    left = b[m, p, rows(trim), :] + total
                    rhs = left if rhs is None else rhs + left
                to_b[n, p, rows(trim), :] = rhs
                update = rhs * to.d[n, p, rows(trim), :]
                to_v[n + 1, p + 1, rows(trim), :] = update
                to_cv[n, p + 1, rows(trim), :] = to.c[n, p + 1, rows(trim), :] * update
            return carry

        planes_loop(body, 0, first, last - first)
        packed = pack_more(stage, to_v, count, number)
        for n in range(count):
            for side in range(2):
                rhs = None
                for m in (2 * n, 2 * n + 1):
                    _, total = strip_pull(sv, scv, w, m, side, trim, 1)
                    left = sb[m, side, rows(trim), :] + total
                    rhs = left if rhs is None else rhs + left
                to_sb[n, side, rows(trim), :] = rhs
                update = rhs * to.sg[n, side, rows(trim), :]
                put_values(to_sv, to_scv, to, n, side, trim, update, packed[n], 1)

    def run_pass(number):
        started, ended = number == 0, number == len(passes) - 1

        def meet(level):
            if ended:
                time_send(level)
            if started:
                time_wait(level)

        for n in range(group):
            for side in range(2):
                put_values(
                    r.se1, r.sce1, fine, n, side, full, r.sres[n, side, rows(full), :] * r.srd[n, side, rows(full), :],
                    r.packed_one[n, rows(full), :], 1,
                )
        meet(1)
        again(number, 1, fine, r.e1, r.ce1, r.se1, r.sce1, r.res, r.sres, r.e2, r.ce2, r.se2, r.sce2, group)
        meet(2)
        coarsen(
            number, 2, fine, mid, r.e2, r.ce2, r.se2, r.sce2, r.res, r.sres, r.mb, r.smb, r.me1, r.cme1, r.sme1,
            r.scme1, 2,
        )
        meet(3)
        again(number, 3, mid, r.me1, r.cme1, r.sme1, r.scme1, r.mb, r.smb, r.me2, r.cme2, r.sme2, r.scme2, 2)
        meet(4)
        coarsen(
            number, 4, mid, top, r.me2, r.cme2, r.sme2, r.scme2, r.mb, r.smb, r.tb, r.stb, r.te, r.cte, r.ste, r.scte,
            1,
        )
        meet(5)
        ghost = ghosts(r.ste, 1, core)

        def body(p, carry):
            value, total = pull(r.te, r.cte, top, 0, ghost, p, core, 1)
            update = value + (r.tb[0, p, real, :] + total) * r.trd[0, p, real, :]
            for n in range(group):
                middle = r.me2[n // 2 + 1, p + 1, real, :] + update
                r.new[n, p, real, :] = r.u[n + 1, p + 1, real, :] + (r.e2[n + 1, p + 1, real, :] + middle)
            return carry

        first, last = reach(number, stages)
        planes_loop(body, 0, first, last - first)
        out_each(1, number, False, lambda copy: copy.start())
        out_copy(1, 0, number).start()

    for n in range(group):
        for side in range(2):
            r.sres[n, side, rows(full), :] = (
                r.strip_in[n, side, 1, rows(full), :] + r.sres[n, side, rows(full), :]
            )
    for part in range(parts):
        if part:
            arrived(u_parts + part)
        inner_update(part)
        if part:
            outer_update(part - 1)
            if part in passes:
                run_pass(passes.index(part))
    outer_update(parts - 1)
    run_pass(len(passes) - 1)

    @pl.when(jnp.logical_not(has_before))
    def _():
        def clear_before(p, carry):
            for i in range(pair):
                r.before[p, :, i * width : (i + 1) * width] = nothing
            return carry

        lax.fori_loop(0, nz, clear_before, 0)

    @pl.when(has_before)
    def _():
        pltpu.make_async_remote_copy(
            src_ref=r.before, dst_ref=r.before, send_sem=r.before_sem.at[0], recv_sem=r.before_sem.at[1],
            device_id={"tm": me}, device_id_type=mesh_ids,
        ).wait_recv()

    far_real = pl.ds(halo, tx)
    bare = (halo, tx)

    def far_out(i):
        return pltpu.make_async_copy(
            r.far_res.at[i], r.res_out.at[0, 0, :, :, columns(far_block + i)], r.far_sem.at[2, i]
        )

    @pl.when(own_work)
    def _():
        for number in range(2):

            @pl.when(flanks[number][0])
            def _():
                row_copy(1 - number).wait_recv()

            for i in range(pair):
                value = r.row_in[number, 0, i]
                r.row_c[number, i] = (half * r.row_in[number, 1, i]) * (1.0 + value * value)
        for ref in (r.lu, r.lc):
            for k in range(pair + 3):
                for plane in (0, nz + 1):
                    ref[k, plane] = blank(tx + pad)

            def clear_outer(p, carry):
                for k in (0, pair + 2):
                    ref[k, p + 1, far_real, :] = nothing
                return carry

            lax.fori_loop(0, nz, clear_outer, 0)

        def far_coefficient(p, carry):
            for k in range(pair + 1):
                value = r.lu[1 + k, p + 1, far_real, :]
                r.lc[1 + k, p + 1, far_real, :] = (half * r.lkap[1 + k, p]) * (1.0 + value * value)
            for i in range(pair):
                k = far_block - near_block + i
                for number, row in enumerate((halo - 1, halo + tx)):
                    r.lu[1 + k, p + 1, pl.ds(row, 1), :] = r.row_in[number, 0, i, pl.ds(p, 1), :]
                    r.lc[1 + k, p + 1, pl.ds(row, 1), :] = r.row_c[number, i, pl.ds(p, 1), :]
            return carry

        lax.fori_loop(0, nz, far_coefficient, 0, unroll=2)
        first_tx, last_tx = lane_tx == 0, lane_tx == width - 1
        for i in range(pair):
            k = 1 + far_block - near_block + i
            own_columns = columns(far_block + i)

            def body(p, carry):
                def near_of(ref):
                    here = ref[k, p + 1, far_real, :]
                    before, after = ref[k - 1, p + 1, far_real, :], ref[k + 1, p + 1, far_real, :]
                    return here, (
                        jnp.where(first_tx, pltpu.roll(before, 1, 1), pltpu.roll(here, 1, 1)),
                        jnp.where(last_tx, pltpu.roll(after, width - 1, 1), pltpu.roll(here, width - 1, 1)),
                        ref[k, p + 1, pl.ds(halo - 1, tx), :], ref[k, p + 1, pl.ds(halo + 1, tx), :],
                        ref[k, p, far_real, :], ref[k, p + 2, far_real, :],
                    )

                value, value_near = near_of(r.lu)
                cc, c_near = near_of(r.lc)
                left = r.own[1, p, :, own_columns] - value + r.before[p, :, i * width : (i + 1) * width]
                for one, two in zip(value_near, c_near):
                    left = left - (cc + two) * (value - one)
                r.far_res[i, p] = left
                return carry

            lax.fori_loop(0, nz, body, 0, unroll=4)
            far_out(i).start()
        for i in range(pair):
            far_out(i).wait()
        for number in range(2):

            @pl.when(flanks[number][0])
            def _():
                row_copy(number).wait_send()

    @pl.when(has_after)
    def _():
        before_copy().wait_send()

    strip_each(False, lambda copy: copy.wait_send())
    for a in range(u_parts + parts):
        for j in order[:3]:
            in_copy(a, j).wait_send()
    for kind in range(u_parts + parts + 3):
        edge_send_wait(kind)
    if chained:

        @pl.when(has_next)
        def _():
            for number in range(len(time_refs)):
                for copy in time_copies(number):
                    copy.wait_send()

    for a in range(2):
        for part in range(len(pieces[a])):
            out_copy(a, 0, part).wait()
            out_each(a, part, False, lambda copy: copy.wait_send())
            out_each(a, part, True, lambda copy: copy.wait_recv())


def shards(tm_size, space_size, iterate, source_term, conductivity):
    _, nz, tx, ty = conductivity.shape
    width = ty // group
    tall = tx + 2 * pad
    f32 = jnp.float32
    dma = pltpu.SemaphoreType.DMA
    kinds = u_parts + parts + 3

    def padded(count):
        return pltpu.VMEM((count, nz + 2, tall, width), f32)

    def plain(*lead):
        return pltpu.VMEM((*lead, nz, tall, width), f32)

    def strip(*lead):
        return pltpu.VMEM((*lead, 2, tall, width), f32)

    scratch = {}
    scratch |= {name: padded(count) for name, count in (
        ("u", 5), ("c", 4), ("cu", 4), ("e1", 5), ("ce1", 4), ("e2", 5), ("ce2", 4), ("mc", 2), ("me1", 3),
        ("cme1", 2), ("me2", 3), ("cme2", 2), ("tc", 1), ("te", 2), ("cte", 1),
    )}
    scratch |= {name: plain(count) for name, count in (
        ("src", 4), ("res", 4), ("wl", 4), ("wr", 4), ("wa", 4), ("rd", 4), ("mwl", 2), ("mwr", 2), ("mwa", 2),
        ("mrd", 2), ("mb", 2), ("twl", 1), ("twr", 1), ("twa", 1), ("trd", 1), ("tb", 1), ("new", 4),
    )}
    scratch["kap"] = plain()
    scratch |= {name: strip(count) for name, count in (
        ("su", 5), ("sc", 4), ("scu", 4), ("se1", 5), ("sce1", 4), ("se2", 5), ("sce2", 4), ("smc", 2),
        ("sme1", 3), ("scme1", 2), ("sme2", 3), ("scme2", 2), ("stc", 1), ("ste", 2), ("scte", 1),
        ("swl", 4), ("swr", 4), ("swd", 4), ("swu", 4), ("swa", 4), ("srd", 4), ("sres", 4),
        ("smwl", 2), ("smwr", 2), ("smwd", 2), ("smwu", 2), ("smwa", 2), ("smrd", 2), ("smb", 2),
        ("stwl", 1), ("stwr", 1), ("stwd", 1), ("stwu", 1), ("stwa", 1), ("strd", 1), ("stb", 1),
    )}
    scratch["kap_strip"] = strip()
    scratch["strip_in"] = strip(group, 2)
    scratch["strip_send"] = pltpu.VMEM((group, 2, 2, tx, width), f32)
    scratch["own"] = pltpu.VMEM((2, nz, tx, ty), f32)
    scratch["beside"] = pltpu.VMEM((2, nz, tx, width), f32)
    pair = group // 2
    scratch["lu"] = pltpu.VMEM((pair + 3, nz + 2, tx + pad, width), f32)
    scratch["lc"] = pltpu.VMEM((pair + 3, nz + 2, tx + pad, width), f32)
    scratch["lkap"] = pltpu.VMEM((pair + 2, nz, tx, width), f32)
    scratch["before"] = pltpu.VMEM((nz, tx, pair * width), f32)
    scratch["far_res"] = pltpu.VMEM((pair, nz, tx, width), f32)
    scratch["row_send"] = pltpu.VMEM((2, 2, pair, nz, width), f32)
    scratch["row_in"] = pltpu.VMEM((2, 2, pair, nz, width), f32)
    scratch["row_c"] = pltpu.VMEM((2, pair, nz, width), f32)
    scratch["packs"] = pltpu.VMEM((stages - 1, group, tall, width), f32)
    scratch["packed_one"] = pltpu.VMEM((group, tall, width), f32)
    scratch["damp"] = pltpu.VMEM((3, tall, width), f32)
    for name, shape in (
        ("loc_sem", (5,)), ("in_lsem", (u_parts + parts,)), ("in_ssem", (u_parts + parts, group - 1)),
        ("in_rsem", (u_parts + parts, group - 1)), ("out_lsem", (2, len(passes) + 1)), ("out_ssem", (2, len(passes) + 1, group - 1)),
        ("out_rsem", (2, len(passes) + 1, group - 1)), ("strip_ssem", (group - 1, 2)), ("strip_rsem", (group - 1, 2)),
        ("edge_ssem", (kinds, 2)), ("edge_rsem", (kinds, 2)), ("time_ssem", (6, 2)), ("far_sem", (3, pair + 1)),
        ("before_sem", (2,)), ("row_sem", (2, 2)),
        ("time_rsem", (6, 2)),
    ):
        scratch[name] = dma(shape)
    names = ("state_in", "source_in", "kappa_in", "new_out", "res_out", *scratch)
    out = jax.ShapeDtypeStruct(iterate.shape, f32)
    hbm = pl.BlockSpec(memory_space=pltpu.HBM)
    new, res = pl.pallas_call(
        functools.partial(kernel, tm_size, space_size, names),
        out_shape=(pltpu.VMEM(iterate.shape, f32),) * 2,
        in_specs=[hbm] * 3,
        out_specs=(pl.BlockSpec(memory_space=pltpu.VMEM),) * 2,
        scratch_shapes=list(scratch.values()),
        compiler_params=pltpu.CompilerParams(
            collective_id=0, has_side_effects=True, vmem_limit_bytes=58 * 1024 * 1024
        ),
    )(iterate, source_term, conductivity)
    return settled(new, res)


def settle(new_in, res_in, new_out, res_out, sems):
    copies = [
        pltpu.make_async_copy(held, out, sems.at[k])
        for k, (held, out) in enumerate(((new_in, new_out), (res_in, res_out)))
    ]
    for copy in copies:
        copy.start()
    for copy in copies:
        copy.wait()


def settled(new, res):
    hbm = pl.BlockSpec(memory_space=pltpu.HBM)
    out = jax.ShapeDtypeStruct(new.shape, jnp.float32)
    return pl.pallas_call(
        settle,
        out_shape=(out, out),
        in_specs=[pl.BlockSpec(memory_space=pltpu.VMEM)] * 2,
        out_specs=(hbm, hbm),
        scratch_shapes=[pltpu.SemaphoreType.DMA((2,))],
        compiler_params=pltpu.CompilerParams(vmem_limit_bytes=1024 * 1024),
    )(new, res)


def solution(mesh):
    tiled = P("tm", "space", None, None, None)
    in_specs = (tiled, tiled, P("space", None, None, None))
    body = functools.partial(shards, mesh.shape["tm"], mesh.shape["space"])
    return jax.shard_map(
        body, mesh=mesh, in_specs=in_specs, out_specs=(tiled, tiled), check_vma=False
    )
```
